32 devices in a mesh: batch: 4 (over y, core), seq: 8 (over z, x).
Axes of the slice: x: 2, y: 2, z: 4, core: 2. Of those that a mesh axis runs over, the one named last changes fastest.
Arguments:
- tokens: bfloat16 [4, 8192, 768], P('batch', 'seq'), may hold values from -6 to 6
- cluster_slot: int32 [4, 12, 8192], P('batch', None, 'seq'), may hold values from 0 to 8191, as said below
- loss_mask: int32 [4, 8192], P('batch', 'seq'), may hold values from 0 to 1, as said below
- out_grad: bfloat16 [4, 8192, 768], P('batch', 'seq'), may hold values from -6 to 6
- query_weight: bfloat16 [768, 768], P(('batch', 'seq')), may hold values from -0.21875 to 0.21875
- key_weight: bfloat16 [768, 768], P(('batch', 'seq')), may hold values from -0.21875 to 0.21875
- value_weight: bfloat16 [768, 768], P(('batch', 'seq')), may hold values from -0.21875 to 0.21875
- output_weight: bfloat16 [768, 768], P(('batch', 'seq')), may hold values from -0.875 to 0.875
- query_bias: bfloat16 [768], P(('batch', 'seq')), may hold values from -1.796875 to 1.796875
- value_bias: bfloat16 [768], P(('batch', 'seq')), may hold values from -1.796875 to 1.796875
- output_bias: bfloat16 [768], P(('batch', 'seq')), may hold values from -1.796875 to 1.796875
- first_gain: bfloat16 [768], P(('batch', 'seq')), may hold values from 0.5 to 1.5
- first_shift: bfloat16 [768], P(('batch', 'seq')), may hold values from -1.796875 to 1.796875
- up_weight: bfloat16 [768, 3072], P(('batch', 'seq')), may hold values from -0.21875 to 0.21875
- up_bias: bfloat16 [3072], P(('batch', 'seq')), may hold values from -1.796875 to 1.796875
- down_weight: bfloat16 [3072, 768], P(('batch', 'seq')), may hold values from -0.109375 to 0.109375
- down_bias: bfloat16 [768], P(('batch', 'seq')), may hold values from -1.796875 to 1.796875
- second_gain: bfloat16 [768], P(('batch', 'seq')), may hold values from 0.5 to 1.5
- second_shift: bfloat16 [768], P(('batch', 'seq')), may hold values from -1.796875 to 1.796875
Outputs:
- output: bfloat16 [4, 8192, 768], P('batch', 'seq')
- grad_tokens: bfloat16 [4, 8192, 768], P('batch', 'seq')
- grad_query_weight: float32 [768, 768], P(('batch', 'seq'))
- grad_key_weight: float32 [768, 768], P(('batch', 'seq'))
- grad_value_weight: float32 [768, 768], P(('batch', 'seq'))
- grad_output_weight: float32 [768, 768], P(('batch', 'seq'))
- grad_query_bias: float32 [768], P(('batch', 'seq'))
- grad_value_bias: float32 [768], P(('batch', 'seq'))
- grad_output_bias: float32 [768], P(('batch', 'seq'))
- grad_first_gain: float32 [768], P(('batch', 'seq'))
- grad_first_shift: float32 [768], P(('batch', 'seq'))
- grad_up_weight: float32 [768, 3072], P(('batch', 'seq'))
- grad_up_bias: float32 [3072], P(('batch', 'seq'))
- grad_down_weight: float32 [3072, 768], P(('batch', 'seq'))
- grad_down_bias: float32 [768], P(('batch', 'seq'))
- grad_second_gain: float32 [768], P(('batch', 'seq'))
- grad_second_shift: float32 [768], P(('batch', 'seq'))
- cluster_stats: float32 [2, 64], P(None, 'seq')
The draws below stay inside these ranges and needn't reach their ends.
Inputs may be any that keep to these rules, and one draw needn't show every extreme that they name: For each sequence and head, cluster_slot is a permutation of 0 to 8191. Cut positions and places into aligned blocks of 1024; the tokens of position block s put exactly 128 tokens into each block of places, and the places they take leave the remainder s when divided by 8. `loss_mask`: the share of ones differs from sequence to sequence.
All inputs are finite; a program needn't handle non-finite values.
Results may differ from the reference program's by a relative error of at most 0.014.
Values may be sent and summed in bfloat16 or wider, within the bound.
A program may use at most 192 MiB of HBM per device.

```python
import jax
import jax.numpy as jnp
from jax import lax

D = 768
HEADS = 12
HEAD_DIM = 64
FF = 3072
CLUSTER = 128
TOK_DEV = 1024
LENGTH = 8192
SEQS = 4
CLUSTERS = 64


def local_order(subkey):
    return jax.random.permutation(subkey, TOK_DEV).astype(jnp.int32)


def draw_cluster_slot(key, part):
    owners = LENGTH // TOK_DEV
    per_owner = TOK_DEV // owners
    subkeys = jax.random.split(jax.random.fold_in(key, 7), SEQS * HEADS * owners)
    places = jax.vmap(local_order)(subkeys).reshape(SEQS, HEADS, owners, TOK_DEV)
    source = jnp.arange(owners, dtype=jnp.int32)[None, None, :, None]
    target = places // per_owner
    within = places % per_owner
    slots = target * TOK_DEV + within * owners + source
    return slots.reshape(SEQS, HEADS, LENGTH).astype(jnp.int32)


def draw_loss_mask(key, part):
    levels = jax.random.randint(jax.random.fold_in(key, 1), (SEQS, 1), 1, 6)
    rising = SEQS + 2 * jnp.arange(SEQS, dtype=jnp.int32)[:, None]
    limits = rising * levels
    draw_value = jax.random.randint(jax.random.fold_in(key, 2), (SEQS, LENGTH), 0, 15 * SEQS)
    return (draw_value < limits).astype(jnp.int32)


def steps_of(stream_key, dims, pieces, least, high):
    level, own = 1.0, jax.random.fold_in(stream_key, 6)
    for position, parts in pieces:
        steps = jnp.exp(jax.random.uniform(jax.random.fold_in(own, position), (parts,), jnp.float32, least / len(pieces), high / len(pieces)))
        level = level * jnp.repeat(steps, dims[position] // parts).reshape([-1 if axis == position else 1 for axis in range(len(dims))])
    return level


def scatter_about(key, extent, scale, bound, shards=(), kind=jnp.bfloat16):
    level = steps_of(key, extent, shards, -0.22, 0.18) if shards else 1.0
    values = jax.random.normal(key, extent, jnp.float32) * scale * level
    return jnp.minimum(jnp.maximum(values, -bound), bound).astype(kind)


def setup_inputs(seed: int = 0) -> dict:
    key_of = jax.random.split(jax.random.key(seed), 20)
    return {
        "tokens": scatter_about(key_of[0], (SEQS, LENGTH, D), 1.0, 6.0, ((0, 4), (1, 8))),
        "cluster_slot": draw_cluster_slot(jax.random.fold_in(key_of[19], 71), 0),
        "loss_mask": draw_loss_mask(jax.random.fold_in(key_of[19], 71), 0),
        "out_grad": scatter_about(key_of[3], (SEQS, LENGTH, D), 1.0, 6.0, ((0, 4), (1, 8))),
        "query_weight": scatter_about(key_of[4], (D, D), D ** -0.5, 0.21875, ((0, 32),)),
        "key_weight": scatter_about(key_of[5], (D, D), D ** -0.5, 0.21875, ((0, 32),)),
        "value_weight": scatter_about(key_of[6], (D, D), D ** -0.5, 0.21875, ((0, 32),)),
        "output_weight": scatter_about(key_of[7], (D, D), (D // 16) ** -0.5, 0.875, ((0, 32),)),
        "query_bias": scatter_about(key_of[8], (D,), 0.3, 1.796875, ((0, 32),)),
        "value_bias": scatter_about(key_of[9], (D,), 0.3, 1.796875, ((0, 32),)),
        "output_bias": scatter_about(key_of[10], (D,), 0.3, 1.796875, ((0, 32),)),
        "first_gain": jnp.clip(1.0 + 0.1 * jax.random.normal(key_of[11], (D,), jnp.float32), 0.5, 1.5).astype(jnp.bfloat16),
        "first_shift": scatter_about(key_of[12], (D,), 0.3, 1.796875, ((0, 32),)),
        "up_weight": scatter_about(key_of[13], (D, FF), D ** -0.5, 0.21875, ((0, 32),)),
        "up_bias": scatter_about(key_of[14], (FF,), 0.3, 1.796875, ((0, 32),)),
        "down_weight": scatter_about(key_of[15], (FF, D), FF ** -0.5, 0.109375, ((0, 32),)),
        "down_bias": scatter_about(key_of[16], (D,), 0.3, 1.796875, ((0, 32),)),
        "second_gain": jnp.clip(1.0 + 0.1 * jax.random.normal(key_of[17], (D,), jnp.float32), 0.5, 1.5).astype(jnp.bfloat16),
        "second_shift": scatter_about(key_of[18], (D,), 0.3, 1.796875, ((0, 32),)),
    }


@jax.custom_vjp
def low(v):
    return lax.optimization_barrier(v.astype(jnp.bfloat16)).astype(jnp.float32)

@jax.custom_vjp
def low_back(v):
    return v

def low_keep(v):
    return (low(v), None)

def low_pass(kept, grad):
    return (grad,)

def back_keep(v):
    return (v, None)

def back_low(kept, grad):
    return (low(grad),)
low.defvjp(low_keep, low_pass)
low_back.defvjp(back_keep, back_low)
EPSILON = 1e-12

def matmul_high(left, right):
    return jnp.dot(left, right, precision=lax.Precision.HIGHEST)

def layer_norm(values, gain, shift):
    centre = lax.optimization_barrier(jnp.mean(values, axis=-1, keepdims=True))
    centred = values - centre
    spread = lax.optimization_barrier(jnp.mean(centred * centred, axis=-1, keepdims=True))
    return centred * lax.rsqrt(spread + EPSILON) * gain + shift

def cluster_head(operands):
    head_query, head_key, head_value, order, slots, mask_row = operands
    scale = HEAD_DIM ** (-0.5)
    clus_query = jnp.take(head_query, order, axis=0).reshape(CLUSTERS, CLUSTER, HEAD_DIM)
    clus_key = jnp.take(head_key, order, axis=0).reshape(CLUSTERS, CLUSTER, HEAD_DIM)
    clus_value = jnp.take(head_value, order, axis=0).reshape(CLUSTERS, CLUSTER, HEAD_DIM)
    scores = low_back(jnp.einsum('cid,cjd->cij', clus_query, clus_key, precision=lax.Precision.HIGHEST) * scale)
    top = lax.optimization_barrier(jnp.max(scores, axis=-1, keepdims=True))
    weights = jnp.exp(scores - top)
    totals = lax.optimization_barrier(jnp.sum(weights, axis=-1, keepdims=True))
    probs = weights / totals
    log_total = top[..., 0] + jnp.log(totals[..., 0])
    mixed = jnp.einsum('cij,cjd->cid', low(probs), clus_value, precision=lax.Precision.HIGHEST)
    placed = jnp.take(mixed.reshape(LENGTH, HEAD_DIM), slots, axis=0)
    entropy = log_total - lax.optimization_barrier(jnp.sum(probs * scores, axis=-1))
    clus_mask = jnp.take(mask_row, order).reshape(CLUSTERS, CLUSTER)
    return (placed, lax.optimization_barrier(jnp.sum(entropy * clus_mask, axis=-1)), lax.optimization_barrier(jnp.sum(clus_mask, axis=-1)))

def forward(inputs, params, order, slots, mask_row):
    query_full, key_full, value_full, out_full, query_add, value_add, out_add, gain_first, shift_first, up_full, up_add, down_full, down_add, gain_second, shift_second = params
    queries = low_back(low(matmul_high(inputs, query_full) + query_add))
    keys = low_back(low(matmul_high(inputs, key_full)))
    values = low_back(low(matmul_high(inputs, value_full) + value_add))

    def split_heads(array):
        return array.reshape(LENGTH, HEADS, HEAD_DIM).transpose(1, 0, 2)
    masks = jnp.broadcast_to(mask_row, (HEADS, LENGTH))
    mixed, entropy_sum, occupancy = lax.map(jax.checkpoint(cluster_head), (split_heads(queries), split_heads(keys), split_heads(values), order, slots, masks))
    attended = low_back(low(mixed.transpose(1, 0, 2).reshape(LENGTH, D)))
    branch = low_back(matmul_high(attended, out_full) + out_add)
    hidden = low(layer_norm(inputs + branch, gain_first, shift_first))
    up_pre = low_back(matmul_high(hidden, up_full) + up_add)
    act = low(jax.nn.gelu(up_pre, approximate=False))
    ffn_out = low_back(matmul_high(act, down_full) + down_add)
    result = layer_norm(hidden + ffn_out, gain_second, shift_second)
    return (result, (lax.optimization_barrier(jnp.sum(entropy_sum, axis=0)), lax.optimization_barrier(jnp.sum(occupancy, axis=0))))

def reference(tokens, cluster_slot, loss_mask, out_grad, query_weight, key_weight, value_weight, output_weight, query_bias, value_bias, output_bias, first_gain, first_shift, up_weight, up_bias, down_weight, down_bias, second_gain, second_shift):
    params = tuple((item.astype(jnp.float32) for item in (query_weight, key_weight, value_weight, output_weight, query_bias, value_bias, output_bias, first_gain, first_shift, up_weight, up_bias, down_weight, down_bias, second_gain, second_shift)))
    positions = jnp.broadcast_to(jnp.arange(LENGTH, dtype=jnp.int32)[None, :], (HEADS, LENGTH))
    head_rows = jnp.arange(HEADS, dtype=jnp.int32)[:, None]

    def one_sequence(carry, operands):
        grads_sum, entropy_total, occupancy_total = carry
        inputs, slots, mask_int, cotangent = operands
        order = jnp.zeros((HEADS, LENGTH), jnp.int32).at[head_rows, slots].set(positions)
        mask_row = mask_int.astype(jnp.float32)

        def seq_forward(inputs_f, params_f):
            return forward(inputs_f, params_f, order, slots, mask_row)
        result, pullback, stats = jax.vjp(seq_forward, inputs.astype(jnp.float32), params, has_aux=True)
        d_inputs, d_params = pullback(cotangent.astype(jnp.float32) * mask_row[:, None])
        grads_sum = tuple((total + part for total, part in zip(grads_sum, d_params)))
        carry = (grads_sum, entropy_total + stats[0], occupancy_total + stats[1])
        return (carry, (result.astype(jnp.bfloat16), d_inputs.astype(jnp.bfloat16)))
    start = (tuple((jnp.zeros_like(item) for item in params)), jnp.zeros((CLUSTERS,), jnp.float32), jnp.zeros((CLUSTERS,), jnp.float32))
    (grads_sum, entropy_total, occupancy_total), (output, grad_tokens) = lax.scan(one_sequence, start, (tokens, cluster_slot, loss_mask, out_grad))
    factor = 1.0 / (HEADS * CLUSTER * SEQS)
    cluster_stats = jnp.stack([entropy_total * factor, occupancy_total * factor])
    return (output, grad_tokens, grads_sum[0], grads_sum[1], grads_sum[2], grads_sum[3], grads_sum[4], grads_sum[5], grads_sum[6], grads_sum[7], grads_sum[8], grads_sum[9], grads_sum[10], grads_sum[11], grads_sum[12], grads_sum[13], grads_sum[14], cluster_stats)
```

```python
import functools

import jax
import jax.numpy as jnp
from jax import lax
from jax.experimental import pallas as pl
from jax.experimental.pallas import tpu as pltpu
from jax.sharding import PartitionSpec as P

MESH = pl.DeviceIdType.MESH
F32 = jnp.float32
BF16 = jnp.bfloat16
EPSILON = 1e-12
CLUSTER = 128
PAIR = 128
Z = 4
VMEM_LIMIT = 58 * 1024 * 1024


class Grid:
    def __init__(self, mesh):
        self.batch, self.seq = mesh.shape["batch"], mesh.shape["seq"]
        self.Y, self.X = self.batch // 2, self.seq // Z
        self.half = self.seq // 2
        self.n = self.batch * self.seq

    def swap_pairs(self):
        pairs = []
        for b in range(self.batch):
            for s in range(self.seq):
                if b % 2 == s // self.half:
                    to = (b, s)
                else:
                    to = (b ^ 1, (s + self.half) % self.seq)
                pairs.append((b * self.seq + s, to[0] * self.seq + to[1]))
        return pairs


def coords(g):
    b, s = lax.axis_index("batch"), lax.axis_index("seq")
    return b // 2, b % 2, s // g.X, s % g.X


def device(g, y, c, z, x):
    return (y * 2 + c, z * g.X + x)


def group_place(g):
    b, s = lax.axis_index("batch"), lax.axis_index("seq")
    return b % 2 * g.half + s % g.half


def group_device(g, place):
    b, s = lax.axis_index("batch"), lax.axis_index("seq")
    return (b // 2 * 2 + place // g.half, s // g.half * g.half + place % g.half)


def line_peers(g):
    y, c, z, x = coords(g)
    peers = [device(g, y, c, (z + k) % Z, x) for k in range(1, Z)]
    peers += [device(g, y, c, z, (x + k) % g.X) for k in range(1, g.X)]
    peers += [device(g, (y + k) % g.Y, c, z, x) for k in range(1, g.Y)]
    peers.append(device(g, y, 1 - c, z, x))
    return peers


def greet(peers):
    barrier = pltpu.get_barrier_semaphore()
    for peer in peers:
        pl.semaphore_signal(barrier, inc=1, device_id=peer, device_id_type=MESH)
    pl.semaphore_wait(barrier, len(peers))


def remote(src, dst, send, recv, peer):
    return pltpu.make_async_remote_copy(
        src_ref=src,
        dst_ref=dst,
        send_sem=send,
        recv_sem=recv,
        device_id=peer,
        device_id_type=MESH,
    )


def lane_pieces(shape):
    rows, cols = shape
    if cols % PAIR or rows * cols <= 24 * 768:
        return [(0, cols)]
    count = {3072: 4, 768: 3}.get(cols, 1)
    return [(k * (cols // count), cols // count) for k in range(count)]


def gather_kernel(g, shapes, *refs):
    n = len(shapes)
    ins, outs = refs[:n], refs[n : 2 * n]
    sends, recvs, local_sem = refs[2 * n :]
    y, c, z, x = coords(g)
    greet(line_peers(g))

    units = []
    for index, shape in enumerate(shapes):
        for start, size in lane_pieces(shape):
            units.append((index, pl.ds(start, size)))
    stages = []
    slot = 0
    for number, (index, cols) in enumerate(units):
        src, out = ins[index], outs[index]

        def put(peer, part, slot, src=None, out=out, cols=cols):
            view = out.at[(*part, slice(None), cols)]
            return remote(
                view if src is None else src, view, sends.at[slot], recvs.at[slot], peer
            )

        own = pltpu.make_async_copy(
            src.at[:, cols], out.at[y, c, z, x, :, cols], local_sem.at[number]
        )
        a, w = slice(None), []
        w.append(
            [
                put(device(g, y, c, (z + k) % Z, x), (y, c, z, x), slot + k - 1, src.at[:, cols])
                for k in range(1, Z)
            ]
        )
        slot += Z - 1
        if number % 2 == 0:
            plan = [("x", (y, c, a, x)), ("y", (y, c, a, a))]
        else:
            plan = [("y", (y, c, a, x)), ("x", (a, c, a, x))]
        for axis, part in plan:
            if axis == "x":
                moves = [
                    put(device(g, y, c, z, (x + k) % g.X), part, slot + k - 1)
                    for k in range(1, g.X)
                ]
            else:
                moves = [
                    put(device(g, (y + k) % g.Y, c, z, x), part, slot + k - 1)
                    for k in range(1, g.Y)
                ]
            slot += len(moves)
            w.append(moves)
        w.append([put(device(g, y, 1 - c, z, x), (a, c, a, a), slot)])
        slot += 1
        stages.append((own, w))

    count = len(units)
    lead = 2
    for t in range(count + lead + 3):
        if t < count:
            own, w = stages[t]
            own.start()
            for copy in w[0]:
                copy.start()
        for level in range(1, 4):
            u = t - lead - level + 1
            if 0 <= u < count:
                own, w = stages[u]
                if level == 1:
                    own.wait()
                for copy in w[level - 1]:
                    copy.wait_recv()
                for copy in w[level]:
                    copy.start()
    for own, w in stages:
        w[3][0].wait_recv()
        for moves in w:
            for copy in moves:
                copy.wait_send()


def gather(g, arrays):
    shapes = [item.shape for item in arrays]
    units = sum(len(lane_pieces(shape)) for shape in shapes)
    slots = units * (Z + g.X + g.Y - 2)
    return pl.pallas_call(
        functools.partial(gather_kernel, g, shapes),
        out_shape=[
            jax.ShapeDtypeStruct((g.Y, 2, Z, g.X, *item.shape), item.dtype) for item in arrays
        ],
        in_specs=[pl.BlockSpec(memory_space=pl.ANY)] * len(arrays),
        out_specs=[pl.BlockSpec(memory_space=pl.ANY)] * len(arrays),
        scratch_shapes=[
            pltpu.SemaphoreType.DMA((slots,)),
            pltpu.SemaphoreType.DMA((slots,)),
            pltpu.SemaphoreType.DMA((units,)),
        ],
        compiler_params=pltpu.CompilerParams(
            collective_id=0, has_side_effects=True, vmem_limit_bytes=VMEM_LIMIT
        ),
        name="weight_gather",
    )(*arrays)


def scatter_kernel(g, shapes, *refs):
    n = len(shapes)
    ins, outs = refs[:n], refs[n : 2 * n]
    by_core, by_one, by_two, by_z = (refs[(2 + k) * n : (3 + k) * n] for k in range(4))
    sends, recvs = refs[6 * n :]
    y, c, z, x = coords(g)
    greet(line_peers(g))

    units = []
    for index, shape in enumerate(shapes):
        for start, size in lane_pieces(shape):
            units.append((index, slice(start, start + size)))

    per = Z + g.X + g.Y - 2

    def copies(number, level):
        index, cols = units[number]
        base = number * per
        every = slice(None)
        first_y = index % 2 == 0
        if level == 0:
            return [
                remote(
                    ins[index].at[:, 1 - c, :, :, :, cols],
                    by_core[index].at[:, :, :, :, cols],
                    sends.at[base],
                    recvs.at[base],
                    device(g, y, 1 - c, z, x),
                )
            ]
        base += 1
        along = {1: "y" if first_y else "x", 2: "x" if first_y else "y", 3: "z"}[level]
        if level == 2:
            base += (g.Y if first_y else g.X) - 1
        if level == 3:
            base += g.Y + g.X - 2
        size = {"y": g.Y, "x": g.X, "z": Z}[along]
        moves = []
        for k in range(1, size):
            if along == "y":
                to = (y + k) % g.Y
                peer = device(g, to, c, z, x)
            elif along == "x":
                to = (x + k) % g.X
                peer = device(g, y, c, z, to)
            else:
                to = (z + k) % Z
                peer = device(g, y, c, to, x)
            if level == 1 and first_y:
                src = by_core[index].at[to, :, :, :, cols]
            elif level == 1:
                src = by_core[index].at[:, :, to, :, cols]
            elif level == 2 and first_y:
                src = by_one[index].at[0, :, to, :, cols]
            elif level == 2:
                src = by_one[index].at[0, to, :, :, cols]
            else:
                src = by_two[index].at[0, to, :, cols]
            held = (by_one, by_two, by_z)[level - 1][index]
            slot = 0 if level < 3 else 0
            dst = held.at[(k, *([every] * (len(held.shape) - 2)), cols)]
            moves.append(remote(src, dst, sends.at[base + k - 1], recvs.at[base + k - 1], peer))
        return moves

    def add(number, level):
        index, cols = units[number]
        first_y = index % 2 == 0
        kind = ins[index].dtype
        if level == 0:

            def one(step, carry):
                for yy in range(g.Y):
                    for xx in range(g.X):
                        total = ins[index][yy, c, step, xx, :, cols].astype(F32)
                        total += by_core[index][yy, step, xx, :, cols].astype(F32)
                        by_core[index][yy, step, xx, :, cols] = total.astype(kind)
                return carry

            lax.fori_loop(0, Z, one, 0)
        elif level == 1:
            size, rest = (g.Y, g.X) if first_y else (g.X, g.Y)

            def one(step, carry):
                for r in range(rest):
                    if first_y:
                        total = by_core[index][y, step, r, :, cols].astype(F32)
                    else:
                        total = by_core[index][r, step, x, :, cols].astype(F32)
                    for k in range(1, size):
                        if first_y:
                            total += by_one[index][k, step, r, :, cols].astype(F32)
                        else:
                            total += by_one[index][k, r, step, :, cols].astype(F32)
                    if first_y:
                        by_one[index][0, step, r, :, cols] = total.astype(kind)
                    else:
                        by_one[index][0, r, step, :, cols] = total.astype(kind)
                return carry

            lax.fori_loop(0, Z, one, 0)
        elif level == 2:
            size = g.X if first_y else g.Y

            def one(step, carry):
                if first_y:
                    total = by_one[index][0, step, x, :, cols].astype(F32)
                else:
                    total = by_one[index][0, y, step, :, cols].astype(F32)
                for k in range(1, size):
                    total += by_two[index][k, step, :, cols].astype(F32)
                by_two[index][0, step, :, cols] = total.astype(kind)
                return carry

            lax.fori_loop(0, Z, one, 0)
        else:
            total = by_two[index][0, z, :, cols].astype(F32)
            for k in range(1, Z):
                total += by_z[index][k, :, cols].astype(F32)
            outs[index][:, cols] = total

    count = len(units)
    started = [[None] * 4 for _ in units]
    for t in range(count + 4):
        if t < count:
            started[t][0] = copies(t, 0)
            for copy in started[t][0]:
                copy.start()
        for level in range(4):
            u = t - level - 1
            if 0 <= u < count:
                for copy in started[u][level]:
                    copy.wait_recv()
                add(u, level)
                if level < 3:
                    started[u][level + 1] = copies(u, level + 1)
                    for copy in started[u][level + 1]:
                        copy.start()
    for levels in started:
        for moves in levels:
            for copy in moves:
                copy.wait_send()


def scatter(g, arrays):
    shapes = [item.shape[4:] for item in arrays]
    units = sum(len(lane_pieces(shape)) for shape in shapes)
    slots = units * (Z + g.X + g.Y - 2)
    scratch = [[], [], [], []]
    for index, (item, shape) in enumerate(zip(arrays, shapes)):
        scratch[0].append(pltpu.VMEM((g.Y, Z, g.X, *shape), item.dtype))
        if index % 2 == 0:
            scratch[1].append(pltpu.VMEM((g.Y, Z, g.X, *shape), item.dtype))
            scratch[2].append(pltpu.VMEM((g.X, Z, *shape), item.dtype))
        else:
            scratch[1].append(pltpu.VMEM((g.X, g.Y, Z, *shape), item.dtype))
            scratch[2].append(pltpu.VMEM((g.Y, Z, *shape), item.dtype))
        scratch[3].append(pltpu.VMEM((Z, *shape), item.dtype))
    return pl.pallas_call(
        functools.partial(scatter_kernel, g, shapes),
        out_shape=[jax.ShapeDtypeStruct(shape, F32) for shape in shapes],
        in_specs=[pl.BlockSpec(memory_space=pltpu.VMEM)] * len(arrays),
        out_specs=[pl.BlockSpec(memory_space=pltpu.VMEM)] * len(arrays),
        scratch_shapes=[item for level in scratch for item in level]
        + [pltpu.SemaphoreType.DMA((slots,)), pltpu.SemaphoreType.DMA((slots,))],
        compiler_params=pltpu.CompilerParams(
            collective_id=1, has_side_effects=True, vmem_limit_bytes=VMEM_LIMIT
        ),
        name="grad_scatter",
    )(*arrays)


def exchange_kernel(g, n, *refs):
    ins, outs = refs[:n], refs[n : 2 * n]
    sends, recvs, local_sem = refs[2 * n :]
    me = group_place(g)
    size = g.seq
    peers = [(me + k) % size for k in range(1, size)]
    greet([group_device(g, peer) for peer in peers])
    copies = []
    for index in range(n):
        own = pltpu.make_async_copy(
            ins[index].at[:, me], outs[index].at[:, me], local_sem.at[index]
        )
        own.start()
        for k, peer in enumerate(peers):
            slot = index * (size - 1) + k
            copy = remote(
                ins[index].at[:, peer],
                outs[index].at[:, me],
                sends.at[slot],
                recvs.at[slot],
                group_device(g, peer),
            )
            copy.start()
            copies.append(copy)
        copies.append(own)
    for copy in copies:
        copy.wait()


def exchange(g, arrays, number):
    n = len(arrays)
    return pl.pallas_call(
        functools.partial(exchange_kernel, g, n),
        out_shape=[jax.ShapeDtypeStruct(item.shape, item.dtype) for item in arrays],
        in_specs=[pl.BlockSpec(memory_space=pl.ANY)] * n,
        out_specs=[pl.BlockSpec(memory_space=pl.ANY)] * n,
        scratch_shapes=[
            pltpu.SemaphoreType.DMA((n * (g.seq - 1),)),
            pltpu.SemaphoreType.DMA((n * (g.seq - 1),)),
            pltpu.SemaphoreType.DMA((n,)),
        ],
        compiler_params=pltpu.CompilerParams(
            collective_id=number, has_side_effects=True, vmem_limit_bytes=VMEM_LIMIT
        ),
        name="exchange",
    )(*arrays)


def dot(left, right):
    return lax.dot_general(left, right, (((1,), (0,)), ((), ())), preferred_element_type=F32)


def dot_nt(left, right):
    return lax.dot_general(left, right, (((1,), (1,)), ((), ())), preferred_element_type=F32)


def dot_tn(left, right):
    return lax.dot_general(left, right, (((0,), (0,)), ((), ())), preferred_element_type=F32)


def head_lanes(shape):
    return lax.broadcasted_iota(jnp.int32, shape, 1) < PAIR // 2


def split_pair(value, axis=0):
    low = head_lanes(value.shape)
    zero = jnp.zeros_like(value)
    return jnp.concatenate(
        [jnp.where(low, value, zero), jnp.where(low, zero, value)], axis=axis
    )


def place_rows(places_ref, pair, start, size):
    tok = places_ref.shape[1]
    rows = lax.broadcasted_iota(jnp.int32, (size, tok), 0) + start
    parts = [
        (rows == places_ref[pl.ds(2 * pair + i, 1), :]).astype(F32).astype(BF16) for i in range(2)
    ]
    return jnp.concatenate(parts, axis=1)


def token_rows(cols_ref, pair, start, size):
    tok = cols_ref.shape[0]
    lanes = lax.broadcasted_iota(jnp.int32, (size, tok), 1)
    parts = [
        (lanes == cols_ref[pl.ds(start, size), 2 * pair + i : 2 * pair + i + 1])
        .astype(F32)
        .astype(BF16)
        for i in range(2)
    ]
    return jnp.concatenate(parts, axis=1)


def gather_rows(block_ref, lead, start, size, lanes):
    part = block_ref[(*lead, slice(None), pl.ds(start, size), lanes)]
    if size % 16:
        part = part.astype(F32)
    return part.reshape(part.shape[0] * size, part.shape[2]).astype(block_ref.dtype)


def spread_rows(value, sources, kind):
    size = value.shape[0] // sources
    if size % 16:
        return value.astype(F32).reshape(sources, size, value.shape[1]).astype(kind)
    return value.astype(kind).reshape(sources, size, value.shape[1])


ROWS = 256


def project_kernel(x_ref, wq_ref, wk_ref, wv_ref, bias_ref, places_ref, cols_ref, out_ref, mask_ref, rhs):
    tok = x_ref.shape[0]
    pairs = out_ref.shape[0]
    heads = 2 * pairs
    lanes = lax.broadcasted_iota(jnp.int32, (ROWS, PAIR), 1)
    for pair in range(pairs):
        head = slice(pair * PAIR, (pair + 1) * PAIR)

        def project(step, carry):
            rows = pl.ds(step * ROWS, ROWS)
            x = x_ref[rows, :]
            for part, w_ref in enumerate((wq_ref, wk_ref, wv_ref)):
                value = dot(x, w_ref[:, head]) + bias_ref[part : part + 1, head]
                value = value.astype(BF16)
                low = head_lanes(value.shape)
                zero = jnp.zeros_like(value)
                to = slice(part * PAIR, (part + 1) * PAIR)
                rhs[rows, to] = jnp.where(low, value, zero)
                rhs[pl.ds(tok + step * ROWS, ROWS), to] = jnp.where(low, zero, value)
            mask = cols_ref[rows, heads : heads + 1].astype(F32)
            for i in range(2):
                rhs[pl.ds(i * tok + step * ROWS, ROWS), 3 * PAIR :] = jnp.where(
                    lanes == 2 * pair + i, mask, 0.0
                ).astype(BF16)
            return carry

        lax.fori_loop(0, tok // ROWS, project, 0)

        def permute(step, carry):
            rows = pl.ds(step * ROWS, ROWS)
            picked = dot(place_rows(places_ref, pair, step * ROWS, ROWS), rhs[...])
            out_ref[pair, rows, :] = picked[:, : 3 * PAIR].astype(BF16)
            if pair == 0:
                mask_ref[rows, :] = picked[:, 3 * PAIR :].astype(BF16)
            else:
                mask_ref[rows, :] = mask_ref[rows, :] + picked[:, 3 * PAIR :].astype(BF16)
            return carry

        lax.fori_loop(0, tok // ROWS, permute, 0)


def vmem_call(kernel, out_shape, scratch, name):
    def call(*args):
        return pl.pallas_call(
            kernel,
            out_shape=out_shape,
            in_specs=[pl.BlockSpec(memory_space=pltpu.VMEM)] * len(args),
            out_specs=jax.tree.map(lambda _: pl.BlockSpec(memory_space=pltpu.VMEM), out_shape),
            scratch_shapes=scratch,
            compiler_params=pltpu.CompilerParams(vmem_limit_bytes=VMEM_LIMIT),
            name=name,
        )(*args)

    return call


def cluster_scores(q, k, scale):
    return dot_nt(q, k) * scale


def attend_kernel(scale, factor, qkv_ref, mask_ref, out_ref, stats_ref):
    pair = pl.program_id(0)
    _, sources, per_owner, _ = qkv_ref.shape
    size = CLUSTER // sources
    clusters = per_owner // size
    lanes = lax.broadcasted_iota(jnp.int32, (CLUSTER, PAIR), 1)
    spot = lax.broadcasted_iota(jnp.int32, stats_ref.shape, 1)
    row = lax.broadcasted_iota(jnp.int32, stats_ref.shape, 0)

    @pl.when(pair == 0)
    def _():
        stats_ref[...] = jnp.zeros_like(stats_ref)

    for cluster in range(clusters):
        q, k, v = (
            gather_rows(qkv_ref, (0,), cluster * size, size, slice(i * PAIR, (i + 1) * PAIR))
            for i in range(3)
        )
        scores = cluster_scores(split_pair(q), k, scale)
        top = jnp.max(scores, axis=1, keepdims=True)
        weights = jnp.exp(scores - top)
        totals = jnp.sum(weights, axis=1, keepdims=True)
        probs = weights / totals
        entropy = top + jnp.log(totals) - jnp.sum(probs * scores, axis=1, keepdims=True)
        low = probs.astype(BF16)
        mixed = dot(
            jnp.concatenate([low[:CLUSTER], low[CLUSTER:]], axis=1), split_pair(v)
        )
        out_ref[0, :, cluster * size : (cluster + 1) * size, :] = spread_rows(mixed, sources, BF16)
        mask = gather_rows(mask_ref, (), cluster * size, size, slice(None)).astype(F32)
        own = jnp.where(lanes == 2 * pair, entropy[:CLUSTER], 0.0) + jnp.where(
            lanes == 2 * pair + 1, entropy[CLUSTER:], 0.0
        )
        in_pair = (lanes == 2 * pair) | (lanes == 2 * pair + 1)
        entropy_sum = jnp.sum(own * mask) * factor
        count = jnp.sum(jnp.where(in_pair, mask, 0.0)) * factor
        stats_ref[...] += jnp.where(
            spot == cluster, jnp.where(row == 0, entropy_sum, jnp.where(row == 1, count, 0.0)), 0.0
        )


def attend(qkv, mask, scale, factor):
    pairs, sources, per_owner, width = qkv.shape
    return pl.pallas_call(
        functools.partial(attend_kernel, scale, factor),
        grid=(pairs,),
        out_shape=[
            jax.ShapeDtypeStruct((pairs, sources, per_owner, PAIR), BF16),
            jax.ShapeDtypeStruct((8, PAIR), F32),
        ],
        in_specs=[
            pl.BlockSpec((1, sources, per_owner, width), lambda i: (i, 0, 0, 0)),
            pl.BlockSpec((sources, per_owner, PAIR), lambda i: (0, 0, 0)),
        ],
        out_specs=[
            pl.BlockSpec((1, sources, per_owner, PAIR), lambda i: (i, 0, 0, 0)),
            pl.BlockSpec((8, PAIR), lambda i: (0, 0)),
        ],
        compiler_params=pltpu.CompilerParams(vmem_limit_bytes=VMEM_LIMIT),
        name="attend",
    )(qkv, mask)


def attend_back_kernel(scale, qkv_ref, grad_ref, out_ref):
    _, sources, per_owner, _ = qkv_ref.shape
    size = CLUSTER // sources
    clusters = per_owner // size
    for cluster in range(clusters):
        q, k, v = (
            gather_rows(qkv_ref, (0,), cluster * size, size, slice(i * PAIR, (i + 1) * PAIR))
            for i in range(3)
        )
        grad = gather_rows(grad_ref, (0,), cluster * size, size, slice(None))
        q2, g2 = split_pair(q), split_pair(grad)
        scores = cluster_scores(q2, k, scale)
        top = jnp.max(scores, axis=1, keepdims=True)
        weights = jnp.exp(scores - top)
        probs = weights / jnp.sum(weights, axis=1, keepdims=True)
        low = probs.astype(BF16)
        d_value = dot_tn(low, g2)
        d_prob = dot_nt(g2, v)
        inner = jnp.sum(probs * d_prob, axis=1, keepdims=True)
        d_score = (probs * (d_prob - inner)).astype(BF16)
        d_query = (
            dot(jnp.concatenate([d_score[:CLUSTER], d_score[CLUSTER:]], axis=1), split_pair(k))
            * scale
        )
        d_key = dot_tn(d_score, q2) * scale
        for i, value in enumerate((d_query, d_key, d_value)):
            out_ref[
                0, :, cluster * size : (cluster + 1) * size, i * PAIR : (i + 1) * PAIR
            ] = spread_rows(value, sources, BF16)


def attend_back(qkv, grad, scale):
    pairs, sources, per_owner, width = qkv.shape
    return pl.pallas_call(
        functools.partial(attend_back_kernel, scale),
        grid=(pairs,),
        out_shape=jax.ShapeDtypeStruct((pairs, sources, per_owner, width), BF16),
        in_specs=[
            pl.BlockSpec((1, sources, per_owner, width), lambda i: (i, 0, 0, 0)),
            pl.BlockSpec((1, sources, per_owner, PAIR), lambda i: (i, 0, 0, 0)),
        ],
        out_specs=pl.BlockSpec((1, sources, per_owner, width), lambda i: (i, 0, 0, 0)),
        compiler_params=pltpu.CompilerParams(vmem_limit_bytes=VMEM_LIMIT),
        name="attend_back",
    )(qkv, grad)


INV_SQRT2 = 0.7071067811865476
INV_SQRT_2PI = 0.3989422804014327


def norm_parts(value):
    centred = value - jnp.mean(value, axis=1, keepdims=True)
    rate = lax.rsqrt(jnp.mean(centred * centred, axis=1, keepdims=True) + EPSILON)
    return centred * rate, rate


def norm_back(grad, gain, normed, rate):
    inner = grad * gain
    return rate * (
        inner
        - jnp.mean(inner, axis=1, keepdims=True)
        - normed * jnp.mean(inner * normed, axis=1, keepdims=True)
    )


TILE = 256
COLS = 768


def middle_kernel(
    x_ref,
    att_ref,
    grad_ref,
    places_ref,
    cols_ref,
    wo_ref,
    up_ref,
    down_ref,
    vec_ref,
    up_bias_ref,
    out_ref,
    dmid_ref,
    datt_ref,
    g_out_ref,
    g_up_ref,
    g_down_ref,
    gvec_ref,
    g_upb_ref,
    attended,
    hidden_all,
    act_all,
    dup_all,
    dffn_all,
    datt_all,
    slope,
    ret,
):
    tok, width = x_ref.shape
    wide = up_ref.shape[1]
    pairs = att_ref.shape[0]
    heads = 2 * pairs
    gvec_ref[...] = jnp.zeros_like(gvec_ref)
    g_upb_ref[...] = jnp.zeros_like(g_upb_ref)
    bo, g1, s1, bd, g2, s2 = (vec_ref[i : i + 1, :] for i in range(6))

    def column_sum(value):
        return jnp.sum(value, axis=0, keepdims=True)

    for pair in range(pairs):
        to = slice(pair * PAIR, (pair + 1) * PAIR)

        def spread(step, carry):
            rows = pl.ds(step * TILE, TILE)
            value = att_ref[pair, rows, :]
            low = head_lanes(value.shape)
            zero = jnp.zeros_like(value)
            ret[rows, :] = jnp.where(low, value, zero)
            ret[pl.ds(tok + step * TILE, TILE), :] = jnp.where(low, zero, value)
            return carry

        lax.fori_loop(0, tok // TILE, spread, 0)

        def unpermute(step, carry):
            start = step * TILE
            attended[pl.ds(start, TILE), to] = dot(
                token_rows(cols_ref, pair, start, TILE), ret[...]
            ).astype(BF16)
            return carry

        lax.fori_loop(0, tok // TILE, unpermute, 0)

    def tile(step, carry):
        rows = pl.ds(step * TILE, TILE)
        branch = dot(attended[rows, :], wo_ref[...]) + bo
        n1, r1 = norm_parts(x_ref[rows, :].astype(F32) + branch)
        hidden = (n1 * g1 + s1).astype(BF16)
        hidden_all[rows, :] = hidden
        ffn = jnp.zeros((TILE, width), F32)
        for col in range(0, wide, COLS):
            to = slice(col, col + COLS)
            pre = dot(hidden, up_ref[:, to]) + up_bias_ref[0:1, to]
            cdf = 0.5 * (1.0 + lax.erf(pre * INV_SQRT2))
            act = (pre * cdf).astype(BF16)
            slope[:, to] = cdf + pre * (jnp.exp(-0.5 * pre * pre) * INV_SQRT_2PI)
            act_all[rows, to] = act
            ffn += dot(act, down_ref[to, :])
        n2, r2 = norm_parts(hidden.astype(F32) + ffn + bd)
        out_ref[rows, :] = (n2 * g2 + s2).astype(BF16)
        mask = cols_ref[rows, heads : heads + 1].astype(F32)
        gout = grad_ref[rows, :].astype(F32) * mask
        gvec_ref[4:5, :] += column_sum(gout * n2)
        gvec_ref[5:6, :] += column_sum(gout)
        d_pre = norm_back(gout, g2, n2, r2)
        d_ffn = d_pre.astype(BF16)
        dffn_all[rows, :] = d_ffn
        gvec_ref[3:4, :] += column_sum(d_ffn.astype(F32))
        d_hidden = d_pre
        for col in range(0, wide, COLS):
            to = slice(col, col + COLS)
            d_up = (dot_nt(d_ffn, down_ref[to, :]) * slope[:, to]).astype(BF16)
            dup_all[rows, to] = d_up
            g_upb_ref[0:1, to] += column_sum(d_up.astype(F32))
            d_hidden += dot_nt(d_up, up_ref[:, to])
        gvec_ref[1:2, :] += column_sum(d_hidden * n1)
        gvec_ref[2:3, :] += column_sum(d_hidden)
        d_mid = norm_back(d_hidden, g1, n1, r1)
        d_branch = d_mid.astype(BF16)
        dmid_ref[rows, :] = d_branch
        gvec_ref[0:1, :] += column_sum(d_branch.astype(F32))
        datt_all[rows, :] = dot_nt(d_branch, wo_ref[...]).astype(BF16)
        return carry

    lax.fori_loop(0, tok // TILE, tile, 0)

    for pair in range(pairs):
        to = slice(pair * PAIR, (pair + 1) * PAIR)

        def spread(step, carry):
            rows = pl.ds(step * TILE, TILE)
            value = datt_all[rows, to]
            low = head_lanes(value.shape)
            zero = jnp.zeros_like(value)
            ret[rows, :] = jnp.where(low, value, zero)
            ret[pl.ds(tok + step * TILE, TILE), :] = jnp.where(low, zero, value)
            return carry

        lax.fori_loop(0, tok // TILE, spread, 0)

        def permute(step, carry):
            start = step * TILE
            datt_ref[pair, pl.ds(start, TILE), :] = dot(
                place_rows(places_ref, pair, start, TILE), ret[...]
            ).astype(BF16)
            return carry

        lax.fori_loop(0, tok // TILE, permute, 0)

    def weights(step, carry):
        to = pl.ds(pl.multiple_of(step * TILE, TILE), TILE)
        g_down_ref[to, :] = dot_tn(act_all[:, to], dffn_all[...]).astype(BF16)
        g_up_ref[:, to] = dot_tn(hidden_all[...], dup_all[:, to]).astype(BF16)
        return carry

    lax.fori_loop(0, wide // TILE, weights, 0)

    def out_weights(step, carry):
        to = pl.ds(pl.multiple_of(step * TILE, TILE), TILE)
        g_out_ref[:, to] = dot_tn(attended[...], dmid_ref[:, to]).astype(BF16)
        return carry

    lax.fori_loop(0, width // TILE, out_weights, 0)


def final_kernel(
    x_ref,
    ret_ref,
    dmid_ref,
    cols_ref,
    wq_ref,
    wk_ref,
    wv_ref,
    gtok_ref,
    gq_ref,
    gk_ref,
    gv_ref,
    gvec_ref,
    rhs,
    dqkv,
):
    tok, width = x_ref.shape
    pairs = ret_ref.shape[0]
    gvec_ref[...] = jnp.zeros_like(gvec_ref)
    for pair in range(pairs):

        def spread(step, carry):
            rows = pl.ds(step * TILE, TILE)
            for part in range(3):
                to = slice(part * PAIR, (part + 1) * PAIR)
                value = ret_ref[pair, rows, to]
                low = head_lanes(value.shape)
                zero = jnp.zeros_like(value)
                rhs[rows, to] = jnp.where(low, value, zero)
                rhs[pl.ds(tok + step * TILE, TILE), to] = jnp.where(low, zero, value)
            return carry

        lax.fori_loop(0, tok // TILE, spread, 0)

        def unpermute(step, carry):
            start = step * TILE
            value = dot(token_rows(cols_ref, pair, start, TILE), rhs[...])
            for part in range(3):
                piece = value[:, part * PAIR : (part + 1) * PAIR]
                dqkv[part, pl.ds(start, TILE), pair * PAIR : (pair + 1) * PAIR] = piece.astype(BF16)
                gvec_ref[part : part + 1, pair * PAIR : (pair + 1) * PAIR] += jnp.sum(
                    piece, axis=0, keepdims=True
                )
            return carry

        lax.fori_loop(0, tok // TILE, unpermute, 0)

    def tokens(step, carry):
        rows = pl.ds(step * TILE, TILE)
        total = dmid_ref[rows, :].astype(F32)
        for part, w_ref in enumerate((wq_ref, wk_ref, wv_ref)):
            total += dot_nt(dqkv[part, rows, :], w_ref[...])
        gtok_ref[rows, :] = total.astype(BF16)
        return carry

    lax.fori_loop(0, tok // TILE, tokens, 0)

    def weights(step, carry):
        to = pl.ds(pl.multiple_of(step * TILE, TILE), TILE)
        for part, g_ref in enumerate((gq_ref, gk_ref, gv_ref)):
            g_ref[:, to] = dot_tn(x_ref[...], dqkv[part, :, to]).astype(BF16)
        return carry

    lax.fori_loop(0, width // TILE, weights, 0)


def body(
    g,
    tokens,
    cluster_slot,
    loss_mask,
    out_grad,
    query_weight,
    key_weight,
    value_weight,
    output_weight,
    query_bias,
    value_bias,
    output_bias,
    first_gain,
    first_shift,
    up_weight,
    up_bias,
    down_weight,
    down_bias,
    second_gain,
    second_shift,
):
    tok, width = tokens.shape[1:]
    heads = cluster_slot.shape[1]
    pairs = heads // 2
    wide = up_weight.shape[1]
    per_owner = tok // g.seq
    scale = (width // heads) ** -0.5
    both = ("batch", "seq")
    swap = functools.partial(lax.ppermute, axis_name=both, perm=g.swap_pairs())

    slots = cluster_slot[0]
    places = slots // tok * per_owner + slots % tok // g.seq
    table = jnp.concatenate(
        [places, loss_mask, jnp.zeros((16 - heads - 1, tok), jnp.int32)], axis=0
    )
    table = swap(table)
    x = swap(tokens[0])
    grad = swap(out_grad[0])
    cols = table.T

    vectors = (
        query_bias,
        value_bias,
        output_bias,
        first_gain,
        first_shift,
        down_bias,
        second_gain,
        second_shift,
    )
    count = query_bias.shape[0]
    packed = jnp.concatenate([*vectors, up_bias])
    room = -packed.shape[0] % PAIR
    packed = jnp.pad(packed, (0, room)).reshape(-1, PAIR)
    weights = (query_weight, key_weight, value_weight, output_weight, up_weight, down_weight)
    gathered = gather(g, [packed, *weights])
    wq, wk, wv, wo, up, down = (
        item.reshape(g.n * item.shape[4], item.shape[5]) for item in gathered[1:]
    )
    flat = gathered[0].reshape(g.n, -1).astype(F32)
    rows = flat[:, : 8 * count].reshape(g.n, 8, count).transpose(1, 0, 2).reshape(8, width)
    up_row = flat[:, 8 * count : 8 * count + up_bias.shape[0]].reshape(1, wide)
    qkv_bias = jnp.stack([rows[0], jnp.zeros((width,), F32), rows[1]])

    sent, sent_mask = vmem_call(
        project_kernel,
        [
            jax.ShapeDtypeStruct((pairs, tok, 3 * PAIR), BF16),
            jax.ShapeDtypeStruct((tok, PAIR), BF16),
        ],
        [pltpu.VMEM((2 * tok, 4 * PAIR), BF16)],
        "project",
    )(x, wq, wk, wv, qkv_bias, table, cols)
    qkv, mask = exchange(
        g,
        [
            sent.reshape(pairs, g.seq, per_owner, 3 * PAIR),
            sent_mask.reshape(1, g.seq, per_owner, PAIR),
        ],
        2,
    )
    mixed, stats = attend(qkv, mask[0], scale, 1.0 / (heads * CLUSTER * g.batch))
    (returned,) = exchange(g, [mixed], 3)

    shape = jax.ShapeDtypeStruct
    (out, d_mid, d_att, g_out, g_up, g_down, g_rows, g_upb) = vmem_call(
        middle_kernel,
        [
            shape((tok, width), BF16),
            shape((tok, width), BF16),
            shape((pairs, tok, PAIR), BF16),
            shape((width, width), BF16),
            shape((width, wide), BF16),
            shape((wide, width), BF16),
            shape((8, width), F32),
            shape((8, wide), F32),
        ],
        [
            pltpu.VMEM((tok, width), BF16),
            pltpu.VMEM((tok, width), BF16),
            pltpu.VMEM((tok, wide), BF16),
            pltpu.VMEM((tok, wide), BF16),
            pltpu.VMEM((tok, width), BF16),
            pltpu.VMEM((tok, width), BF16),
            pltpu.VMEM((TILE, wide), F32),
            pltpu.VMEM((2 * tok, PAIR), BF16),
        ],
        "middle",
    )(x, returned.reshape(pairs, tok, PAIR), grad, table, cols, wo, up, down, rows[2:], up_row)

    (routed,) = exchange(g, [d_att.reshape(pairs, g.seq, per_owner, PAIR)], 4)
    d_qkv = attend_back(qkv, routed, scale)
    (d_home,) = exchange(g, [d_qkv], 5)

    grad_tokens, g_query, g_key, g_value, g_rows_attn = vmem_call(
        final_kernel,
        [
            shape((tok, width), BF16),
            shape((width, width), BF16),
            shape((width, width), BF16),
            shape((width, width), BF16),
            shape((8, width), F32),
        ],
        [
            pltpu.VMEM((2 * tok, 3 * PAIR), BF16),
            pltpu.VMEM((3, tok, width), BF16),
        ],
        "final",
    )(x, d_home.reshape(pairs, tok, 3 * PAIR), d_mid, cols, wq, wk, wv)

    lines = jnp.stack([g_rows_attn[0], g_rows_attn[2], *(g_rows[i] for i in range(6))])
    lines = lines.reshape(8, g.n, count).transpose(1, 0, 2).reshape(g.n, 8 * count)
    place = group_place(g)
    blocks = stats.shape[1] and tok // CLUSTER
    here = jnp.arange(g.n, dtype=jnp.int32)[:, None] % g.seq == place
    own = jnp.where(here, stats[:2, :blocks].reshape(1, 2 * blocks), 0.0)
    small = jnp.concatenate([lines, g_upb[0].reshape(g.n, wide // g.n), own], axis=1)
    used = small.shape[1]
    small = jnp.pad(small, ((0, 0), (0, -used % (8 * PAIR))))
    split = (g.Y, 2, Z, g.X)

    def parts(item):
        rows, cols = item.shape[0] // g.n, item.shape[1]
        if rows % 8:
            rows, cols = rows * cols // PAIR, PAIR
        return item.reshape(*split, rows, cols)

    sums = scatter(
        g,
        [
            small.reshape(*split, -1, PAIR),
            parts(g_up),
            parts(g_down),
            parts(g_out),
            parts(g_query),
            parts(g_key),
            parts(g_value),
        ],
    )
    vector = sums[0].reshape(-1)
    gq, gv, go, gg1, gs1, gd, gg2, gs2 = (
        vector[i * count : (i + 1) * count] for i in range(8)
    )
    gu = vector[8 * count : 8 * count + wide // g.n]
    cluster_stats = vector[used - 2 * blocks : used].reshape(2, blocks)
    s_up, s_down, s_out, s_query, s_key, s_value = (
        item.reshape(local.shape)
        for item, local in zip(
            sums[1:],
            (up_weight, down_weight, output_weight, query_weight, key_weight, value_weight),
        )
    )
    return (
        swap(out)[None],
        swap(grad_tokens)[None],
        s_query,
        s_key,
        s_value,
        s_out,
        gq,
        gv,
        go,
        gg1,
        gs1,
        s_up,
        gu,
        s_down,
        gd,
        gg2,
        gs2,
        cluster_stats,
    )


def solution(mesh):
    g = Grid(mesh)
    tokens, rows, flat = P("batch", "seq", None), P(("batch", "seq"), None), P(("batch", "seq"))
    return jax.shard_map(
        functools.partial(body, g),
        mesh=mesh,
        in_specs=(
            tokens,
            P("batch", None, "seq"),
            P("batch", "seq"),
            tokens,
            *([rows] * 4),
            *([flat] * 5),
            rows,
            flat,
            rows,
            *([flat] * 3),
        ),
        out_specs=(
            tokens,
            tokens,
            *([rows] * 4),
            *([flat] * 5),
            rows,
            flat,
            rows,
            *([flat] * 3),
            P(None, "seq"),
        ),
        check_vma=False,
    )
```

```python
import functools

import jax
import jax.numpy as jnp
from jax import lax
from jax.experimental import pallas as pl
from jax.experimental.pallas import tpu as pltpu
from jax.sharding import PartitionSpec as P

MESH = pl.DeviceIdType.MESH
F32 = jnp.float32
BF16 = jnp.bfloat16
EPSILON = 1e-12
CLUSTER = 128
PAIR = 128
Z = 4
VMEM_LIMIT = 58 * 1024 * 1024


class Grid:
    def __init__(self, mesh):
        self.batch, self.seq = mesh.shape["batch"], mesh.shape["seq"]
        self.Y, self.X = self.batch // 2, self.seq // Z
        self.half = self.seq // 2
        self.n = self.batch * self.seq

    def swap_pairs(self):
        pairs = []
        for b in range(self.batch):
            for s in range(self.seq):
                if b % 2 == s // self.half:
                    to = (b, s)
                else:
                    to = (b ^ 1, (s + self.half) % self.seq)
                pairs.append((b * self.seq + s, to[0] * self.seq + to[1]))
        return pairs


def coords(g):
    b, s = lax.axis_index("batch"), lax.axis_index("seq")
    return b // 2, b % 2, s // g.X, s % g.X


def device(g, y, c, z, x):
    return (y * 2 + c, z * g.X + x)


def group_place(g):
    b, s = lax.axis_index("batch"), lax.axis_index("seq")
    return b % 2 * g.half + s % g.half


def group_device(g, place):
    b, s = lax.axis_index("batch"), lax.axis_index("seq")
    return (b // 2 * 2 + place // g.half, s // g.half * g.half + place % g.half)


def line_peers(g):
    y, c, z, x = coords(g)
    peers = [device(g, y, c, (z + k) % Z, x) for k in range(1, Z)]
    peers += [device(g, y, c, z, (x + k) % g.X) for k in range(1, g.X)]
    peers += [device(g, (y + k) % g.Y, c, z, x) for k in range(1, g.Y)]
    peers.append(device(g, y, 1 - c, z, x))
    return peers


def greet(peers):
    barrier = pltpu.get_barrier_semaphore()
    for peer in peers:
        pl.semaphore_signal(barrier, inc=1, device_id=peer, device_id_type=MESH)
    pl.semaphore_wait(barrier, len(peers))


def remote(src, dst, send, recv, peer):
    return pltpu.make_async_remote_copy(
        src_ref=src,
        dst_ref=dst,
        send_sem=send,
        recv_sem=recv,
        device_id=peer,
        device_id_type=MESH,
    )


def lane_pieces(shape):
    rows, cols = shape
    if cols % PAIR or rows * cols <= 24 * 768:
        return [(0, cols)]
    count = {3072: 4, 768: 3}.get(cols, 1)
    return [(k * (cols // count), cols // count) for k in range(count)]


class Gather:
    def __init__(self, g, ins, outs, sends, recvs, local_sem, mixed):
        self.g, self.ins, self.outs = g, ins, outs
        self.sends, self.recvs, self.local_sem = sends, recvs, local_sem
        self.at = coords(g)
        self.mixed = mixed
        self.units = [
            (index, pl.ds(start, size))
            for index, item in enumerate(ins)
            for start, size in lane_pieces(item.shape)
        ]

    @staticmethod
    def slots(g, shapes):
        units = sum(len(lane_pieces(shape)) for shape in shapes)
        return units, units * (Z + g.X + g.Y - 2)

    def own(self, unit):
        index, cols = self.units[unit]
        y, c, z, x = self.at
        return pltpu.make_async_copy(
            self.ins[index].at[:, cols],
            self.outs[index].at[y, c, z, x, :, cols],
            self.local_sem.at[unit],
        )

    def moves(self, unit, level):
        g = self.g
        index, cols = self.units[unit]
        out = self.outs[index]
        y, c, z, x = self.at
        a = slice(None)
        base = unit * (Z + g.X + g.Y - 2)
        x_first = not self.mixed or unit % 2 == 0
        axis = ("z", "x" if x_first else "y", "y" if x_first else "x", "c")[level]
        base += (0, Z - 1, Z - 1 + (g.X if x_first else g.Y) - 1, Z + g.X + g.Y - 3)[level]
        if level == 0:
            part = (y, c, z, x)
        elif level == 1:
            part = (y, c, a, x)
        elif level == 2:
            part = (y, c, a, a) if x_first else (a, c, a, x)
        else:
            part = (a, c, a, a)
        view = out.at[(*part, a, cols)]
        src = self.ins[index].at[:, cols] if level == 0 else view
        size = {"z": Z, "x": g.X, "y": g.Y, "c": 2}[axis]
        made = []
        for k in range(1, size):
            peer = {
                "z": (y, c, (z + k) % Z, x),
                "x": (y, c, z, (x + k) % g.X),
                "y": ((y + k) % g.Y, c, z, x),
                "c": (y, 1 - c, z, x),
            }[axis]
            slot = base + k - 1
            made.append(
                remote(src, view, self.sends.at[slot], self.recvs.at[slot], device(g, *peer))
            )
        return made

    def start(self, unit, level):
        if level == 0:
            self.own(unit).start()
        else:
            if level == 1:
                self.own(unit).wait()
            for copy in self.moves(unit, level - 1):
                copy.wait_recv()
        for copy in self.moves(unit, level):
            copy.start()

    def finish(self):
        for unit in range(len(self.units)):
            for copy in self.moves(unit, 3):
                copy.wait_recv()
        for unit in range(len(self.units)):
            for level in range(4):
                for copy in self.moves(unit, level):
                    copy.wait_send()


class Swap:
    def __init__(self, g, src, dst, send, recv):
        b, s = lax.axis_index("batch"), lax.axis_index("seq")
        self.native = b % 2 == s // g.half
        self.peer = swap_partner(g)
        self.ends = (src, dst, send, recv)

    def start(self):
        src, dst, send, recv = self.ends

        @pl.when(self.native)
        def _():
            pltpu.make_async_copy(src, dst, recv).start()

        @pl.when(jnp.logical_not(self.native))
        def _():
            remote(src, dst, send, recv, self.peer).start()

    def wait(self):
        src, dst, send, recv = self.ends

        @pl.when(self.native)
        def _():
            pltpu.make_async_copy(src, dst, recv).wait()

        @pl.when(jnp.logical_not(self.native))
        def _():
            remote(src, dst, send, recv, self.peer).wait()


def swap_partner(g):
    b, s = lax.axis_index("batch"), lax.axis_index("seq")
    return (b // 2 * 2 + 1 - b % 2, (s + g.half) % g.seq)


def open_kernel(g, *refs):
    n = 5
    ins, outs = refs[:n], refs[n + 2 : 2 * n + 2]
    x_ref, table_ref = refs[n : n + 2]
    x_out, table_out = refs[2 * n + 2 : 2 * n + 4]
    sends, recvs, local_sem, swap_send, swap_recv = refs[2 * n + 4 :]
    greet(line_peers(g) + [swap_partner(g)])
    plan = Gather(g, ins, outs, sends, recvs, local_sem, True)
    count = len(plan.units)
    for unit in range(count):
        plan.start(unit, 0)
    swaps = [
        Swap(g, x_ref, x_out, swap_send.at[0], swap_recv.at[0]),
        Swap(g, table_ref, table_out, swap_send.at[1], swap_recv.at[1]),
    ]
    for swap in swaps:
        swap.start()
    lag = 2
    for t in range(count + 2 * lag):
        for level in range(1, 4):
            unit = t - (level - 1) * lag
            if 0 <= unit < count:
                plan.start(unit, level)
    plan.finish()
    for swap in swaps:
        swap.wait()


def open_call(g, arrays, x, table):
    units, slots = Gather.slots(g, [item.shape for item in arrays])
    any_space = pl.BlockSpec(memory_space=pl.ANY)
    shape = jax.ShapeDtypeStruct
    made = pl.pallas_call(
        functools.partial(open_kernel, g),
        out_shape=[
            *(shape((g.Y, 2, Z, g.X, *item.shape), item.dtype) for item in arrays),
            shape(x.shape, x.dtype),
            shape(table.shape, table.dtype),
        ],
        in_specs=[any_space] * (len(arrays) + 2),
        out_specs=[any_space] * (len(arrays) + 2),
        scratch_shapes=[
            pltpu.SemaphoreType.DMA((slots,)),
            pltpu.SemaphoreType.DMA((slots,)),
            pltpu.SemaphoreType.DMA((units,)),
            pltpu.SemaphoreType.DMA((2,)),
            pltpu.SemaphoreType.DMA((2,)),
        ],
        compiler_params=pltpu.CompilerParams(
            collective_id=0, has_side_effects=True, vmem_limit_bytes=VMEM_LIMIT
        ),
        name="open",
    )(*arrays, x, table)
    return made[:-2], made[-2], made[-1]


def scatter_kernel(g, shapes, *refs):
    n = len(shapes)
    ins, outs = refs[:n], refs[n : 2 * n]
    by_core, by_one, by_two, by_z = (refs[(2 + k) * n : (3 + k) * n] for k in range(4))
    sends, recvs = refs[6 * n :]
    y, c, z, x = coords(g)
    greet(line_peers(g))

    units = []
    for index, shape in enumerate(shapes):
        for start, size in lane_pieces(shape):
            units.append((index, slice(start, start + size)))

    per = Z + g.X + g.Y - 2

    def copies(number, level):
        index, cols = units[number]
        base = number * per
        every = slice(None)
        first_y = index % 2 == 0
        if level == 0:
            return [
                remote(
                    ins[index].at[:, 1 - c, :, :, :, cols],
                    by_core[index].at[:, :, :, :, cols],
                    sends.at[base],
                    recvs.at[base],
                    device(g, y, 1 - c, z, x),
                )
            ]
        base += 1
        along = {1: "y" if first_y else "x", 2: "x" if first_y else "y", 3: "z"}[level]
        if level == 2:
            base += (g.Y if first_y else g.X) - 1
        if level == 3:
            base += g.Y + g.X - 2
        size = {"y": g.Y, "x": g.X, "z": Z}[along]
        moves = []
        for k in range(1, size):
            if along == "y":
                to = (y + k) % g.Y
                peer = device(g, to, c, z, x)
            elif along == "x":
                to = (x + k) % g.X
                peer = device(g, y, c, z, to)
            else:
                to = (z + k) % Z
                peer = device(g, y, c, to, x)
            if level == 1 and first_y:
                src = by_core[index].at[to, :, :, :, cols]
            elif level == 1:
                src = by_core[index].at[:, :, to, :, cols]
            elif level == 2 and first_y:
                src = by_one[index].at[0, :, to, :, cols]
            elif level == 2:
                src = by_one[index].at[0, to, :, :, cols]
            else:
                src = by_two[index].at[0, to, :, cols]
            held = (by_one, by_two, by_z)[level - 1][index]
            slot = 0 if level < 3 else 0
            dst = held.at[(k, *([every] * (len(held.shape) - 2)), cols)]
            moves.append(remote(src, dst, sends.at[base + k - 1], recvs.at[base + k - 1], peer))
        return moves

    def add(number, level):
        index, cols = units[number]
        first_y = index % 2 == 0
        kind = ins[index].dtype
        if level == 0:

            def one(step, carry):
                for yy in range(g.Y):
                    for xx in range(g.X):
                        total = ins[index][yy, c, step, xx, :, cols].astype(F32)
                        total += by_core[index][yy, step, xx, :, cols].astype(F32)
                        by_core[index][yy, step, xx, :, cols] = total.astype(kind)
                return carry

            lax.fori_loop(0, Z, one, 0)
        elif level == 1:
            size, rest = (g.Y, g.X) if first_y else (g.X, g.Y)

            def one(step, carry):
                for r in range(rest):
                    if first_y:
                        total = by_core[index][y, step, r, :, cols].astype(F32)
                    else:
                        total = by_core[index][r, step, x, :, cols].astype(F32)
                    for k in range(1, size):
                        if first_y:
                            total += by_one[index][k, step, r, :, cols].astype(F32)
                        else:
                            total += by_one[index][k, r, step, :, cols].astype(F32)
                    if first_y:
                        by_one[index][0, step, r, :, cols] = total.astype(kind)
                    else:
                        by_one[index][0, r, step, :, cols] = total.astype(kind)
                return carry

            lax.fori_loop(0, Z, one, 0)
        elif level == 2:
            size = g.X if first_y else g.Y

            def one(step, carry):
                if first_y:
                    total = by_one[index][0, step, x, :, cols].astype(F32)
                else:
                    total = by_one[index][0, y, step, :, cols].astype(F32)
                for k in range(1, size):
                    total += by_two[index][k, step, :, cols].astype(F32)
                by_two[index][0, step, :, cols] = total.astype(kind)
                return carry

            lax.fori_loop(0, Z, one, 0)
        else:
            total = by_two[index][0, z, :, cols].astype(F32)
            for k in range(1, Z):
                total += by_z[index][k, :, cols].astype(F32)
            outs[index][:, cols] = total

    count = len(units)
    started = [[None] * 4 for _ in units]
    for t in range(count + 4):
        if t < count:
            started[t][0] = copies(t, 0)
            for copy in started[t][0]:
                copy.start()
        for level in range(4):
            u = t - level - 1
            if 0 <= u < count:
                for copy in started[u][level]:
                    copy.wait_recv()
                add(u, level)
                if level < 3:
                    started[u][level + 1] = copies(u, level + 1)
                    for copy in started[u][level + 1]:
                        copy.start()
    for levels in started:
        for moves in levels:
            for copy in moves:
                copy.wait_send()


def scatter(g, arrays):
    shapes = [item.shape[4:] for item in arrays]
    units = sum(len(lane_pieces(shape)) for shape in shapes)
    slots = units * (Z + g.X + g.Y - 2)
    scratch = [[], [], [], []]
    for index, (item, shape) in enumerate(zip(arrays, shapes)):
        scratch[0].append(pltpu.VMEM((g.Y, Z, g.X, *shape), item.dtype))
        if index % 2 == 0:
            scratch[1].append(pltpu.VMEM((g.Y, Z, g.X, *shape), item.dtype))
            scratch[2].append(pltpu.VMEM((g.X, Z, *shape), item.dtype))
        else:
            scratch[1].append(pltpu.VMEM((g.X, g.Y, Z, *shape), item.dtype))
            scratch[2].append(pltpu.VMEM((g.Y, Z, *shape), item.dtype))
        scratch[3].append(pltpu.VMEM((Z, *shape), item.dtype))
    return pl.pallas_call(
        functools.partial(scatter_kernel, g, shapes),
        out_shape=[jax.ShapeDtypeStruct(shape, F32) for shape in shapes],
        in_specs=[pl.BlockSpec(memory_space=pltpu.VMEM)] * len(arrays),
        out_specs=[pl.BlockSpec(memory_space=pltpu.VMEM)] * len(arrays),
        scratch_shapes=[item for level in scratch for item in level]
        + [pltpu.SemaphoreType.DMA((slots,)), pltpu.SemaphoreType.DMA((slots,))],
        compiler_params=pltpu.CompilerParams(
            collective_id=1, has_side_effects=True, vmem_limit_bytes=VMEM_LIMIT
        ),
        name="grad_scatter",
    )(*arrays)


def exchange_kernel(g, n, *refs):
    ins, outs = refs[:n], refs[n : 2 * n]
    sends, recvs, local_sem = refs[2 * n :]
    me = group_place(g)
    size = g.seq
    peers = [(me + k) % size for k in range(1, size)]
    greet([group_device(g, peer) for peer in peers])
    copies = []
    for index in range(n):
        own = pltpu.make_async_copy(
            ins[index].at[:, me], outs[index].at[:, me], local_sem.at[index]
        )
        own.start()
        for k, peer in enumerate(peers):
            slot = index * (size - 1) + k
            copy = remote(
                ins[index].at[:, peer],
                outs[index].at[:, me],
                sends.at[slot],
                recvs.at[slot],
                group_device(g, peer),
            )
            copy.start()
            copies.append(copy)
        copies.append(own)
    for copy in copies:
        copy.wait()


def exchange(g, arrays, number):
    n = len(arrays)
    return pl.pallas_call(
        functools.partial(exchange_kernel, g, n),
        out_shape=[jax.ShapeDtypeStruct(item.shape, item.dtype) for item in arrays],
        in_specs=[pl.BlockSpec(memory_space=pl.ANY)] * n,
        out_specs=[pl.BlockSpec(memory_space=pl.ANY)] * n,
        scratch_shapes=[
            pltpu.SemaphoreType.DMA((n * (g.seq - 1),)),
            pltpu.SemaphoreType.DMA((n * (g.seq - 1),)),
            pltpu.SemaphoreType.DMA((n,)),
        ],
        compiler_params=pltpu.CompilerParams(
            collective_id=number, has_side_effects=True, vmem_limit_bytes=VMEM_LIMIT
        ),
        name="exchange",
    )(*arrays)


def dot(left, right):
    return lax.dot_general(left, right, (((1,), (0,)), ((), ())), preferred_element_type=F32)


def dot_nt(left, right):
    return lax.dot_general(left, right, (((1,), (1,)), ((), ())), preferred_element_type=F32)


def dot_tn(left, right):
    return lax.dot_general(left, right, (((0,), (0,)), ((), ())), preferred_element_type=F32)


def head_lanes(shape):
    return lax.broadcasted_iota(jnp.int32, shape, 1) < PAIR // 2


def split_pair(value, axis=0):
    low = head_lanes(value.shape)
    zero = jnp.zeros_like(value)
    return jnp.concatenate(
        [jnp.where(low, value, zero), jnp.where(low, zero, value)], axis=axis
    )


def place_rows(places_ref, pair, start, size):
    tok = places_ref.shape[1]
    rows = lax.broadcasted_iota(jnp.int32, (size, tok), 0) + start
    parts = [
        (rows == places_ref[pl.ds(2 * pair + i, 1), :]).astype(F32).astype(BF16) for i in range(2)
    ]
    return jnp.concatenate(parts, axis=1)


def token_rows(cols_ref, pair, start, size):
    tok = cols_ref.shape[0]
    lanes = lax.broadcasted_iota(jnp.int32, (size, tok), 1)
    parts = [
        (lanes == cols_ref[pl.ds(start, size), 2 * pair + i : 2 * pair + i + 1])
        .astype(F32)
        .astype(BF16)
        for i in range(2)
    ]
    return jnp.concatenate(parts, axis=1)


def gather_rows(block_ref, lead, start, size, lanes):
    part = block_ref[(*lead, slice(None), pl.ds(start, size), lanes)]
    if size % 16:
        part = part.astype(F32)
    return part.reshape(part.shape[0] * size, part.shape[2]).astype(block_ref.dtype)


def spread_rows(value, sources, kind):
    size = value.shape[0] // sources
    if size % 16:
        return value.astype(F32).reshape(sources, size, value.shape[1]).astype(kind)
    return value.astype(kind).reshape(sources, size, value.shape[1])


ROWS = 256


def project_pair(pair, x_ref, w_refs, bias_ref, places_ref, cols_ref, out_ref, mask_ref, rhs):
    tok = x_ref.shape[0]
    heads = bias_ref.shape[1] // (PAIR // 2)
    lanes = lax.broadcasted_iota(jnp.int32, (ROWS, PAIR), 1)
    head = pl.ds(pl.multiple_of(pair * PAIR, PAIR), PAIR)

    def project(step, carry):
        rows = pl.ds(step * ROWS, ROWS)
        x = x_ref[rows, :]
        for part, w_ref in enumerate(w_refs):
            value = dot(x, w_ref[:, head]) + bias_ref[part : part + 1, head]
            value = value.astype(BF16)
            low = head_lanes(value.shape)
            zero = jnp.zeros_like(value)
            to = slice(part * PAIR, (part + 1) * PAIR)
            rhs[rows, to] = jnp.where(low, value, zero)
            rhs[pl.ds(tok + step * ROWS, ROWS), to] = jnp.where(low, zero, value)
        mask = cols_ref[rows, heads : heads + 1].astype(F32)
        for i in range(2):
            rhs[pl.ds(i * tok + step * ROWS, ROWS), 3 * PAIR :] = jnp.where(
                lanes == 2 * pair + i, mask, 0.0
            ).astype(BF16)
        return carry

    lax.fori_loop(0, tok // ROWS, project, 0)

    def permute(step, carry):
        rows = pl.ds(step * ROWS, ROWS)
        picked = dot(place_rows(places_ref, pair, step * ROWS, ROWS), rhs[...])
        out_ref[pair, rows, :] = picked[:, : 3 * PAIR].astype(BF16)
        mask_ref[rows, :] = mask_ref[rows, :] + picked[:, 3 * PAIR :].astype(BF16)
        return carry

    lax.fori_loop(0, tok // ROWS, permute, 0)


def attend_pair(pair, scale, qkv_ref, out_ref, entropy_ref):
    _, sources, per_owner, _ = qkv_ref.shape
    size = CLUSTER // sources
    clusters = per_owner // size
    lanes = lax.broadcasted_iota(jnp.int32, (CLUSTER, PAIR), 1)
    for cluster in range(clusters):
        q, k, v = (
            gather_rows(qkv_ref, (pair,), cluster * size, size, slice(i * PAIR, (i + 1) * PAIR))
            for i in range(3)
        )
        scores = cluster_scores(split_pair(q), k, scale)
        top = jnp.max(scores, axis=1, keepdims=True)
        weights = jnp.exp(scores - top)
        totals = jnp.sum(weights, axis=1, keepdims=True)
        probs = weights / totals
        entropy = top + jnp.log(totals) - jnp.sum(probs * scores, axis=1, keepdims=True)
        low = probs.astype(BF16)
        mixed = dot(
            jnp.concatenate([low[:CLUSTER], low[CLUSTER:]], axis=1), split_pair(v)
        )
        out_ref[pair, :, cluster * size : (cluster + 1) * size, :] = spread_rows(
            mixed, sources, BF16
        )
        entropy_ref[cluster] = jnp.where(
            lanes == 2 * pair,
            entropy[:CLUSTER],
            jnp.where(lanes == 2 * pair + 1, entropy[CLUSTER:], entropy_ref[cluster]),
        )


class Exchange:
    def __init__(self, g, src, dst, sends, recvs, local_sem):
        self.g, self.src, self.dst = g, src, dst
        self.sends, self.recvs, self.local_sem = sends, recvs, local_sem
        self.me = group_place(g)

    def block(self, pair, peer):
        if len(self.src.shape) == 4:
            return self.src.at[pair, peer]
        per = self.src.shape[1] // self.g.seq
        return self.src.at[pair, pl.ds(pl.multiple_of(peer * per, per), per), :]

    def own(self, pair):
        return pltpu.make_async_copy(
            self.block(pair, self.me), self.dst.at[pair, self.me], self.local_sem.at[pair]
        )

    def moves(self, pair):
        g = self.g
        made = []
        for k in range(1, g.seq):
            peer = (self.me + k) % g.seq
            made.append(
                remote(
                    self.block(pair, peer),
                    self.dst.at[pair, self.me],
                    self.sends.at[pair, k - 1],
                    self.recvs.at[pair, k - 1],
                    group_device(g, peer),
                )
            )
        return made

    def start(self, pair):
        for copy in self.moves(pair):
            copy.start()
        self.own(pair).start()

    def arrive(self, pair):
        self.own(pair).wait()
        for copy in self.moves(pair):
            copy.wait_recv()

    def sent(self, pair):
        for copy in self.moves(pair):
            copy.wait_send()


def exchange_sems(g, pairs):
    return [
        pltpu.SemaphoreType.DMA((pairs, g.seq - 1)),
        pltpu.SemaphoreType.DMA((pairs, g.seq - 1)),
        pltpu.SemaphoreType.DMA((pairs,)),
    ]


LAG = 2


def forward_kernel(
    g,
    scale,
    factor,
    x_ref,
    wq_ref,
    wk_ref,
    wv_ref,
    bias_ref,
    places_ref,
    cols_ref,
    up_ref,
    down_ref,
    grad_ref,
    up_all,
    down_all,
    grad_out,
    qkv_out,
    ret_out,
    stats_ref,
    rhs,
    sent,
    routed,
    mixed,
    mask_sent,
    mask_routed,
    entropy,
    *sems,
):
    pairs = sent.shape[0]
    group = [group_device(g, (group_place(g) + k) % g.seq) for k in range(1, g.seq)]
    greet(line_peers(g) + group + [swap_partner(g)])
    plan = Gather(g, [up_ref, down_ref], [up_all, down_all], *sems[:3], False)
    swap = Swap(g, grad_ref, grad_out, *(sem.at[0] for sem in sems[3:5]))
    there = Exchange(g, sent, routed, *sems[5:8])
    back = Exchange(g, mixed, ret_out, *sems[8:11])
    masks = Exchange(g, mask_sent, mask_routed, *sems[11:14])
    save_sem = sems[14]
    units = len(plan.units)

    def keep(pair):
        return pltpu.make_async_copy(routed.at[pair], qkv_out.at[pair], save_sem.at[pair])

    mask_sent[...] = jnp.zeros_like(mask_sent)
    entropy[...] = jnp.zeros_like(entropy)

    def step(t, carry):
        for when in range(pairs + LAG):
            todo = [
                (unit, level)
                for level in (3, 2, 1, 0)
                for unit in range(units)
                if unit // 2 + level == when
            ]
            if todo or when == 1:

                @pl.when(t == when)
                def _(todo=todo, when=when):
                    for unit, level in todo:
                        plan.start(unit, level)
                    if when == 1:
                        swap.start()

        @pl.when(t < pairs)
        def _():
            project_pair(
                t,
                x_ref,
                (wq_ref, wk_ref, wv_ref),
                bias_ref,
                places_ref,
                cols_ref,
                sent,
                mask_sent.at[0],
                rhs,
            )
            there.start(t)

        @pl.when(t == pairs - 1)
        def _():
            masks.start(0)

        @pl.when(t >= LAG)
        def _():
            pair = t - LAG
            there.arrive(pair)
            keep(pair).start()
            attend_pair(pair, scale, routed, mixed, entropy)
            back.start(pair)

        return carry

    lax.fori_loop(0, pairs + LAG, step, 0)

    masks.arrive(0)
    sources, per_owner = mask_routed.shape[1:3]
    size = CLUSTER // sources
    spot = lax.broadcasted_iota(jnp.int32, stats_ref.shape, 1)
    row = lax.broadcasted_iota(jnp.int32, stats_ref.shape, 0)
    stats = jnp.zeros(stats_ref.shape, F32)
    for cluster in range(per_owner // size):
        mask = gather_rows(mask_routed, (0,), cluster * size, size, slice(None)).astype(F32)
        entropy_sum = jnp.sum(entropy[cluster] * mask) * factor
        count = jnp.sum(mask) * factor
        stats += jnp.where(
            spot == cluster, jnp.where(row == 0, entropy_sum, jnp.where(row == 1, count, 0.0)), 0.0
        )
    stats_ref[...] = stats
    plan.finish()
    swap.wait()

    def close(pair, carry):
        keep(pair).wait()
        back.arrive(pair)
        there.sent(pair)
        back.sent(pair)
        return carry

    lax.fori_loop(0, pairs, close, 0)
    masks.sent(0)


def forward(g, scale, factor, x, wq, wk, wv, bias, places, cols, up, down, grad):
    tok, width = x.shape
    pairs = width // PAIR
    per_owner = tok // g.seq
    clusters = tok // CLUSTER
    units, slots = Gather.slots(g, [up.shape, down.shape])
    shape = jax.ShapeDtypeStruct
    any_space, vmem = pl.BlockSpec(memory_space=pl.ANY), pl.BlockSpec(memory_space=pltpu.VMEM)
    dma = pltpu.SemaphoreType.DMA
    return pl.pallas_call(
        functools.partial(forward_kernel, g, scale, factor),
        out_shape=[
            shape((g.Y, 2, Z, g.X, *up.shape), BF16),
            shape((g.Y, 2, Z, g.X, *down.shape), BF16),
            shape(grad.shape, BF16),
            shape((pairs, g.seq, per_owner, 3 * PAIR), BF16),
            shape((pairs, g.seq, per_owner, PAIR), BF16),
            shape((8, PAIR), F32),
        ],
        in_specs=[vmem] * 7 + [any_space] * 3,
        out_specs=[any_space] * 5 + [vmem],
        scratch_shapes=[
            pltpu.VMEM((2 * tok, 4 * PAIR), BF16),
            pltpu.VMEM((pairs, tok, 3 * PAIR), BF16),
            pltpu.VMEM((pairs, g.seq, per_owner, 3 * PAIR), BF16),
            pltpu.VMEM((pairs, g.seq, per_owner, PAIR), BF16),
            pltpu.VMEM((1, tok, PAIR), BF16),
            pltpu.VMEM((1, g.seq, per_owner, PAIR), BF16),
            pltpu.VMEM((clusters, CLUSTER, PAIR), F32),
            dma((slots,)),
            dma((slots,)),
            dma((units,)),
            dma((1,)),
            dma((1,)),
            *exchange_sems(g, pairs),
            *exchange_sems(g, pairs),
            *exchange_sems(g, 1),
            dma((pairs,)),
        ],
        compiler_params=pltpu.CompilerParams(
            collective_id=2, has_side_effects=True, vmem_limit_bytes=VMEM_LIMIT
        ),
        name="forward",
    )(x, wq, wk, wv, bias, places, cols, up, down, grad)


def vmem_call(kernel, out_shape, scratch, name):
    def call(*args):
        return pl.pallas_call(
            kernel,
            out_shape=out_shape,
            in_specs=[pl.BlockSpec(memory_space=pltpu.VMEM)] * len(args),
            out_specs=jax.tree.map(lambda _: pl.BlockSpec(memory_space=pltpu.VMEM), out_shape),
            scratch_shapes=scratch,
            compiler_params=pltpu.CompilerParams(vmem_limit_bytes=VMEM_LIMIT),
            name=name,
        )(*args)

    return call


def cluster_scores(q, k, scale):
    return dot_nt(q, k) * scale


def attend_back_kernel(scale, qkv_ref, grad_ref, out_ref):
    _, sources, per_owner, _ = qkv_ref.shape
    size = CLUSTER // sources
    clusters = per_owner // size
    for cluster in range(clusters):
        q, k, v = (
            gather_rows(qkv_ref, (0,), cluster * size, size, slice(i * PAIR, (i + 1) * PAIR))
            for i in range(3)
        )
        grad = gather_rows(grad_ref, (0,), cluster * size, size, slice(None))
        q2, g2 = split_pair(q), split_pair(grad)
        scores = cluster_scores(q2, k, scale)
        top = jnp.max(scores, axis=1, keepdims=True)
        weights = jnp.exp(scores - top)
        probs = weights / jnp.sum(weights, axis=1, keepdims=True)
        low = probs.astype(BF16)
        d_value = dot_tn(low, g2)
        d_prob = dot_nt(g2, v)
        inner = jnp.sum(probs * d_prob, axis=1, keepdims=True)
        d_score = (probs * (d_prob - inner)).astype(BF16)
        d_query = (
            dot(jnp.concatenate([d_score[:CLUSTER], d_score[CLUSTER:]], axis=1), split_pair(k))
            * scale
        )
        d_key = dot_tn(d_score, q2) * scale
        for i, value in enumerate((d_query, d_key, d_value)):
            out_ref[
                0, :, cluster * size : (cluster + 1) * size, i * PAIR : (i + 1) * PAIR
            ] = spread_rows(value, sources, BF16)


def attend_back(qkv, grad, scale):
    pairs, sources, per_owner, width = qkv.shape
    return pl.pallas_call(
        functools.partial(attend_back_kernel, scale),
        grid=(pairs,),
        out_shape=jax.ShapeDtypeStruct((pairs, sources, per_owner, width), BF16),
        in_specs=[
            pl.BlockSpec((1, sources, per_owner, width), lambda i: (i, 0, 0, 0)),
            pl.BlockSpec((1, sources, per_owner, PAIR), lambda i: (i, 0, 0, 0)),
        ],
        out_specs=pl.BlockSpec((1, sources, per_owner, width), lambda i: (i, 0, 0, 0)),
        compiler_params=pltpu.CompilerParams(vmem_limit_bytes=VMEM_LIMIT),
        name="attend_back",
    )(qkv, grad)


INV_SQRT2 = 0.7071067811865476
INV_SQRT_2PI = 0.3989422804014327


def norm_parts(value):
    centred = value - jnp.mean(value, axis=1, keepdims=True)
    rate = lax.rsqrt(jnp.mean(centred * centred, axis=1, keepdims=True) + EPSILON)
    return centred * rate, rate


def norm_back(grad, gain, normed, rate):
    inner = grad * gain
    return rate * (
        inner
        - jnp.mean(inner, axis=1, keepdims=True)
        - normed * jnp.mean(inner * normed, axis=1, keepdims=True)
    )


TILE = 256
COLS = 768


def middle_kernel(
    x_ref,
    att_ref,
    grad_ref,
    places_ref,
    cols_ref,
    wo_ref,
    up_ref,
    down_ref,
    vec_ref,
    up_bias_ref,
    out_ref,
    dmid_ref,
    datt_ref,
    g_out_ref,
    g_up_ref,
    g_down_ref,
    gvec_ref,
    g_upb_ref,
    attended,
    hidden_all,
    act_all,
    dup_all,
    dffn_all,
    datt_all,
    slope,
    ret,
):
    tok, width = x_ref.shape
    wide = up_ref.shape[1]
    pairs = att_ref.shape[0]
    heads = 2 * pairs
    gvec_ref[...] = jnp.zeros_like(gvec_ref)
    g_upb_ref[...] = jnp.zeros_like(g_upb_ref)
    bo, g1, s1, bd, g2, s2 = (vec_ref[i : i + 1, :] for i in range(6))

    def column_sum(value):
        return jnp.sum(value, axis=0, keepdims=True)

    for pair in range(pairs):
        to = slice(pair * PAIR, (pair + 1) * PAIR)

        def spread(step, carry):
            rows = pl.ds(step * TILE, TILE)
            value = att_ref[pair, rows, :]
            low = head_lanes(value.shape)
            zero = jnp.zeros_like(value)
            ret[rows, :] = jnp.where(low, value, zero)
            ret[pl.ds(tok + step * TILE, TILE), :] = jnp.where(low, zero, value)
            return carry

        lax.fori_loop(0, tok // TILE, spread, 0)

        def unpermute(step, carry):
            start = step * TILE
            attended[pl.ds(start, TILE), to] = dot(
                token_rows(cols_ref, pair, start, TILE), ret[...]
            ).astype(BF16)
            return carry

        lax.fori_loop(0, tok // TILE, unpermute, 0)

    def tile(step, carry):
        rows = pl.ds(step * TILE, TILE)
        branch = dot(attended[rows, :], wo_ref[...]) + bo
        n1, r1 = norm_parts(x_ref[rows, :].astype(F32) + branch)
        hidden = (n1 * g1 + s1).astype(BF16)
        hidden_all[rows, :] = hidden
        ffn = jnp.zeros((TILE, width), F32)
        for col in range(0, wide, COLS):
            to = slice(col, col + COLS)
            pre = dot(hidden, up_ref[:, to]) + up_bias_ref[0:1, to]
            cdf = 0.5 * (1.0 + lax.erf(pre * INV_SQRT2))
            act = (pre * cdf).astype(BF16)
            slope[:, to] = cdf + pre * (jnp.exp(-0.5 * pre * pre) * INV_SQRT_2PI)
            act_all[rows, to] = act
            ffn += dot(act, down_ref[to, :])
        n2, r2 = norm_parts(hidden.astype(F32) + ffn + bd)
        out_ref[rows, :] = (n2 * g2 + s2).astype(BF16)
        mask = cols_ref[rows, heads : heads + 1].astype(F32)
        gout = grad_ref[rows, :].astype(F32) * mask
        gvec_ref[4:5, :] += column_sum(gout * n2)
        gvec_ref[5:6, :] += column_sum(gout)
        d_pre = norm_back(gout, g2, n2, r2)
        d_ffn = d_pre.astype(BF16)
        dffn_all[rows, :] = d_ffn
        gvec_ref[3:4, :] += column_sum(d_ffn.astype(F32))
        d_hidden = d_pre
        for col in range(0, wide, COLS):
            to = slice(col, col + COLS)
            d_up = (dot_nt(d_ffn, down_ref[to, :]) * slope[:, to]).astype(BF16)
            dup_all[rows, to] = d_up
            g_upb_ref[0:1, to] += column_sum(d_up.astype(F32))
            d_hidden += dot_nt(d_up, up_ref[:, to])
        gvec_ref[1:2, :] += column_sum(d_hidden * n1)
        gvec_ref[2:3, :] += column_sum(d_hidden)
        d_mid = norm_back(d_hidden, g1, n1, r1)
        d_branch = d_mid.astype(BF16)
        dmid_ref[rows, :] = d_branch
        gvec_ref[0:1, :] += column_sum(d_branch.astype(F32))
        datt_all[rows, :] = dot_nt(d_branch, wo_ref[...]).astype(BF16)
        return carry

    lax.fori_loop(0, tok // TILE, tile, 0)

    for pair in range(pairs):
        to = slice(pair * PAIR, (pair + 1) * PAIR)

        def spread(step, carry):
            rows = pl.ds(step * TILE, TILE)
            value = datt_all[rows, to]
            low = head_lanes(value.shape)
            zero = jnp.zeros_like(value)
            ret[rows, :] = jnp.where(low, value, zero)
            ret[pl.ds(tok + step * TILE, TILE), :] = jnp.where(low, zero, value)
            return carry

        lax.fori_loop(0, tok // TILE, spread, 0)

        def permute(step, carry):
            start = step * TILE
            datt_ref[pair, pl.ds(start, TILE), :] = dot(
                place_rows(places_ref, pair, start, TILE), ret[...]
            ).astype(BF16)
            return carry

        lax.fori_loop(0, tok // TILE, permute, 0)

    def weights(step, carry):
        to = pl.ds(pl.multiple_of(step * TILE, TILE), TILE)
        g_down_ref[to, :] = dot_tn(act_all[:, to], dffn_all[...]).astype(BF16)
        g_up_ref[:, to] = dot_tn(hidden_all[...], dup_all[:, to]).astype(BF16)
        return carry

    lax.fori_loop(0, wide // TILE, weights, 0)

    def out_weights(step, carry):
        to = pl.ds(pl.multiple_of(step * TILE, TILE), TILE)
        g_out_ref[:, to] = dot_tn(attended[...], dmid_ref[:, to]).astype(BF16)
        return carry

    lax.fori_loop(0, width // TILE, out_weights, 0)


def final_kernel(
    x_ref,
    ret_ref,
    dmid_ref,
    cols_ref,
    wq_ref,
    wk_ref,
    wv_ref,
    gtok_ref,
    gq_ref,
    gk_ref,
    gv_ref,
    gvec_ref,
    rhs,
    dqkv,
):
    tok, width = x_ref.shape
    pairs = ret_ref.shape[0]
    gvec_ref[...] = jnp.zeros_like(gvec_ref)
    for pair in range(pairs):

        def spread(step, carry):
            rows = pl.ds(step * TILE, TILE)
            for part in range(3):
                to = slice(part * PAIR, (part + 1) * PAIR)
                value = ret_ref[pair, rows, to]
                low = head_lanes(value.shape)
                zero = jnp.zeros_like(value)
                rhs[rows, to] = jnp.where(low, value, zero)
                rhs[pl.ds(tok + step * TILE, TILE), to] = jnp.where(low, zero, value)
            return carry

        lax.fori_loop(0, tok // TILE, spread, 0)

        def unpermute(step, carry):
            start = step * TILE
            value = dot(token_rows(cols_ref, pair, start, TILE), rhs[...])
            for part in range(3):
                piece = value[:, part * PAIR : (part + 1) * PAIR]
                dqkv[part, pl.ds(start, TILE), pair * PAIR : (pair + 1) * PAIR] = piece.astype(BF16)
                gvec_ref[part : part + 1, pair * PAIR : (pair + 1) * PAIR] += jnp.sum(
                    piece, axis=0, keepdims=True
                )
            return carry

        lax.fori_loop(0, tok // TILE, unpermute, 0)

    def tokens(step, carry):
        rows = pl.ds(step * TILE, TILE)
        total = dmid_ref[rows, :].astype(F32)
        for part, w_ref in enumerate((wq_ref, wk_ref, wv_ref)):
            total += dot_nt(dqkv[part, rows, :], w_ref[...])
        gtok_ref[rows, :] = total.astype(BF16)
        return carry

    lax.fori_loop(0, tok // TILE, tokens, 0)

    def weights(step, carry):
        to = pl.ds(pl.multiple_of(step * TILE, TILE), TILE)
        for part, g_ref in enumerate((gq_ref, gk_ref, gv_ref)):
            g_ref[:, to] = dot_tn(x_ref[...], dqkv[part, :, to]).astype(BF16)
        return carry

    lax.fori_loop(0, width // TILE, weights, 0)


def body(
    g,
    tokens,
    cluster_slot,
    loss_mask,
    out_grad,
    query_weight,
    key_weight,
    value_weight,
    output_weight,
    query_bias,
    value_bias,
    output_bias,
    first_gain,
    first_shift,
    up_weight,
    up_bias,
    down_weight,
    down_bias,
    second_gain,
    second_shift,
):
    tok, width = tokens.shape[1:]
    heads = cluster_slot.shape[1]
    pairs = heads // 2
    wide = up_weight.shape[1]
    per_owner = tok // g.seq
    scale = (width // heads) ** -0.5
    both = ("batch", "seq")
    swap = functools.partial(lax.ppermute, axis_name=both, perm=g.swap_pairs())

    slots = cluster_slot[0]
    places = slots // tok * per_owner + slots % tok // g.seq
    table = jnp.concatenate(
        [places, loss_mask, jnp.zeros((16 - heads - 1, tok), jnp.int32)], axis=0
    )
    vectors = (
        query_bias,
        value_bias,
        output_bias,
        first_gain,
        first_shift,
        down_bias,
        second_gain,
        second_shift,
    )
    count = query_bias.shape[0]
    packed = jnp.concatenate([*vectors, up_bias])
    room = -packed.shape[0] % PAIR
    packed = jnp.pad(packed, (0, room)).reshape(-1, PAIR)
    weights = (query_weight, key_weight, value_weight, output_weight)
    gathered, x, table = open_call(g, [packed, *weights], tokens[0], table)
    cols = table.T
    wq, wk, wv, wo = (item.reshape(g.n * item.shape[4], item.shape[5]) for item in gathered[1:])
    flat = gathered[0].reshape(g.n, -1).astype(F32)
    rows = flat[:, : 8 * count].reshape(g.n, 8, count).transpose(1, 0, 2).reshape(8, width)
    up_row = flat[:, 8 * count : 8 * count + up_bias.shape[0]].reshape(1, wide)
    qkv_bias = jnp.stack([rows[0], jnp.zeros((width,), F32), rows[1]])

    up, down, grad, qkv, returned, stats = forward(
        g,
        scale,
        1.0 / (heads * CLUSTER * g.batch),
        x,
        wq,
        wk,
        wv,
        qkv_bias,
        table,
        cols,
        up_weight,
        down_weight,
        out_grad[0],
    )
    up, down = (item.reshape(g.n * item.shape[4], item.shape[5]) for item in (up, down))

    shape = jax.ShapeDtypeStruct
    (out, d_mid, d_att, g_out, g_up, g_down, g_rows, g_upb) = vmem_call(
        middle_kernel,
        [
            shape((tok, width), BF16),
            shape((tok, width), BF16),
            shape((pairs, tok, PAIR), BF16),
            shape((width, width), BF16),
            shape((width, wide), BF16),
            shape((wide, width), BF16),
            shape((8, width), F32),
            shape((8, wide), F32),
        ],
        [
            pltpu.VMEM((tok, width), BF16),
            pltpu.VMEM((tok, width), BF16),
            pltpu.VMEM((tok, wide), BF16),
            pltpu.VMEM((tok, wide), BF16),
            pltpu.VMEM((tok, width), BF16),
            pltpu.VMEM((tok, width), BF16),
            pltpu.VMEM((TILE, wide), F32),
            pltpu.VMEM((2 * tok, PAIR), BF16),
        ],
        "middle",
    )(x, returned.reshape(pairs, tok, PAIR), grad, table, cols, wo, up, down, rows[2:], up_row)

    (routed,) = exchange(g, [d_att.reshape(pairs, g.seq, per_owner, PAIR)], 4)
    d_qkv = attend_back(qkv, routed, scale)
    (d_home,) = exchange(g, [d_qkv], 5)

    grad_tokens, g_query, g_key, g_value, g_rows_attn = vmem_call(
        final_kernel,
        [
            shape((tok, width), BF16),
            shape((width, width), BF16),
            shape((width, width), BF16),
            shape((width, width), BF16),
            shape((8, width), F32),
        ],
        [
            pltpu.VMEM((2 * tok, 3 * PAIR), BF16),
            pltpu.VMEM((3, tok, width), BF16),
        ],
        "final",
    )(x, d_home.reshape(pairs, tok, 3 * PAIR), d_mid, cols, wq, wk, wv)

    lines = jnp.stack([g_rows_attn[0], g_rows_attn[2], *(g_rows[i] for i in range(6))])
    lines = lines.reshape(8, g.n, count).transpose(1, 0, 2).reshape(g.n, 8 * count)
    place = group_place(g)
    blocks = stats.shape[1] and tok // CLUSTER
    here = jnp.arange(g.n, dtype=jnp.int32)[:, None] % g.seq == place
    own = jnp.where(here, stats[:2, :blocks].reshape(1, 2 * blocks), 0.0)
    small = jnp.concatenate([lines, g_upb[0].reshape(g.n, wide // g.n), own], axis=1)
    used = small.shape[1]
    small = jnp.pad(small, ((0, 0), (0, -used % (8 * PAIR))))
    split = (g.Y, 2, Z, g.X)

    def parts(item):
        rows, cols = item.shape[0] // g.n, item.shape[1]
        if rows % 8:
            rows, cols = rows * cols // PAIR, PAIR
        return item.reshape(*split, rows, cols)

    sums = scatter(
        g,
        [
            small.reshape(*split, -1, PAIR),
            parts(g_up),
            parts(g_down),
            parts(g_out),
            parts(g_query),
            parts(g_key),
            parts(g_value),
        ],
    )
    vector = sums[0].reshape(-1)
    gq, gv, go, gg1, gs1, gd, gg2, gs2 = (
        vector[i * count : (i + 1) * count] for i in range(8)
    )
    gu = vector[8 * count : 8 * count + wide // g.n]
    cluster_stats = vector[used - 2 * blocks : used].reshape(2, blocks)
    s_up, s_down, s_out, s_query, s_key, s_value = (
        item.reshape(local.shape)
        for item, local in zip(
            sums[1:],
            (up_weight, down_weight, output_weight, query_weight, key_weight, value_weight),
        )
    )
    return (
        swap(out)[None],
        swap(grad_tokens)[None],
        s_query,
        s_key,
        s_value,
        s_out,
        gq,
        gv,
        go,
        gg1,
        gs1,
        s_up,
        gu,
        s_down,
        gd,
        gg2,
        gs2,
        cluster_stats,
    )


def solution(mesh):
    g = Grid(mesh)
    tokens, rows, flat = P("batch", "seq", None), P(("batch", "seq"), None), P(("batch", "seq"))
    return jax.shard_map(
        functools.partial(body, g),
        mesh=mesh,
        in_specs=(
            tokens,
            P("batch", None, "seq"),
            P("batch", "seq"),
            tokens,
            *([rows] * 4),
            *([flat] * 5),
            rows,
            flat,
            rows,
            *([flat] * 3),
        ),
        out_specs=(
            tokens,
            tokens,
            *([rows] * 4),
            *([flat] * 5),
            rows,
            flat,
            rows,
            *([flat] * 3),
            P(None, "seq"),
        ),
        check_vma=False,
    )
```

```python
import functools

import jax
import jax.numpy as jnp
from jax import lax
from jax.experimental import pallas as pl
from jax.experimental.pallas import tpu as pltpu
from jax.sharding import PartitionSpec as P

MESH = pl.DeviceIdType.MESH
F32 = jnp.float32
BF16 = jnp.bfloat16
EPSILON = 1e-12
CLUSTER = 128
PAIR = 128
Z = 4
VMEM_LIMIT = 58 * 1024 * 1024


class Grid:
    def __init__(self, mesh):
        self.batch, self.seq = mesh.shape["batch"], mesh.shape["seq"]
        self.Y, self.X = self.batch // 2, self.seq // Z
        self.half = self.seq // 2
        self.n = self.batch * self.seq


def coords(g):
    b, s = lax.axis_index("batch"), lax.axis_index("seq")
    return b // 2, b % 2, s // g.X, s % g.X


def device(g, y, c, z, x):
    return (y * 2 + c, z * g.X + x)


def group_place(g):
    b, s = lax.axis_index("batch"), lax.axis_index("seq")
    return b % 2 * g.half + s % g.half


def group_device(g, place):
    b, s = lax.axis_index("batch"), lax.axis_index("seq")
    return (b // 2 * 2 + place // g.half, s // g.half * g.half + place % g.half)


def line_peers(g):
    y, c, z, x = coords(g)
    peers = [device(g, y, c, (z + k) % Z, x) for k in range(1, Z)]
    peers += [device(g, y, c, z, (x + k) % g.X) for k in range(1, g.X)]
    peers += [device(g, (y + k) % g.Y, c, z, x) for k in range(1, g.Y)]
    peers.append(device(g, y, 1 - c, z, x))
    return peers


def greet(peers):
    barrier = pltpu.get_barrier_semaphore()
    for peer in peers:
        pl.semaphore_signal(barrier, inc=1, device_id=peer, device_id_type=MESH)
    pl.semaphore_wait(barrier, len(peers))


def remote(src, dst, send, recv, peer):
    return pltpu.make_async_remote_copy(
        src_ref=src,
        dst_ref=dst,
        send_sem=send,
        recv_sem=recv,
        device_id=peer,
        device_id_type=MESH,
    )


def lane_pieces(shape):
    rows, cols = shape
    if cols % PAIR or rows * cols <= 24 * 768:
        return [(0, cols)]
    count = {3072: 4, 768: 3}.get(cols, 1)
    return [(k * (cols // count), cols // count) for k in range(count)]


class Gather:
    def __init__(self, g, ins, outs, sends, recvs, local_sem, mixed):
        self.g, self.ins, self.outs = g, ins, outs
        self.sends, self.recvs, self.local_sem = sends, recvs, local_sem
        self.at = coords(g)
        self.mixed = mixed
        self.units = [
            (index, pl.ds(start, size))
            for index, item in enumerate(ins)
            for start, size in lane_pieces(item.shape)
        ]

    @staticmethod
    def slots(g, shapes):
        units = sum(len(lane_pieces(shape)) for shape in shapes)
        return units, units * (Z + g.X + g.Y - 2)

    def own(self, unit):
        index, cols = self.units[unit]
        y, c, z, x = self.at
        return pltpu.make_async_copy(
            self.ins[index].at[:, cols],
            self.outs[index].at[y, c, z, x, :, cols],
            self.local_sem.at[unit],
        )

    def moves(self, unit, level):
        g = self.g
        index, cols = self.units[unit]
        out = self.outs[index]
        y, c, z, x = self.at
        a = slice(None)
        base = unit * (Z + g.X + g.Y - 2)
        x_first = not self.mixed or unit % 2 == 0
        axis = ("z", "x" if x_first else "y", "y" if x_first else "x", "c")[level]
        base += (0, Z - 1, Z - 1 + (g.X if x_first else g.Y) - 1, Z + g.X + g.Y - 3)[level]
        if level == 0:
            part = (y, c, z, x)
        elif level == 1:
            part = (y, c, a, x)
        elif level == 2:
            part = (y, c, a, a) if x_first else (a, c, a, x)
        else:
            part = (a, c, a, a)
        view = out.at[(*part, a, cols)]
        src = self.ins[index].at[:, cols] if level == 0 else view
        size = {"z": Z, "x": g.X, "y": g.Y, "c": 2}[axis]
        made = []
        for k in range(1, size):
            peer = {
                "z": (y, c, (z + k) % Z, x),
                "x": (y, c, z, (x + k) % g.X),
                "y": ((y + k) % g.Y, c, z, x),
                "c": (y, 1 - c, z, x),
            }[axis]
            slot = base + k - 1
            made.append(
                remote(src, view, self.sends.at[slot], self.recvs.at[slot], device(g, *peer))
            )
        return made

    def start(self, unit, level):
        if level == 0:
            self.own(unit).start()
        else:
            if level == 1:
                self.own(unit).wait()
            for copy in self.moves(unit, level - 1):
                copy.wait_recv()
        for copy in self.moves(unit, level):
            copy.start()

    def finish(self):
        for unit in range(len(self.units)):
            for copy in self.moves(unit, 3):
                copy.wait_recv()
        for unit in range(len(self.units)):
            for level in range(4):
                for copy in self.moves(unit, level):
                    copy.wait_send()


class Swap:
    def __init__(self, g, src, dst, send, recv):
        b, s = lax.axis_index("batch"), lax.axis_index("seq")
        self.native = b % 2 == s // g.half
        self.peer = swap_partner(g)
        self.ends = (src, dst, send, recv)

    def start(self):
        src, dst, send, recv = self.ends

        @pl.when(self.native)
        def _():
            pltpu.make_async_copy(src, dst, recv).start()

        @pl.when(jnp.logical_not(self.native))
        def _():
            remote(src, dst, send, recv, self.peer).start()

    def wait(self):
        src, dst, send, recv = self.ends

        @pl.when(self.native)
        def _():
            pltpu.make_async_copy(src, dst, recv).wait()

        @pl.when(jnp.logical_not(self.native))
        def _():
            remote(src, dst, send, recv, self.peer).wait()


def swap_partner(g):
    b, s = lax.axis_index("batch"), lax.axis_index("seq")
    return (b // 2 * 2 + 1 - b % 2, (s + g.half) % g.seq)


def open_kernel(g, *refs):
    n = 5
    ins, outs = refs[:n], refs[n + 2 : 2 * n + 2]
    x_ref, table_ref = refs[n : n + 2]
    x_out, table_out = refs[2 * n + 2 : 2 * n + 4]
    sends, recvs, local_sem, swap_send, swap_recv = refs[2 * n + 4 :]
    greet(line_peers(g) + [swap_partner(g)])
    plan = Gather(g, ins, outs, sends, recvs, local_sem, True)
    count = len(plan.units)
    for unit in range(count):
        plan.start(unit, 0)
    swaps = [
        Swap(g, x_ref, x_out, swap_send.at[0], swap_recv.at[0]),
        Swap(g, table_ref, table_out, swap_send.at[1], swap_recv.at[1]),
    ]
    for swap in swaps:
        swap.start()
    lag = 2
    for t in range(count + 2 * lag):
        for level in range(1, 4):
            unit = t - (level - 1) * lag
            if 0 <= unit < count:
                plan.start(unit, level)
    plan.finish()
    for swap in swaps:
        swap.wait()


def open_call(g, arrays, x, table):
    units, slots = Gather.slots(g, [item.shape for item in arrays])
    any_space = pl.BlockSpec(memory_space=pl.ANY)
    shape = jax.ShapeDtypeStruct
    made = pl.pallas_call(
        functools.partial(open_kernel, g),
        out_shape=[
            *(shape((g.Y, 2, Z, g.X, *item.shape), item.dtype) for item in arrays),
            shape(x.shape, x.dtype),
            shape(table.shape, table.dtype),
        ],
        in_specs=[any_space] * (len(arrays) + 2),
        out_specs=[any_space] * (len(arrays) + 2),
        scratch_shapes=[
            pltpu.SemaphoreType.DMA((slots,)),
            pltpu.SemaphoreType.DMA((slots,)),
            pltpu.SemaphoreType.DMA((units,)),
            pltpu.SemaphoreType.DMA((2,)),
            pltpu.SemaphoreType.DMA((2,)),
        ],
        compiler_params=pltpu.CompilerParams(
            collective_id=0, has_side_effects=True, vmem_limit_bytes=VMEM_LIMIT
        ),
        name="open",
    )(*arrays, x, table)
    return made[:-2], made[-2], made[-1]


class Scatter:
    def __init__(self, g, ins, outs, bufs, sends, recvs, mixed):
        self.g, self.ins, self.outs, self.bufs = g, ins, outs, bufs
        self.sends, self.recvs, self.mixed = sends, recvs, mixed
        self.at = coords(g)
        self.units = [
            (index, pl.ds(start, size))
            for index, item in enumerate(ins)
            for start, size in lane_pieces(item.shape[4:])
        ]

    @staticmethod
    def scratch(g, shapes, mixed):
        made = []
        for index, (y, _, z, x, rows, cols) in enumerate(shapes):
            made.append(pltpu.VMEM((y, z, x, rows, cols), BF16))
            if Scatter.y_first(index, mixed):
                made.append(pltpu.VMEM((max(y - 1, 1), z, x, rows, cols), BF16))
                made.append(pltpu.VMEM((max(x - 1, 1), z, rows, cols), BF16))
            else:
                made.append(pltpu.VMEM((max(x - 1, 1), y, z, rows, cols), BF16))
                made.append(pltpu.VMEM((max(y - 1, 1), z, rows, cols), BF16))
            made.append(pltpu.VMEM((z - 1, rows, cols), BF16))
        units = sum(len(lane_pieces(shape[4:])) for shape in shapes)
        slots = units * (Z + g.X + g.Y - 2)
        return [*made, pltpu.SemaphoreType.DMA((slots,)), pltpu.SemaphoreType.DMA((slots,))]

    @staticmethod
    def y_first(index, mixed):
        return not mixed or index % 2 == 0

    def moves(self, unit, level):
        g = self.g
        index, cols = self.units[unit]
        y, c, z, x = self.at
        a = slice(None)
        core, one, two, three = self.bufs[4 * index : 4 * index + 4]
        y_first = self.y_first(index, self.mixed)
        axis = ("c", "y" if y_first else "x", "x" if y_first else "y", "z")[level]
        base = unit * (Z + g.X + g.Y - 2)
        base += (0, 1, (g.Y if y_first else g.X), g.X + g.Y - 1)[level]
        if level == 0:
            return [
                remote(
                    self.ins[index].at[a, 1 - c, a, a, a, cols],
                    core.at[a, a, a, a, cols],
                    self.sends.at[base],
                    self.recvs.at[base],
                    device(g, y, 1 - c, z, x),
                )
            ]
        held = (one, two, three)[level - 1]
        size = {"y": g.Y, "x": g.X, "z": Z}[axis]
        made = []
        for k in range(1, size):
            to_y, to_x, to_z = (y + k) % g.Y, (x + k) % g.X, (z + k) % Z
            peer, src = {
                ("y", 1): ((to_y, c, z, x), (to_y, a, a)),
                ("x", 1): ((y, c, z, to_x), (a, a, to_x)),
                ("x", 2): ((y, c, z, to_x), (y, a, to_x)),
                ("y", 2): ((to_y, c, z, x), (to_y, a, x)),
                ("z", 3): ((y, c, to_z, x), (y, to_z, x)),
            }[axis, level]
            rest = (a,) * (len(held.shape) - 2)
            slot = base + k - 1
            made.append(
                remote(
                    core.at[(*src, a, cols)],
                    held.at[(k - 1, *rest, cols)],
                    self.sends.at[slot],
                    self.recvs.at[slot],
                    device(g, *peer),
                )
            )
        return made

    def add(self, unit, level):
        g = self.g
        index, cols = self.units[unit]
        y, c, z, x = self.at
        core, one, two, three = self.bufs[4 * index : 4 * index + 4]
        y_first = self.y_first(index, self.mixed)
        a = slice(None)

        def fold(where, *others):
            total = core[(*where, a, cols)].astype(F32)
            for ref, spot in others:
                total += ref[(*spot, a, cols)].astype(F32)
            core[(*where, a, cols)] = total.astype(BF16)

        if level == 3:
            total = core[y, z, x, :, cols].astype(F32)
            for k in range(Z - 1):
                total += three[k, :, cols].astype(F32)
            self.outs[index][:, cols] = total
            return

        def one_z(zz, carry):
            if level == 0:
                for yy in range(g.Y):
                    for xx in range(g.X):
                        fold((yy, zz, xx), (self.ins[index], (yy, c, zz, xx)))
            elif level == 1 and y_first:
                for xx in range(g.X):
                    fold((y, zz, xx), *((one, (k, zz, xx)) for k in range(g.Y - 1)))
            elif level == 1:
                for yy in range(g.Y):
                    fold((yy, zz, x), *((one, (k, yy, zz)) for k in range(g.X - 1)))
            else:
                size = g.X if y_first else g.Y
                fold((y, zz, x), *((two, (k, zz)) for k in range(size - 1)))
            return carry

        lax.fori_loop(0, Z, one_z, 0)

    def step(self, unit, level):
        if level:
            for copy in self.moves(unit, level - 1):
                copy.wait_recv()
            self.add(unit, level - 1)
        if level < 4:
            for copy in self.moves(unit, level):
                copy.start()

    def sent(self):
        for unit in range(len(self.units)):
            for level in range(4):
                for copy in self.moves(unit, level):
                    copy.wait_send()


class Total:
    def __init__(self, g, held, bufs, sends, recvs):
        self.g, self.held, self.bufs = g, held, bufs
        self.sends, self.recvs = sends, recvs
        self.at = coords(g)

    @staticmethod
    def scratch(g, shape):
        sizes = (2, g.Y, g.X, Z)
        slots = sum(sizes)
        return [
            *(pltpu.VMEM((size, *shape), F32) for size in sizes),
            pltpu.SemaphoreType.DMA((slots,)),
            pltpu.SemaphoreType.DMA((slots,)),
        ]

    def moves(self, level):
        g = self.g
        y, c, z, x = self.at
        sizes = (2, g.Y, g.X, Z)
        mine = (c, y, x, z)[level]
        made = []
        for k in range(1, sizes[level]):
            to = (mine + k) % sizes[level]
            peer = ((y, to, z, x), (to, c, z, x), (y, c, z, to), (y, c, to, x))[level]
            slot = sum(sizes[:level]) + k
            view = self.bufs[level].at[mine]
            made.append(
                remote(view, view, self.sends.at[slot], self.recvs.at[slot], device(g, *peer))
            )
        return made

    def start(self, level, value):
        y, c, z, x = self.at
        self.bufs[level][(c, y, x, z)[level]] = value
        for copy in self.moves(level):
            copy.start()

    def take(self, level):
        for copy in self.moves(level):
            copy.wait_recv()
        buf = self.bufs[level]
        total = buf[0]
        for k in range(1, buf.shape[0]):
            total = total + buf[k]
        return total

    def sent(self):
        for level in range(4):
            for copy in self.moves(level):
                copy.wait_send()


def dot(left, right):
    return lax.dot_general(left, right, (((1,), (0,)), ((), ())), preferred_element_type=F32)


def dot_nt(left, right):
    return lax.dot_general(left, right, (((1,), (1,)), ((), ())), preferred_element_type=F32)


def dot_tn(left, right):
    return lax.dot_general(left, right, (((0,), (0,)), ((), ())), preferred_element_type=F32)


def head_lanes(shape):
    return lax.broadcasted_iota(jnp.int32, shape, 1) < PAIR // 2


def split_pair(value, axis=0):
    low = head_lanes(value.shape)
    zero = jnp.zeros_like(value)
    return jnp.concatenate(
        [jnp.where(low, value, zero), jnp.where(low, zero, value)], axis=axis
    )


def place_rows(places_ref, pair, start, size):
    tok = places_ref.shape[1]
    rows = lax.broadcasted_iota(jnp.int32, (size, tok), 0) + start
    parts = [
        (rows == places_ref[pl.ds(2 * pair + i, 1), :]).astype(F32).astype(BF16) for i in range(2)
    ]
    return jnp.concatenate(parts, axis=1)


def token_rows(cols_ref, pair, start, size):
    tok, width = cols_ref.shape
    lanes = lax.broadcasted_iota(jnp.int32, (size, tok), 1)
    heads = lax.broadcasted_iota(jnp.int32, (size, width), 1)
    table = cols_ref[pl.ds(start, size), :].astype(F32)
    parts = []
    for i in range(2):
        place = jnp.sum(jnp.where(heads == 2 * pair + i, table, 0.0), axis=1, keepdims=True)
        parts.append((lanes == place.astype(jnp.int32)).astype(F32).astype(BF16))
    return jnp.concatenate(parts, axis=1)


def gather_rows(block_ref, lead, start, size, lanes):
    part = block_ref[(*lead, slice(None), pl.ds(start, size), lanes)]
    if size % 16:
        part = part.astype(F32)
    return part.reshape(part.shape[0] * size, part.shape[2]).astype(block_ref.dtype)


def spread_rows(value, sources, kind):
    size = value.shape[0] // sources
    if size % 16:
        return value.astype(F32).reshape(sources, size, value.shape[1]).astype(kind)
    return value.astype(kind).reshape(sources, size, value.shape[1])


ROWS = 256


def project_pair(pair, x_ref, w_refs, bias_ref, places_ref, cols_ref, out_ref, mask_ref, rhs):
    tok = x_ref.shape[0]
    heads = bias_ref.shape[1] // (PAIR // 2)
    lanes = lax.broadcasted_iota(jnp.int32, (ROWS, PAIR), 1)
    head = pl.ds(pl.multiple_of(pair * PAIR, PAIR), PAIR)

    def project(step, carry):
        rows = pl.ds(step * ROWS, ROWS)
        x = x_ref[rows, :]
        for part, w_ref in enumerate(w_refs):
            value = dot(x, w_ref[:, head]) + bias_ref[part : part + 1, head]
            value = value.astype(BF16)
            low = head_lanes(value.shape)
            zero = jnp.zeros_like(value)
            to = slice(part * PAIR, (part + 1) * PAIR)
            rhs[rows, to] = jnp.where(low, value, zero)
            rhs[pl.ds(tok + step * ROWS, ROWS), to] = jnp.where(low, zero, value)
        mask = cols_ref[rows, heads : heads + 1].astype(F32)
        for i in range(2):
            rhs[pl.ds(i * tok + step * ROWS, ROWS), 3 * PAIR :] = jnp.where(
                lanes == 2 * pair + i, mask, 0.0
            ).astype(BF16)
        return carry

    lax.fori_loop(0, tok // ROWS, project, 0)

    def permute(step, carry):
        rows = pl.ds(step * ROWS, ROWS)
        picked = dot(place_rows(places_ref, pair, step * ROWS, ROWS), rhs[...])
        out_ref[pair, rows, :] = picked[:, : 3 * PAIR].astype(BF16)
        mask_ref[rows, :] = mask_ref[rows, :] + picked[:, 3 * PAIR :].astype(BF16)
        return carry

    lax.fori_loop(0, tok // ROWS, permute, 0)


def attend_pair(pair, scale, qkv_ref, out_ref, entropy_ref):
    _, sources, per_owner, _ = qkv_ref.shape
    size = CLUSTER // sources
    clusters = per_owner // size
    lanes = lax.broadcasted_iota(jnp.int32, (CLUSTER, PAIR), 1)
    for cluster in range(clusters):
        q, k, v = (
            gather_rows(qkv_ref, (pair,), cluster * size, size, slice(i * PAIR, (i + 1) * PAIR))
            for i in range(3)
        )
        scores = cluster_scores(split_pair(q), k, scale)
        top = jnp.max(scores, axis=1, keepdims=True)
        weights = jnp.exp(scores - top)
        totals = jnp.sum(weights, axis=1, keepdims=True)
        probs = weights / totals
        entropy = top + jnp.log(totals) - jnp.sum(probs * scores, axis=1, keepdims=True)
        low = probs.astype(BF16)
        mixed = dot(
            jnp.concatenate([low[:CLUSTER], low[CLUSTER:]], axis=1), split_pair(v)
        )
        out_ref[pair, :, cluster * size : (cluster + 1) * size, :] = spread_rows(
            mixed, sources, BF16
        )
        entropy_ref[cluster] = jnp.where(
            lanes == 2 * pair,
            entropy[:CLUSTER],
            jnp.where(lanes == 2 * pair + 1, entropy[CLUSTER:], entropy_ref[cluster]),
        )


class Exchange:
    def __init__(self, g, src, dst, sends, recvs, local_sem):
        self.g, self.src, self.dst = g, src, dst
        self.sends, self.recvs, self.local_sem = sends, recvs, local_sem
        self.me = group_place(g)

    def block(self, pair, peer):
        if len(self.src.shape) == 4:
            return self.src.at[pair, peer]
        per = self.src.shape[1] // self.g.seq
        return self.src.at[pair, pl.ds(pl.multiple_of(peer * per, per), per), :]

    def own(self, pair):
        return pltpu.make_async_copy(
            self.block(pair, self.me), self.dst.at[pair, self.me], self.local_sem.at[pair]
        )

    def moves(self, pair):
        g = self.g
        made = []
        for k in range(1, g.seq):
            peer = (self.me + k) % g.seq
            made.append(
                remote(
                    self.block(pair, peer),
                    self.dst.at[pair, self.me],
                    self.sends.at[pair, k - 1],
                    self.recvs.at[pair, k - 1],
                    group_device(g, peer),
                )
            )
        return made

    def start(self, pair):
        for copy in self.moves(pair):
            copy.start()
        self.own(pair).start()

    def arrive(self, pair):
        self.own(pair).wait()
        for copy in self.moves(pair):
            copy.wait_recv()

    def sent(self, pair):
        for copy in self.moves(pair):
            copy.wait_send()


def exchange_sems(g, pairs):
    return [
        pltpu.SemaphoreType.DMA((pairs, g.seq - 1)),
        pltpu.SemaphoreType.DMA((pairs, g.seq - 1)),
        pltpu.SemaphoreType.DMA((pairs,)),
    ]


LAG = 2


def forward_kernel(
    g,
    scale,
    factor,
    x_ref,
    wq_ref,
    wk_ref,
    wv_ref,
    bias_ref,
    places_ref,
    cols_ref,
    up_ref,
    down_ref,
    grad_ref,
    up_all,
    down_all,
    grad_out,
    qkv_out,
    ret_out,
    stats_ref,
    rhs,
    sent,
    routed,
    mixed,
    mask_sent,
    mask_routed,
    entropy,
    *sems,
):
    pairs = sent.shape[0]
    group = [group_device(g, (group_place(g) + k) % g.seq) for k in range(1, g.seq)]
    greet(line_peers(g) + group + [swap_partner(g)])
    plan = Gather(g, [up_ref, down_ref], [up_all, down_all], *sems[:3], False)
    swap = Swap(g, grad_ref, grad_out, *(sem.at[0] for sem in sems[3:5]))
    there = Exchange(g, sent, routed, *sems[5:8])
    back = Exchange(g, mixed, ret_out, *sems[8:11])
    masks = Exchange(g, mask_sent, mask_routed, *sems[11:14])
    save_sem = sems[14]
    units = len(plan.units)

    def keep(pair):
        return pltpu.make_async_copy(routed.at[pair], qkv_out.at[pair], save_sem.at[pair])

    mask_sent[...] = jnp.zeros_like(mask_sent)
    entropy[...] = jnp.zeros_like(entropy)

    def step(t, carry):
        for when in range(pairs + LAG):
            todo = [
                (unit, level)
                for level in (3, 2, 1, 0)
                for unit in range(units)
                if unit // 2 + level == when
            ]
            if todo or when == 1:

                @pl.when(t == when)
                def _(todo=todo, when=when):
                    for unit, level in todo:
                        plan.start(unit, level)
                    if when == 1:
                        swap.start()

        @pl.when(t < pairs)
        def _():
            project_pair(
                t,
                x_ref,
                (wq_ref, wk_ref, wv_ref),
                bias_ref,
                places_ref,
                cols_ref,
                sent,
                mask_sent.at[0],
                rhs,
            )
            there.start(t)

        @pl.when(t == pairs - 1)
        def _():
            masks.start(0)

        @pl.when(t >= LAG)
        def _():
            pair = t - LAG
            there.arrive(pair)
            keep(pair).start()
            attend_pair(pair, scale, routed, mixed, entropy)
            back.start(pair)

        return carry

    lax.fori_loop(0, pairs + LAG, step, 0)

    masks.arrive(0)
    sources, per_owner = mask_routed.shape[1:3]
    size = CLUSTER // sources
    spot = lax.broadcasted_iota(jnp.int32, stats_ref.shape, 1)
    row = lax.broadcasted_iota(jnp.int32, stats_ref.shape, 0)
    stats = jnp.zeros(stats_ref.shape, F32)
    for cluster in range(per_owner // size):
        mask = gather_rows(mask_routed, (0,), cluster * size, size, slice(None)).astype(F32)
        entropy_sum = jnp.sum(entropy[cluster] * mask) * factor
        count = jnp.sum(mask) * factor
        stats += jnp.where(
            spot == group_place(g) * (per_owner // size) + cluster,
            jnp.where(row == 0, entropy_sum, jnp.where(row == 1, count, 0.0)), 0.0
        )
    stats_ref[...] = stats
    plan.finish()
    swap.wait()

    def close(pair, carry):
        keep(pair).wait()
        back.arrive(pair)
        there.sent(pair)
        back.sent(pair)
        return carry

    lax.fori_loop(0, pairs, close, 0)
    masks.sent(0)


def forward(g, scale, factor, x, wq, wk, wv, bias, places, cols, up, down, grad):
    tok, width = x.shape
    pairs = width // PAIR
    per_owner = tok // g.seq
    clusters = tok // CLUSTER
    units, slots = Gather.slots(g, [up.shape, down.shape])
    shape = jax.ShapeDtypeStruct
    any_space, vmem = pl.BlockSpec(memory_space=pl.ANY), pl.BlockSpec(memory_space=pltpu.VMEM)
    dma = pltpu.SemaphoreType.DMA
    return pl.pallas_call(
        functools.partial(forward_kernel, g, scale, factor),
        out_shape=[
            shape((g.Y, 2, Z, g.X, *up.shape), BF16),
            shape((g.Y, 2, Z, g.X, *down.shape), BF16),
            shape(grad.shape, BF16),
            shape((pairs, g.seq, per_owner, 3 * PAIR), BF16),
            shape((pairs, g.seq, per_owner, PAIR), BF16),
            shape((8, PAIR), F32),
        ],
        in_specs=[vmem] * 7 + [any_space] * 3,
        out_specs=[any_space] * 5 + [vmem],
        scratch_shapes=[
            pltpu.VMEM((2 * tok, 4 * PAIR), BF16),
            pltpu.VMEM((pairs, tok, 3 * PAIR), BF16),
            pltpu.VMEM((pairs, g.seq, per_owner, 3 * PAIR), BF16),
            pltpu.VMEM((pairs, g.seq, per_owner, PAIR), BF16),
            pltpu.VMEM((1, tok, PAIR), BF16),
            pltpu.VMEM((1, g.seq, per_owner, PAIR), BF16),
            pltpu.VMEM((clusters, CLUSTER, PAIR), F32),
            dma((slots,)),
            dma((slots,)),
            dma((units,)),
            dma((1,)),
            dma((1,)),
            *exchange_sems(g, pairs),
            *exchange_sems(g, pairs),
            *exchange_sems(g, 1),
            dma((pairs,)),
        ],
        compiler_params=pltpu.CompilerParams(
            collective_id=2, has_side_effects=True, vmem_limit_bytes=VMEM_LIMIT
        ),
        name="forward",
    )(x, wq, wk, wv, bias, places, cols, up, down, grad)


def cluster_scores(q, k, scale):
    return dot_nt(q, k) * scale


def attend_back_pair(slot, pair, scale, qkv_ref, grad_ref, out_ref):
    _, sources, per_owner, _ = qkv_ref.shape
    size = CLUSTER // sources
    clusters = per_owner // size
    for cluster in range(clusters):
        q, k, v = (
            gather_rows(qkv_ref, (slot,), cluster * size, size, slice(i * PAIR, (i + 1) * PAIR))
            for i in range(3)
        )
        grad = gather_rows(grad_ref, (slot,), cluster * size, size, slice(None))
        q2, g2 = split_pair(q), split_pair(grad)
        scores = cluster_scores(q2, k, scale)
        top = jnp.max(scores, axis=1, keepdims=True)
        weights = jnp.exp(scores - top)
        probs = weights / jnp.sum(weights, axis=1, keepdims=True)
        low = probs.astype(BF16)
        d_value = dot_tn(low, g2)
        d_prob = dot_nt(g2, v)
        inner = jnp.sum(probs * d_prob, axis=1, keepdims=True)
        d_score = (probs * (d_prob - inner)).astype(BF16)
        d_query = (
            dot(jnp.concatenate([d_score[:CLUSTER], d_score[CLUSTER:]], axis=1), split_pair(k))
            * scale
        )
        d_key = dot_tn(d_score, q2) * scale
        for i, value in enumerate((d_query, d_key, d_value)):
            out_ref[
                pair, :, cluster * size : (cluster + 1) * size, i * PAIR : (i + 1) * PAIR
            ] = spread_rows(value, sources, BF16)


INV_SQRT2 = 0.7071067811865476
INV_SQRT_2PI = 0.3989422804014327


def norm_parts(value):
    centred = value - jnp.mean(value, axis=1, keepdims=True)
    rate = lax.rsqrt(jnp.mean(centred * centred, axis=1, keepdims=True) + EPSILON)
    return centred * rate, rate


def norm_back(grad, gain, normed, rate):
    inner = grad * gain
    return rate * (
        inner
        - jnp.mean(inner, axis=1, keepdims=True)
        - normed * jnp.mean(inner * normed, axis=1, keepdims=True)
    )


TILE = 256
COLS = 768


def middle_kernel(
    g,
    x_ref,
    att_ref,
    grad_ref,
    places_ref,
    cols_ref,
    wo_ref,
    up_ref,
    down_ref,
    vec_ref,
    up_bias_ref,
    out_ref,
    dmid_ref,
    datt_ref,
    g_out_ref,
    g_up_ref,
    g_down_ref,
    gvec_ref,
    g_upb_ref,
    attended,
    hidden_all,
    act_all,
    dup_all,
    dffn_all,
    datt_all,
    slope,
    ret,
    datt_sent,
    ex_send,
    ex_recv,
    ex_local,
):
    greet([group_device(g, (group_place(g) + k) % g.seq) for k in range(1, g.seq)])
    there = Exchange(g, datt_sent, datt_ref, ex_send, ex_recv, ex_local)
    tok, width = x_ref.shape
    wide = up_ref.shape[1]
    pairs = att_ref.shape[0]
    heads = 2 * pairs
    gvec_ref[...] = jnp.zeros_like(gvec_ref)
    g_upb_ref[...] = jnp.zeros_like(g_upb_ref)
    bo, g1, s1, bd, g2, s2 = (vec_ref[i : i + 1, :] for i in range(6))

    def column_sum(value):
        return jnp.sum(value, axis=0, keepdims=True)

    for pair in range(pairs):
        to = slice(pair * PAIR, (pair + 1) * PAIR)

        def spread(step, carry):
            rows = pl.ds(step * TILE, TILE)
            value = att_ref[pair, rows, :]
            low = head_lanes(value.shape)
            zero = jnp.zeros_like(value)
            ret[rows, :] = jnp.where(low, value, zero)
            ret[pl.ds(tok + step * TILE, TILE), :] = jnp.where(low, zero, value)
            return carry

        lax.fori_loop(0, tok // TILE, spread, 0)

        def unpermute(step, carry):
            start = step * TILE
            attended[pl.ds(start, TILE), to] = dot(
                token_rows(cols_ref, pair, start, TILE), ret[...]
            ).astype(BF16)
            return carry

        lax.fori_loop(0, tok // TILE, unpermute, 0)

    def tile(step, carry):
        rows = pl.ds(step * TILE, TILE)
        branch = dot(attended[rows, :], wo_ref[...]) + bo
        n1, r1 = norm_parts(x_ref[rows, :].astype(F32) + branch)
        hidden = (n1 * g1 + s1).astype(BF16)
        hidden_all[rows, :] = hidden
        ffn = jnp.zeros((TILE, width), F32)
        for col in range(0, wide, COLS):
            to = slice(col, col + COLS)
            pre = dot(hidden, up_ref[:, to]) + up_bias_ref[0:1, to]
            cdf = 0.5 * (1.0 + lax.erf(pre * INV_SQRT2))
            act = (pre * cdf).astype(BF16)
            slope[:, to] = cdf + pre * (jnp.exp(-0.5 * pre * pre) * INV_SQRT_2PI)
            act_all[rows, to] = act
            ffn += dot(act, down_ref[to, :])
        n2, r2 = norm_parts(hidden.astype(F32) + ffn + bd)
        out_ref[rows, :] = (n2 * g2 + s2).astype(BF16)
        mask = cols_ref[rows, heads : heads + 1].astype(F32)
        gout = grad_ref[rows, :].astype(F32) * mask
        gvec_ref[4:5, :] += column_sum(gout * n2)
        gvec_ref[5:6, :] += column_sum(gout)
        d_pre = norm_back(gout, g2, n2, r2)
        d_ffn = d_pre.astype(BF16)
        dffn_all[rows, :] = d_ffn
        gvec_ref[3:4, :] += column_sum(d_ffn.astype(F32))
        d_hidden = d_pre
        for col in range(0, wide, COLS):
            to = slice(col, col + COLS)
            d_up = (dot_nt(d_ffn, down_ref[to, :]) * slope[:, to]).astype(BF16)
            dup_all[rows, to] = d_up
            g_upb_ref[0:1, to] += column_sum(d_up.astype(F32))
            d_hidden += dot_nt(d_up, up_ref[:, to])
        gvec_ref[1:2, :] += column_sum(d_hidden * n1)
        gvec_ref[2:3, :] += column_sum(d_hidden)
        d_mid = norm_back(d_hidden, g1, n1, r1)
        d_branch = d_mid.astype(BF16)
        dmid_ref[rows, :] = d_branch
        gvec_ref[0:1, :] += column_sum(d_branch.astype(F32))
        datt_all[rows, :] = dot_nt(d_branch, wo_ref[...]).astype(BF16)
        return carry

    lax.fori_loop(0, tok // TILE, tile, 0)

    for pair in range(pairs):
        to = slice(pair * PAIR, (pair + 1) * PAIR)

        def spread(step, carry):
            rows = pl.ds(step * TILE, TILE)
            value = datt_all[rows, to]
            low = head_lanes(value.shape)
            zero = jnp.zeros_like(value)
            ret[rows, :] = jnp.where(low, value, zero)
            ret[pl.ds(tok + step * TILE, TILE), :] = jnp.where(low, zero, value)
            return carry

        lax.fori_loop(0, tok // TILE, spread, 0)

        def permute(step, carry):
            start = step * TILE
            datt_sent[pair, pl.ds(start, TILE), :] = dot(
                place_rows(places_ref, pair, start, TILE), ret[...]
            ).astype(BF16)
            return carry

        lax.fori_loop(0, tok // TILE, permute, 0)
        there.start(pair)

    def weights(step, carry):
        to = pl.ds(pl.multiple_of(step * TILE, TILE), TILE)
        g_down_ref[to, :] = dot_tn(act_all[:, to], dffn_all[...]).astype(BF16)
        g_up_ref[:, to] = dot_tn(hidden_all[...], dup_all[:, to]).astype(BF16)
        return carry

    lax.fori_loop(0, wide // TILE, weights, 0)

    def out_weights(step, carry):
        to = pl.ds(pl.multiple_of(step * TILE, TILE), TILE)
        g_out_ref[:, to] = dot_tn(attended[...], dmid_ref[:, to]).astype(BF16)
        return carry

    lax.fori_loop(0, width // TILE, out_weights, 0)
    for pair in range(pairs):
        there.arrive(pair)
        there.sent(pair)


def middle(g, *args):
    x, up = args[0], args[6]
    tok, width = x.shape
    wide = up.shape[1]
    pairs = width // PAIR
    shape = jax.ShapeDtypeStruct
    any_space, vmem = pl.BlockSpec(memory_space=pl.ANY), pl.BlockSpec(memory_space=pltpu.VMEM)
    return pl.pallas_call(
        functools.partial(middle_kernel, g),
        out_shape=[
            shape((tok, width), BF16),
            shape((tok, width), BF16),
            shape((pairs, g.seq, tok // g.seq, PAIR), BF16),
            shape((width, width), BF16),
            shape((width, wide), BF16),
            shape((wide, width), BF16),
            shape((8, width), F32),
            shape((8, wide), F32),
        ],
        in_specs=[vmem] * len(args),
        out_specs=[vmem, vmem, any_space] + [vmem] * 5,
        scratch_shapes=[
            pltpu.VMEM((tok, width), BF16),
            pltpu.VMEM((tok, width), BF16),
            pltpu.VMEM((tok, wide), BF16),
            pltpu.VMEM((tok, wide), BF16),
            pltpu.VMEM((tok, width), BF16),
            pltpu.VMEM((tok, width), BF16),
            pltpu.VMEM((TILE, wide), F32),
            pltpu.VMEM((2 * tok, PAIR), BF16),
            pltpu.VMEM((pairs, tok, PAIR), BF16),
            *exchange_sems(g, pairs),
        ],
        compiler_params=pltpu.CompilerParams(
            collective_id=3, has_side_effects=True, vmem_limit_bytes=VMEM_LIMIT
        ),
        name="middle",
    )(*args)


def backward_kernel(
    g,
    scale,
    n,
    x_ref,
    wq_ref,
    wk_ref,
    wv_ref,
    dmid_ref,
    cols_ref,
    *refs,
):
    terms, refs = refs[:n], refs[n:]
    qkv_ref, grad_ref, out_ref, gtok_ref, gq_ref, gk_ref, gv_ref, gvec_ref = refs[:8]
    sums, refs = refs[8 : 8 + n], refs[8 + n :]
    out_home, qkv_slots, grad_slots, sent, home, rhs, local, flat, total = refs[:9]
    bufs, refs = refs[9 : 9 + 4 * n], refs[9 + 4 * n :]
    rs_send, rs_recv, ex_send, ex_recv, ex_local, load_sem, swap_send, swap_recv = refs
    pairs = sent.shape[0]
    tok, width = x_ref.shape
    group = [group_device(g, (group_place(g) + k) % g.seq) for k in range(1, g.seq)]
    greet(line_peers(g) + group + [swap_partner(g)])
    plan = Scatter(g, terms, sums, bufs, rs_send, rs_recv, False)
    swap = Swap(g, out_ref, out_home, swap_send.at[0], swap_recv.at[0])
    there = Exchange(g, sent, home, ex_send, ex_recv, ex_local)
    units = len(plan.units)

    def loads(pair):
        slot = pair % 2
        return (
            pltpu.make_async_copy(qkv_ref.at[pair], qkv_slots.at[slot], load_sem.at[0, slot]),
            pltpu.make_async_copy(grad_ref.at[pair], grad_slots.at[slot], load_sem.at[1, slot]),
        )

    for copy in loads(0):
        copy.start()
    gvec_ref[...] = jnp.zeros_like(gvec_ref)
    total[...] = dmid_ref[...].astype(F32)

    def step(t, carry):
        @pl.when(t < pairs)
        def _():
            for copy in loads(t):
                copy.wait()

            @pl.when(t + 1 < pairs)
            def _():
                for copy in loads(t + 1):
                    copy.start()

            attend_back_pair(t % 2, t, scale, qkv_slots, grad_slots, sent)
            there.start(t)

        for when in range(pairs + LAG):
            todo = [
                (unit, level)
                for level in (4, 3, 2, 1, 0)
                for unit in range(units)
                if unit // 2 + level == when
            ]
            if todo or when == 1:

                @pl.when(t == when)
                def _(todo=todo, when=when):
                    for unit, level in todo:
                        plan.step(unit, level)
                    if when == 1:
                        swap.start()

        @pl.when(t >= LAG)
        def _():
            pair = t - LAG
            head = pl.ds(pl.multiple_of(pair * PAIR, PAIR), PAIR)
            there.arrive(pair)
            per = tok // g.seq

            def spread(owner, carry):
                for part in range(3):
                    to = slice(part * PAIR, (part + 1) * PAIR)
                    value = home[pair, owner, :, to]
                    low = head_lanes(value.shape)
                    zero = jnp.zeros_like(value)
                    at = pl.multiple_of(owner * per, per)
                    rhs[pl.ds(at, per), to] = jnp.where(low, value, zero)
                    rhs[pl.ds(tok + at, per), to] = jnp.where(low, zero, value)
                return carry

            lax.fori_loop(0, g.seq, spread, 0)
            for part, w_ref in enumerate((wq_ref, wk_ref, wv_ref)):
                flat[:, part * PAIR : (part + 1) * PAIR] = w_ref[:, head]

            def unpermute(k, carry):
                start = k * TILE
                rows = pl.ds(start, TILE)
                value = dot(token_rows(cols_ref, pair, start, TILE), rhs[...])
                for part in range(3):
                    piece = value[:, part * PAIR : (part + 1) * PAIR]
                    gvec_ref[part : part + 1, head] += jnp.sum(piece, axis=0, keepdims=True)
                value = value.astype(BF16)
                local[rows, :] = value
                total[rows, :] += dot_nt(value, flat[...])
                return carry

            lax.fori_loop(0, tok // TILE, unpermute, 0)

            def weights(k, carry):
                rows = pl.ds(pl.multiple_of(k * TILE, TILE), TILE)
                value = dot_tn(x_ref[:, rows], local[...]).astype(BF16)
                for part, g_ref in enumerate((gq_ref, gk_ref, gv_ref)):
                    g_ref[rows, head] = value[:, part * PAIR : (part + 1) * PAIR]
                return carry

            lax.fori_loop(0, width // TILE, weights, 0)

        return carry

    lax.fori_loop(0, pairs + LAG, step, 0)
    gtok_ref[...] = total[...].astype(BF16)
    for when in range(pairs + LAG, units // 2 + 6):
        for level in (4, 3, 2, 1, 0):
            for unit in range(units):
                if unit // 2 + level == when:
                    plan.step(unit, level)
    swap.wait()
    plan.sent()

    def close(pair, carry):
        there.sent(pair)
        return carry

    lax.fori_loop(0, pairs, close, 0)


def backward(g, scale, x, wq, wk, wv, d_mid, cols, terms, qkv, grad, out):
    tok, width = x.shape
    pairs = width // PAIR
    n = len(terms)
    shape = jax.ShapeDtypeStruct
    any_space, vmem = pl.BlockSpec(memory_space=pl.ANY), pl.BlockSpec(memory_space=pltpu.VMEM)
    dma = pltpu.SemaphoreType.DMA
    made = pl.pallas_call(
        functools.partial(backward_kernel, g, scale, n),
        out_shape=[
            shape((tok, width), BF16),
            *([shape((width, width), BF16)] * 3),
            shape((8, width), F32),
            *(shape(item.shape[4:], F32) for item in terms),
            shape(out.shape, BF16),
        ],
        in_specs=[vmem] * (6 + n) + [any_space] * 3,
        out_specs=[vmem] * (5 + n) + [any_space],
        scratch_shapes=[
            pltpu.VMEM((2, *qkv.shape[1:]), BF16),
            pltpu.VMEM((2, *grad.shape[1:]), BF16),
            pltpu.VMEM(qkv.shape, BF16),
            pltpu.VMEM(qkv.shape, BF16),
            pltpu.VMEM((2 * tok, 3 * PAIR), BF16),
            pltpu.VMEM((tok, 3 * PAIR), BF16),
            pltpu.VMEM((width, 3 * PAIR), BF16),
            pltpu.VMEM((tok, width), F32),
            *Scatter.scratch(g, [item.shape for item in terms], False),
            *exchange_sems(g, pairs),
            dma((2, 2)),
            dma((1,)),
            dma((1,)),
        ],
        compiler_params=pltpu.CompilerParams(
            collective_id=5, has_side_effects=True, vmem_limit_bytes=VMEM_LIMIT
        ),
        name="backward",
    )(x, wq, wk, wv, d_mid, cols, *terms, qkv, grad, out)
    return made[0], made[1:4], made[4], made[5 : 5 + n], made[-1]


def close_kernel(g, n, small_ref, *refs):
    terms, gtok_ref, refs = refs[:n], refs[n], refs[n + 1 :]
    small_out, sums, gtok_home, refs = refs[0], refs[1 : 1 + n], refs[1 + n], refs[2 + n :]
    bufs, refs = refs[: 4 * n], refs[4 * n :]
    rs_send, rs_recv, small_bufs, refs = refs[0], refs[1], refs[2:6], refs[6:]
    small_send, small_recv, swap_send, swap_recv = refs
    greet(line_peers(g) + [swap_partner(g)])
    plan = Scatter(g, terms, sums, bufs, rs_send, rs_recv, True)
    swap = Swap(g, gtok_ref, gtok_home, swap_send.at[0], swap_recv.at[0])
    small = Total(g, small_ref, small_bufs, small_send, small_recv)
    units = len(plan.units)
    for unit in range(units):
        plan.step(unit, 0)
    small.start(0, small_ref[...])
    swap.start()
    for level in range(1, 5):
        for unit in range(units):
            plan.step(unit, level)
        value = small.take(level - 1)
        if level < 4:
            small.start(level, value)
        else:
            small_out[...] = value
    swap.wait()
    plan.sent()
    small.sent()


def close_call(g, small, terms, gtok):
    n = len(terms)
    shape = jax.ShapeDtypeStruct
    any_space, vmem = pl.BlockSpec(memory_space=pl.ANY), pl.BlockSpec(memory_space=pltpu.VMEM)
    dma = pltpu.SemaphoreType.DMA
    made = pl.pallas_call(
        functools.partial(close_kernel, g, n),
        out_shape=[
            shape(small.shape, F32),
            *(shape(item.shape[4:], F32) for item in terms),
            shape(gtok.shape, BF16),
        ],
        in_specs=[vmem] * (1 + n) + [any_space],
        out_specs=[vmem] * (1 + n) + [any_space],
        scratch_shapes=[
            *Scatter.scratch(g, [item.shape for item in terms], True),
            *Total.scratch(g, small.shape),
            dma((1,)),
            dma((1,)),
        ],
        compiler_params=pltpu.CompilerParams(
            collective_id=6, has_side_effects=True, vmem_limit_bytes=VMEM_LIMIT
        ),
        name="close",
    )(small, *terms, gtok)
    return made[0], made[1:-1], made[-1]


def body(
    g,
    tokens,
    cluster_slot,
    loss_mask,
    out_grad,
    query_weight,
    key_weight,
    value_weight,
    output_weight,
    query_bias,
    value_bias,
    output_bias,
    first_gain,
    first_shift,
    up_weight,
    up_bias,
    down_weight,
    down_bias,
    second_gain,
    second_shift,
):
    tok, width = tokens.shape[1:]
    heads = cluster_slot.shape[1]
    pairs = heads // 2
    wide = up_weight.shape[1]
    per_owner = tok // g.seq
    scale = (width // heads) ** -0.5

    slots = cluster_slot[0]
    places = slots // tok * per_owner + slots % tok // g.seq
    table = jnp.concatenate(
        [places, loss_mask, jnp.zeros((16 - heads - 1, tok), jnp.int32)], axis=0
    )
    vectors = (
        query_bias,
        value_bias,
        output_bias,
        first_gain,
        first_shift,
        down_bias,
        second_gain,
        second_shift,
    )
    count = query_bias.shape[0]
    packed = jnp.concatenate([*vectors, up_bias])
    room = -packed.shape[0] % PAIR
    packed = jnp.pad(packed, (0, room)).reshape(-1, PAIR)
    weights = (query_weight, key_weight, value_weight, output_weight)
    gathered, x, table = open_call(g, [packed, *weights], tokens[0], table)
    cols = table.T
    wq, wk, wv, wo = (item.reshape(g.n * item.shape[4], item.shape[5]) for item in gathered[1:])
    flat = gathered[0].reshape(g.n, -1).astype(F32)
    rows = flat[:, : 8 * count].reshape(g.n, 8, count).transpose(1, 0, 2).reshape(8, width)
    up_row = flat[:, 8 * count : 8 * count + up_bias.shape[0]].reshape(1, wide)
    qkv_bias = jnp.stack([rows[0], jnp.zeros((width,), F32), rows[1]])

    up, down, grad, qkv, returned, stats = forward(
        g,
        scale,
        1.0 / (heads * CLUSTER * g.batch),
        x,
        wq,
        wk,
        wv,
        qkv_bias,
        table,
        cols,
        up_weight,
        down_weight,
        out_grad[0],
    )
    up, down = (item.reshape(g.n * item.shape[4], item.shape[5]) for item in (up, down))

    out, d_mid, routed, g_out, g_up, g_down, g_rows, g_upb = middle(
        g,
        x,
        returned.reshape(pairs, tok, PAIR),
        grad,
        table,
        cols,
        wo,
        up,
        down,
        rows[2:],
        up_row,
    )

    def parts(item):
        rows, cols = item.shape[0] // g.n, item.shape[1]
        if rows % 8:
            rows, cols = rows * cols // PAIR, PAIR
        return item.reshape(g.Y, 2, Z, g.X, rows, cols)

    grad_tokens, g_attn, g_bias, s_ffn, out = backward(
        g, scale, x, wq, wk, wv, d_mid, cols, [parts(g_up), parts(g_down), parts(g_out)], qkv, routed, out
    )
    lines = wide // width
    small = jnp.concatenate(
        [
            g_bias[0:1],
            g_bias[2:3],
            g_rows[:6],
            g_upb[0].reshape(lines, width),
            jnp.pad(stats[:2], ((0, 0), (0, width - stats.shape[1]))),
            jnp.zeros((6 - lines, width), F32),
        ],
        axis=0,
    )
    small, s_attn, grad_tokens = close_call(g, small, [parts(item) for item in g_attn], grad_tokens)

    b, s = lax.axis_index("batch"), lax.axis_index("seq")
    here = b * g.seq + s
    mine = lax.dynamic_slice(small, (0, here * count), (8, count))
    wide_count = wide // g.n
    gu = lax.dynamic_slice(small[8 : 8 + lines].reshape(wide), (here * wide_count,), (wide_count,))
    blocks = tok // CLUSTER
    cluster_stats = lax.dynamic_slice(small, (8 + lines, s * blocks), (2, blocks))
    s_up, s_down, s_out, s_query, s_key, s_value = (
        item.reshape(local.shape)
        for item, local in zip(
            (*s_ffn, *s_attn),
            (up_weight, down_weight, output_weight, query_weight, key_weight, value_weight),
        )
    )
    gq, gv, go, gg1, gs1, gd, gg2, gs2 = (mine[i] for i in range(8))
    return (
        out[None],
        grad_tokens[None],
        s_query,
        s_key,
        s_value,
        s_out,
        gq,
        gv,
        go,
        gg1,
        gs1,
        s_up,
        gu,
        s_down,
        gd,
        gg2,
        gs2,
        cluster_stats,
    )


def solution(mesh):
    g = Grid(mesh)
    tokens, rows, flat = P("batch", "seq", None), P(("batch", "seq"), None), P(("batch", "seq"))
    return jax.shard_map(
        functools.partial(body, g),
        mesh=mesh,
        in_specs=(
            tokens,
            P("batch", None, "seq"),
            P("batch", "seq"),
            tokens,
            *([rows] * 4),
            *([flat] * 5),
            rows,
            flat,
            rows,
            *([flat] * 3),
        ),
        out_specs=(
            tokens,
            tokens,
            *([rows] * 4),
            *([flat] * 5),
            rows,
            flat,
            rows,
            *([flat] * 3),
            P(None, "seq"),
        ),
        check_vma=False,
    )
```

```python
import functools

import jax
import jax.numpy as jnp
from jax import lax
from jax.experimental import pallas as pl
from jax.experimental.pallas import tpu as pltpu
from jax.sharding import PartitionSpec as P

MESH = pl.DeviceIdType.MESH
F32 = jnp.float32
BF16 = jnp.bfloat16
EPSILON = 1e-12
CLUSTER = 128
PAIR = 128
Z = 4
VMEM_LIMIT = 58 * 1024 * 1024


class Grid:
    def __init__(self, mesh):
        self.batch, self.seq = mesh.shape["batch"], mesh.shape["seq"]
        self.Y, self.X = self.batch // 2, self.seq // Z
        self.half = self.seq // 2
        self.n = self.batch * self.seq


AXES = ("y", "c", "h", "l", "x")


def sizes(g):
    return {"y": g.Y, "c": 2, "h": 2, "l": Z // 2, "x": g.X}


def coords(g):
    b, s = lax.axis_index("batch"), lax.axis_index("seq")
    z = s // g.X
    return {"y": b // 2, "c": b % 2, "h": z // (Z // 2), "l": z % (Z // 2), "x": s % g.X}


def device(g, at):
    return (at["y"] * 2 + at["c"], (at["h"] * (Z // 2) + at["l"]) * g.X + at["x"])


def along(g, at, axis):
    size = sizes(g)[axis]
    places = [(at[axis] + k) % size for k in range(1, size)]
    return [(place, device(g, {**at, axis: place})) for place in places]


def group_place(g):
    b, s = lax.axis_index("batch"), lax.axis_index("seq")
    return b % 2 * g.half + s % g.half


def group_device(g, place):
    b, s = lax.axis_index("batch"), lax.axis_index("seq")
    return (b // 2 * 2 + place // g.half, s // g.half * g.half + place % g.half)


def line_peers(g, axes=AXES):
    at = coords(g)
    return [peer for axis in axes for _, peer in along(g, at, axis)]


def greet(peers):
    barrier = pltpu.get_barrier_semaphore()
    for peer in peers:
        pl.semaphore_signal(barrier, inc=1, device_id=peer, device_id_type=MESH)
    pl.semaphore_wait(barrier, len(peers))


def remote(src, dst, send, recv, peer):
    return pltpu.make_async_remote_copy(
        src_ref=src,
        dst_ref=dst,
        send_sem=send,
        recv_sem=recv,
        device_id=peer,
        device_id_type=MESH,
    )


def lane_pieces(shape):
    rows, cols = shape
    if cols % PAIR or rows * cols <= 24 * 768:
        return [(0, cols)]
    count = {3072: 4, 768: 3}.get(cols, 1)
    return [(k * (cols // count), cols // count) for k in range(count)]


class Gather:
    def __init__(self, g, ins, outs, dims, done, plan, sends, recvs, local_sem):
        self.g, self.ins, self.outs, self.dims, self.done = g, ins, outs, dims, done
        self.plan = plan
        self.sends, self.recvs, self.local_sem = sends, recvs, local_sem
        self.at = coords(g)
        self.units = [
            (index, pl.ds(start, size))
            for index, item in enumerate(ins)
            for start, size in lane_pieces(item.shape[-2:])
        ]

    @staticmethod
    def sems(g, shapes):
        units = sum(len(lane_pieces(shape[-2:])) for shape in shapes)
        slots = units * sum(sizes(g).values())
        dma = pltpu.SemaphoreType.DMA
        return [dma((slots,)), dma((slots,)), dma((units,))]

    def source(self, unit):
        index, cols = self.units[unit]
        return self.ins[index].at[(*([slice(None)] * (len(self.ins[index].shape) - 1)), cols)]

    def view(self, unit, done):
        index, cols = self.units[unit]
        spot = tuple(slice(None) if axis in done else self.at[axis] for axis in self.dims)
        return self.outs[index].at[(*spot, slice(None), cols)]

    def own(self, unit):
        return pltpu.make_async_copy(
            self.source(unit), self.view(unit, self.done), self.local_sem.at[unit]
        )

    def levels(self, unit):
        return self.plan(unit)

    def moves(self, unit, level):
        g = self.g
        axes = self.levels(unit)
        view = self.view(unit, (*self.done, *axes[:level]))
        src = self.source(unit) if level == 0 else view
        size = sizes(g)
        base = unit * sum(size.values())
        for axis in AXES[: AXES.index(axes[level])]:
            base += size[axis]
        return [
            remote(src, view, self.sends.at[base + k], self.recvs.at[base + k], peer)
            for k, (_, peer) in enumerate(along(g, self.at, axes[level]))
        ]

    def start(self, unit, level):
        if level == 0:
            self.own(unit).start()
        else:
            if level == 1:
                self.own(unit).wait()
            for copy in self.moves(unit, level - 1):
                copy.wait_recv()
        for copy in self.moves(unit, level):
            copy.start()

    def finish(self):
        count = len(self.units)
        for unit in range(count):
            for copy in self.moves(unit, len(self.levels(unit)) - 1):
                copy.wait_recv()
        for unit in range(count):
            for level in range(len(self.levels(unit))):
                for copy in self.moves(unit, level):
                    copy.wait_send()


class Swap:
    def __init__(self, g, src, dst, sends, recvs, pieces=1):
        b, s = lax.axis_index("batch"), lax.axis_index("seq")
        self.native = b % 2 == s // g.half
        self.peer = swap_partner(g)
        self.ends = (src, dst, sends, recvs)
        self.pieces = pieces

    @staticmethod
    def sems(pieces=1):
        return [pltpu.SemaphoreType.DMA((pieces,)), pltpu.SemaphoreType.DMA((pieces,))]

    def piece(self, k):
        src, dst, sends, recvs = self.ends
        size = src.shape[0] // self.pieces
        rows = pl.ds(pl.multiple_of(k * size, size), size)
        return src.at[rows], dst.at[rows], sends.at[k], recvs.at[k]

    def start(self, k=0):
        src, dst, send, recv = self.piece(k)

        @pl.when(self.native)
        def _():
            pltpu.make_async_copy(src, dst, recv).start()

        @pl.when(jnp.logical_not(self.native))
        def _():
            remote(src, dst, send, recv, self.peer).start()

    def wait(self):
        for k in range(self.pieces):
            self.wait_piece(k)

    def wait_piece(self, k):
        src, dst, send, recv = self.piece(k)

        @pl.when(self.native)
        def _():
            pltpu.make_async_copy(src, dst, recv).wait()

        @pl.when(jnp.logical_not(self.native))
        def _():
            remote(src, dst, send, recv, self.peer).wait()


def swap_partner(g):
    b, s = lax.axis_index("batch"), lax.axis_index("seq")
    return (b // 2 * 2 + 1 - b % 2, (s + g.half) % g.seq)


PART = ("h", "l", "x")
PIECES, WINDOW = 16, 2


MASK_AT = 4


def masks_in_order(heads, table_ref, block, size, out_ref):
    tok = table_ref.shape[1]
    start = block * size
    rows = lax.broadcasted_iota(jnp.int32, (size, tok), 0) + start
    lanes = lax.broadcasted_iota(jnp.int32, (size, PAIR), 1)
    mask = table_ref[heads : heads + 1, :] > 0
    made = jnp.zeros((size, PAIR), F32)
    for head in range(heads):
        places = jnp.where(mask, table_ref[head : head + 1, :], -1)
        found = jnp.sum(jnp.where(rows == places, 1.0, 0.0), axis=1, keepdims=True)
        made = jnp.where(lanes == head, found, made)
    out_ref[start : start + size, :] = made.astype(BF16)


def open_kernel(g, n, m, *refs):
    ins, refs = refs[: n + m], refs[n + m :]
    swap_in, refs = refs[:2], refs[2:]
    outs, refs = refs[: n + m], refs[n + m :]
    swap_out, mask_ref, sems = refs[:2], refs[2], refs[3:]
    greet(line_peers(g) + [swap_partner(g)])
    whole = Gather(
        g,
        ins[:n],
        outs[:n],
        AXES,
        (),
        lambda unit: ("h", "l", "x", "y", "c"),
        *sems[:3],
    )
    part = Gather(g, ins[n:], outs[n:], PART, (), lambda unit: PART, *sems[3:6])
    tokens = Swap(g, swap_in[0], swap_out[0], *sems[6:8], PIECES)
    table = Swap(g, swap_in[1], swap_out[1], *sems[8:10])
    plans = [(whole, unit) for unit in range(len(whole.units))]
    plans += [(part, unit) for unit in range(len(part.units))]
    table.start()
    tok, width = swap_in[0].shape
    heads, blocks = width * 2 // PAIR, 8
    for t in range(len(plans) + 4 * WINDOW):
        for level in range(5):
            k = t - level * WINDOW
            if 0 <= k < len(plans):
                plan, unit = plans[k]
                if level < len(plan.levels(unit)):
                    plan.start(unit, level)
        if t < PIECES:
            tokens.start(t)
        if t == MASK_AT:
            table.wait()
        if 0 <= t - MASK_AT < blocks:
            masks_in_order(heads, swap_out[1], t - MASK_AT, tok // blocks, mask_ref)
    whole.finish()
    part.finish()
    tokens.wait()


def open_call(g, whole, part, swapped):
    any_space = pl.BlockSpec(memory_space=pl.ANY)
    shape = jax.ShapeDtypeStruct
    size = sizes(g)
    n, m = len(whole), len(part)
    outs = [
        *(shape((*(size[axis] for axis in AXES), *item.shape), item.dtype) for item in whole),
        *(shape((*(size[axis] for axis in PART), *item.shape), item.dtype) for item in part),
        *(shape(item.shape, item.dtype) for item in swapped),
    ]
    vmem = pl.BlockSpec(memory_space=pltpu.VMEM)
    made = pl.pallas_call(
        functools.partial(open_kernel, g, n, m),
        out_shape=[*outs, shape((swapped[0].shape[0], PAIR), BF16)],
        in_specs=[any_space] * len(outs),
        out_specs=[any_space] * (len(outs) - 1) + [vmem] * 2,
        scratch_shapes=[
            *Gather.sems(g, [item.shape for item in whole]),
            *Gather.sems(g, [item.shape for item in part]),
            *Swap.sems(PIECES),
            *Swap.sems(),
        ],
        compiler_params=pltpu.CompilerParams(
            collective_id=0, has_side_effects=True, vmem_limit_bytes=VMEM_LIMIT
        ),
        name="open",
    )(*whole, *part, *swapped)
    return made[:n], made[n : n + m], made[n + m :]


class Scatter:
    def __init__(self, g, ins, bufs, plans, sends, recvs):
        self.g, self.ins, self.bufs, self.plans = g, ins, bufs, plans
        self.sends, self.recvs = sends, recvs
        self.at = coords(g)
        self.units = [
            (index, pl.ds(start, size))
            for index, item in enumerate(ins)
            for start, size in lane_pieces(item.shape[-2:])
        ]

    @staticmethod
    def scratch(g, shapes, plans):
        size = sizes(g)
        made = []
        for shape, plan in zip(shapes, plans):
            left = list(AXES)
            for axis in plan:
                left.remove(axis)
                lead = (size[axis] - 1, *(size[other] for other in left))
                made.append(pltpu.VMEM((*lead, *shape[-2:]), BF16))
        units = sum(len(lane_pieces(shape[-2:])) for shape in shapes)
        slots = units * sum(size.values())
        return [*made, pltpu.SemaphoreType.DMA((slots,)), pltpu.SemaphoreType.DMA((slots,))]

    def held(self, index, level):
        return self.bufs[index * len(AXES) + level]

    def store(self, index, level):
        if level == 0:
            return self.ins[index], AXES
        left = tuple(axis for axis in AXES if axis not in self.plans[index][:level])
        return self.held(index, level - 1).at[0], left

    def moves(self, unit, level):
        g = self.g
        index, cols = self.units[unit]
        axis = self.plans[index][level]
        src, left = self.store(index, level)
        held = self.held(index, level)
        size = sizes(g)
        base = unit * sum(size.values())
        for other in AXES[: AXES.index(axis)]:
            base += size[other]
        a = slice(None)
        rest = (a,) * len(left)
        made = []
        for k, (place, peer) in enumerate(along(g, self.at, axis)):
            spot = tuple(place if other == axis else a for other in left)
            made.append(
                remote(
                    src.at[(*spot, a, cols)],
                    held.at[(k, *rest, cols)],
                    self.sends.at[base + k],
                    self.recvs.at[base + k],
                    peer,
                )
            )
        return made

    def add(self, unit, level, out=None):
        g = self.g
        index, cols = self.units[unit]
        axis = self.plans[index][level]
        src, left = self.store(index, level)
        held = self.held(index, level)
        size = sizes(g)
        rest = [other for other in left if other != axis]
        loop = [other for other in rest if other in ("h", "l")]
        count = 1
        for other in loop:
            count *= size[other]
        static = [other for other in rest if other not in loop]
        a = slice(None)

        def some(step, carry):
            spots = [{}]
            for other in static:
                spots = [{**spot, other: k} for spot in spots for k in range(size[other])]
            for spot in spots:
                if len(loop) == 2:
                    spot = {**spot, "h": step // size["l"], "l": step % size["l"]}
                elif loop:
                    spot = {**spot, loop[0]: step}
                where = tuple(spot[other] for other in rest)
                mine = tuple(self.at[axis] if other == axis else spot[other] for other in left)
                total = src[(*mine, a, cols)].astype(F32)
                for k in range(size[axis] - 1):
                    total += held[(k, *where, a, cols)].astype(F32)
                if out is None:
                    held[(0, *where, a, cols)] = total.astype(BF16)
                else:
                    out[(*where, a, cols)] = total.astype(out.dtype)
            return carry

        lax.fori_loop(0, count, some, 0)

    def step(self, unit, level, out=None):
        if level:
            for copy in self.moves(unit, level - 1):
                copy.wait_recv()
            last = level == len(AXES)
            self.add(unit, level - 1, out[self.units[unit][0]] if last else None)
        if level < len(AXES):
            for copy in self.moves(unit, level):
                copy.start()

    def sent(self):
        for unit in range(len(self.units)):
            for level in range(len(AXES)):
                for copy in self.moves(unit, level):
                    copy.wait_send()


class Total:
    def __init__(self, g, held, bufs, sends, recvs):
        self.g, self.held, self.bufs = g, held, bufs
        self.sends, self.recvs = sends, recvs
        self.at = coords(g)

    @staticmethod
    def scratch(g, shape):
        slots = sum(sizes(g).values())
        return [
            *(pltpu.VMEM((sizes(g)[axis], *shape), F32) for axis in AXES),
            pltpu.SemaphoreType.DMA((slots,)),
            pltpu.SemaphoreType.DMA((slots,)),
        ]

    def moves(self, level):
        g = self.g
        axis = AXES[level]
        view = self.bufs[level].at[self.at[axis]]
        base = sum(sizes(g)[other] for other in AXES[:level])
        return [
            remote(view, view, self.sends.at[base + k], self.recvs.at[base + k], peer)
            for k, (_, peer) in enumerate(along(g, self.at, axis))
        ]

    def start(self, level, value):
        self.bufs[level][self.at[AXES[level]]] = value
        for copy in self.moves(level):
            copy.start()

    def take(self, level):
        for copy in self.moves(level):
            copy.wait_recv()
        buf = self.bufs[level]
        total = buf[0]
        for k in range(1, buf.shape[0]):
            total = total + buf[k]
        return total

    def sent(self):
        for level in range(len(AXES)):
            for copy in self.moves(level):
                copy.wait_send()


def dot(left, right):
    return lax.dot_general(left, right, (((1,), (0,)), ((), ())), preferred_element_type=F32)


def dot_nt(left, right):
    return lax.dot_general(left, right, (((1,), (1,)), ((), ())), preferred_element_type=F32)


def dot_tn(left, right):
    return lax.dot_general(left, right, (((0,), (0,)), ((), ())), preferred_element_type=F32)


def head_lanes(shape):
    return lax.broadcasted_iota(jnp.int32, shape, 1) < PAIR // 2


def split_pair(value, axis=0):
    low = head_lanes(value.shape)
    zero = jnp.zeros_like(value)
    return jnp.concatenate(
        [jnp.where(low, value, zero), jnp.where(low, zero, value)], axis=axis
    )


def swap_halves(value):
    return pltpu.roll(value.astype(F32), PAIR // 2, 1).astype(value.dtype)


def pack(q, k, v):
    low = head_lanes(q.shape)
    k = swap_halves(k)
    return jnp.where(low, q, k), jnp.where(low, v, q), jnp.where(low, k, v)


def unpack(first, second, third):
    low = head_lanes(first.shape)
    return (
        jnp.where(low, first, second),
        swap_halves(jnp.where(low, third, first)),
        jnp.where(low, second, third),
    )


def place_rows(places_ref, head, start, size):
    tok = places_ref.shape[1]
    rows = lax.broadcasted_iota(jnp.int32, (size, tok), 0) + start
    return (rows == places_ref[pl.ds(head, 1), :]).astype(F32).astype(BF16)


def token_rows(cols_ref, head, start, size):
    tok, width = cols_ref.shape
    lanes = lax.broadcasted_iota(jnp.int32, (size, tok), 1)
    heads = lax.broadcasted_iota(jnp.int32, (size, width), 1)
    table = cols_ref[pl.ds(start, size), :].astype(F32)
    place = jnp.sum(jnp.where(heads == head, table, 0.0), axis=1, keepdims=True)
    return (lanes == place.astype(jnp.int32)).astype(F32).astype(BF16)


def move_rows(pick, value_ref):
    one = dot(pick(0), value_ref[:, : 2 * PAIR])
    two = dot(pick(1), value_ref[:, PAIR:])
    low = head_lanes((one.shape[0], PAIR))
    return one[:, :PAIR], jnp.where(low, one[:, PAIR:], two[:, :PAIR]), two[:, PAIR:]


def move_pair(pick, value):
    one, two = dot(pick(0), value), dot(pick(1), value)
    return jnp.where(head_lanes(one.shape), one, two)


def gather_rows(block_ref, lead, start, size, lanes):
    part = block_ref[(*lead, slice(None), pl.ds(start, size), lanes)]
    if size % 16:
        part = part.astype(F32)
    return part.reshape(part.shape[0] * size, part.shape[2]).astype(block_ref.dtype)


def spread_rows(value, sources, kind):
    size = value.shape[0] // sources
    if size % 16:
        return value.astype(F32).reshape(sources, size, value.shape[1]).astype(kind)
    return value.astype(kind).reshape(sources, size, value.shape[1])


ROWS = 512


def pair_weights(pair, w_refs, out_ref):
    head = pl.ds(pl.multiple_of(pair * PAIR, PAIR), PAIR)
    for part, value in enumerate(pack(*(w_ref[:, head] for w_ref in w_refs))):
        out_ref[:, part * PAIR : (part + 1) * PAIR] = value


def project_pair(pair, x_ref, w_refs, bias_ref, places_ref, flat, rhs, out_ref):
    tok = x_ref.shape[0]
    head = pl.ds(pl.multiple_of(pair * PAIR, PAIR), PAIR)
    pair_weights(pair, w_refs, flat)
    bias = jnp.concatenate(
        pack(*(jnp.broadcast_to(bias_ref[i : i + 1, head], (8, PAIR)) for i in range(3))), axis=1
    )[0:1]

    def project(step, carry):
        rows = pl.ds(step * ROWS, ROWS)
        rhs[rows, :] = (dot(x_ref[rows, :], flat[...]) + bias).astype(BF16)
        return carry

    lax.fori_loop(0, tok // ROWS, project, 0)

    def permute(step, carry):
        start = step * ROWS
        made = move_rows(lambda i: place_rows(places_ref, 2 * pair + i, start, ROWS), rhs)
        for part, value in enumerate(made):
            out_ref[pair, pl.ds(start, ROWS), part * PAIR : (part + 1) * PAIR] = value.astype(BF16)
        return carry

    lax.fori_loop(0, tok // ROWS, permute, 0)


def attend_pair(pair, scale, qkv_ref, out_ref, entropy_ref):
    _, sources, per_owner, _ = qkv_ref.shape
    size = CLUSTER // sources
    clusters = per_owner // size
    lanes = lax.broadcasted_iota(jnp.int32, (CLUSTER, PAIR), 1)
    for cluster in range(clusters):
        q, k, v = unpack(
            *(
                gather_rows(qkv_ref, (pair,), cluster * size, size, slice(i * PAIR, (i + 1) * PAIR))
                for i in range(3)
            )
        )
        scores = cluster_scores(split_pair(q), k, scale)
        top = jnp.max(scores, axis=1, keepdims=True)
        weights = jnp.exp(scores - top)
        totals = jnp.sum(weights, axis=1, keepdims=True)
        probs = weights / totals
        entropy = top + jnp.log(totals) - jnp.sum(probs * scores, axis=1, keepdims=True)
        low = probs.astype(BF16)
        mixed = dot(
            jnp.concatenate([low[:CLUSTER], low[CLUSTER:]], axis=1), split_pair(v)
        )
        out_ref[pair, :, cluster * size : (cluster + 1) * size, :] = spread_rows(
            mixed, sources, BF16
        )
        entropy_ref[cluster] = jnp.where(
            lanes == 2 * pair,
            entropy[:CLUSTER],
            jnp.where(lanes == 2 * pair + 1, entropy[CLUSTER:], entropy_ref[cluster]),
        )


class Exchange:
    def __init__(self, g, kind, src, dst, sends, recvs, local_sem):
        self.g, self.kind, self.src, self.dst = g, kind, src, dst
        self.sends, self.recvs, self.local_sem = sends, recvs, local_sem
        b, s = lax.axis_index("batch"), lax.axis_index("seq")
        self.b, self.s = b, s
        self.me = s if kind == "work" else group_place(g)
        self.native = b % 2 == s // g.half

    def target(self, place):
        g, b, s = self.g, self.b, self.s
        if self.kind == "home":
            return (b // 2 * 2 + s // g.half, place)
        if self.kind == "work":
            return (b // 2 * 2 + place // g.half, b % 2 * g.half + place % g.half)
        return group_device(g, place)

    @staticmethod
    def senders(g, kind):
        b, s = lax.axis_index("batch"), lax.axis_index("seq")
        if kind == "home":
            places = [(s + k) % g.seq for k in range(1, g.seq)]
            return [
                (b // 2 * 2 + place // g.half, b % 2 * g.half + place % g.half) for place in places
            ]
        places = [(group_place(g) + k) % g.seq for k in range(1, g.seq)]
        if kind == "work":
            return [(b // 2 * 2 + s // g.half, place) for place in places]
        return [group_device(g, place) for place in places]

    def block(self, pair, peer):
        if len(self.src.shape) == 4:
            return self.src.at[pair, peer]
        per = self.src.shape[1] // self.g.seq
        return self.src.at[pair, pl.ds(pl.multiple_of(peer * per, per), per), :]

    def own(self, pair):
        return pltpu.make_async_copy(
            self.block(pair, self.me), self.dst.at[pair, self.me], self.local_sem.at[pair]
        )

    def crossing(self, pair):
        return remote(
            self.block(pair, self.me),
            self.dst.at[pair, self.me],
            self.sends.at[pair, self.g.seq - 1],
            self.local_sem.at[pair],
            swap_partner(self.g),
        )

    def moves(self, pair):
        g = self.g
        made = []
        for k in range(1, g.seq):
            peer = (self.me + k) % g.seq
            made.append(
                remote(
                    self.block(pair, peer),
                    self.dst.at[pair, self.me],
                    self.sends.at[pair, k - 1],
                    self.recvs.at[pair, k - 1],
                    self.target(peer),
                )
            )
        return made

    def either(self, here, there):
        if self.kind == "group":
            here()
            return
        pl.when(self.native)(here)
        pl.when(jnp.logical_not(self.native))(there)

    def start(self, pair):
        self.either(lambda: self.own(pair).start(), lambda: self.crossing(pair).start())
        for copy in self.moves(pair):
            copy.start()

    def arrive(self, pair):
        self.either(lambda: self.own(pair).wait(), lambda: self.crossing(pair).wait_recv())
        for copy in self.moves(pair):
            copy.wait_recv()

    def sent(self, pair):
        self.either(lambda: None, lambda: self.crossing(pair).wait_send())
        for copy in self.moves(pair):
            copy.wait_send()


def exchange_sems(g, pairs):
    return [
        pltpu.SemaphoreType.DMA((pairs, g.seq)),
        pltpu.SemaphoreType.DMA((pairs, g.seq)),
        pltpu.SemaphoreType.DMA((pairs,)),
    ]


LAG = 2
BACK = 2


def unpermute_pair(pair, cols_ref, ret_ref, out_ref):
    tok = out_ref.shape[0]
    head = pl.ds(pl.multiple_of(pair * PAIR, PAIR), PAIR)

    def pick(step, carry):
        start = step * ROWS
        value = ret_ref[pair].reshape(tok, PAIR)
        out_ref[pl.ds(start, ROWS), head] = move_pair(
            lambda i: token_rows(cols_ref, 2 * pair + i, start, ROWS), value
        ).astype(BF16)
        return carry

    lax.fori_loop(0, tok // ROWS, pick, 0)


def forward_kernel(
    g,
    scale,
    factor,
    x_ref,
    wq_ref,
    wk_ref,
    wv_ref,
    bias_ref,
    places_ref,
    cols_ref,
    mask_sent,
    *refs,
):
    parts, wholes = refs[:3], refs[3:6]
    qkv_out, attended_ref, stats_ref = refs[6:9]
    flat, rhs, sent, routed, mixed, ret, mask_routed, entropy = refs[9:17]
    sems = refs[17:]
    pairs = sent.shape[0]
    greet(line_peers(g, ("y", "c")) + Exchange.senders(g, "group"))
    plan = Gather(g, parts, wholes, AXES, PART, lambda unit: ("y", "c"), *sems[:3])
    there = Exchange(g, "group", sent, routed, *sems[3:6])
    back = Exchange(g, "group", mixed, ret, *sems[6:9])
    masks = Exchange(g, "group", mask_sent, mask_routed, *sems[9:12])
    save_sem = sems[12]
    units = len(plan.units)

    def keep(pair):
        return pltpu.make_async_copy(routed.at[pair], qkv_out.at[pair], save_sem.at[pair])

    masks.start(0)
    entropy[...] = jnp.zeros_like(entropy)
    steps = pairs + LAG + BACK

    def step(t, carry):
        @pl.when(t < pairs)
        def _():
            project_pair(
                t,
                x_ref,
                (wq_ref, wk_ref, wv_ref),
                bias_ref,
                places_ref,
                flat,
                rhs,
                sent,
            )
            there.start(t)

        for when in range(steps):
            todo = [
                (unit, level)
                for level in (1, 0)
                for unit in range(units)
                if min(unit + level * WINDOW, steps - 1) == when
            ]
            if todo:

                @pl.when(t == when)
                def _(todo=todo):
                    for unit, level in todo:
                        plan.start(unit, level)

        @pl.when((t >= LAG) & (t < pairs + LAG))
        def _():
            pair = t - LAG
            there.arrive(pair)
            keep(pair).start()
            attend_pair(pair, scale, routed, mixed, entropy)
            back.start(pair)

        @pl.when(t >= LAG + BACK)
        def _():
            pair = t - LAG - BACK
            back.arrive(pair)
            unpermute_pair(pair, cols_ref, ret, attended_ref)

        return carry

    lax.fori_loop(0, steps, step, 0)

    masks.arrive(0)
    sources, per_owner = mask_routed.shape[1:3]
    size = CLUSTER // sources
    blocks = per_owner // size
    spot = lax.broadcasted_iota(jnp.int32, stats_ref.shape, 1) - group_place(g) * blocks
    row = lax.broadcasted_iota(jnp.int32, stats_ref.shape, 0)
    stats = jnp.zeros(stats_ref.shape, F32)
    for cluster in range(blocks):
        mask = gather_rows(mask_routed, (0,), cluster * size, size, slice(None)).astype(F32)
        entropy_sum = jnp.sum(entropy[cluster] * mask) * factor
        count = jnp.sum(mask) * factor
        stats += jnp.where(
            spot == cluster, jnp.where(row == 0, entropy_sum, jnp.where(row == 1, count, 0.0)), 0.0
        )
    stats_ref[...] = stats
    plan.finish()

    def close(pair, carry):
        keep(pair).wait()
        there.sent(pair)
        back.sent(pair)
        return carry

    lax.fori_loop(0, pairs, close, 0)
    masks.sent(0)


def forward(g, scale, factor, x, wq, wk, wv, bias, places, cols, mask, parts):
    tok, width = x.shape
    pairs = width // PAIR
    per_owner = tok // g.seq
    clusters = tok // CLUSTER
    shape = jax.ShapeDtypeStruct
    any_space, vmem = pl.BlockSpec(memory_space=pl.ANY), pl.BlockSpec(memory_space=pltpu.VMEM)
    lead = tuple(sizes(g)[axis] for axis in AXES)
    made = pl.pallas_call(
        functools.partial(forward_kernel, g, scale, factor),
        out_shape=[
            *(shape((*lead, *item.shape[-2:]), BF16) for item in parts),
            shape((pairs, g.seq, per_owner, 3 * PAIR), BF16),
            shape((tok, width), BF16),
            shape((8, PAIR), F32),
        ],
        in_specs=[vmem] * 7 + [any_space] * 4,
        out_specs=[any_space] * 4 + [vmem, vmem],
        scratch_shapes=[
            pltpu.VMEM((width, 3 * PAIR), BF16),
            pltpu.VMEM((tok, 3 * PAIR), BF16),
            pltpu.VMEM((pairs, tok, 3 * PAIR), BF16),
            pltpu.VMEM((pairs, g.seq, per_owner, 3 * PAIR), BF16),
            pltpu.VMEM((pairs, g.seq, per_owner, PAIR), BF16),
            pltpu.VMEM((pairs, g.seq, per_owner, PAIR), BF16),
            pltpu.VMEM((1, g.seq, per_owner, PAIR), BF16),
            pltpu.VMEM((clusters, CLUSTER, PAIR), F32),
            *Gather.sems(g, [item.shape for item in parts]),
            *exchange_sems(g, pairs),
            *exchange_sems(g, pairs),
            *exchange_sems(g, 1),
            pltpu.SemaphoreType.DMA((pairs,)),
        ],
        compiler_params=pltpu.CompilerParams(
            collective_id=2, has_side_effects=True, vmem_limit_bytes=VMEM_LIMIT
        ),
        name="forward",
    )(x, wq, wk, wv, bias, places, cols, mask, *parts)
    return made[:3], made[3:]


def cluster_scores(q, k, scale):
    return dot_nt(q, k) * scale


def attend_back_pair(slot, pair, scale, qkv_ref, grad_ref, out_ref):
    _, sources, per_owner, _ = qkv_ref.shape
    size = CLUSTER // sources
    clusters = per_owner // size
    for cluster in range(clusters):
        q, k, v = unpack(
            *(
                gather_rows(qkv_ref, (slot,), cluster * size, size, slice(i * PAIR, (i + 1) * PAIR))
                for i in range(3)
            )
        )
        grad = gather_rows(grad_ref, (slot,), cluster * size, size, slice(None))
        q2, g2 = split_pair(q), split_pair(grad)
        scores = cluster_scores(q2, k, scale)
        top = jnp.max(scores, axis=1, keepdims=True)
        weights = jnp.exp(scores - top)
        probs = weights / jnp.sum(weights, axis=1, keepdims=True)
        low = probs.astype(BF16)
        d_value = dot_tn(low, g2)
        d_prob = dot_nt(g2, v)
        inner = jnp.sum(probs * d_prob, axis=1, keepdims=True)
        d_score = (probs * (d_prob - inner)).astype(BF16)
        d_query = (
            dot(jnp.concatenate([d_score[:CLUSTER], d_score[CLUSTER:]], axis=1), split_pair(k))
            * scale
        )
        d_key = dot_tn(d_score, q2) * scale
        for i, value in enumerate(pack(d_query, d_key, d_value)):
            out_ref[
                pair, :, cluster * size : (cluster + 1) * size, i * PAIR : (i + 1) * PAIR
            ] = spread_rows(value, sources, BF16)


INV_SQRT2 = 0.7071067811865476
INV_SQRT_2PI = 0.3989422804014327


def norm_parts(value):
    centred = value - jnp.mean(value, axis=1, keepdims=True)
    rate = lax.rsqrt(jnp.mean(centred * centred, axis=1, keepdims=True) + EPSILON)
    return centred * rate, rate


def norm_back(grad, gain, normed, rate):
    inner = grad * gain
    return rate * (
        inner
        - jnp.mean(inner, axis=1, keepdims=True)
        - normed * jnp.mean(inner * normed, axis=1, keepdims=True)
    )


TILE = 512
COLS = 512
PART_ROWS = 256


def column_sum(value):
    return jnp.sum(value, axis=0, keepdims=True)


def middle_forward(x_ref, attended, w_refs, vec_ref, up_bias_ref, out_ref, kept):
    wo_ref, up_ref, down_ref = w_refs
    hidden_all, act_all, dup_all, n1_all, n2_all, r1_all, r2_all = kept
    tok, width = x_ref.shape
    wide = up_ref.shape[1]
    bo, g1, s1, bd, g2, s2 = (vec_ref[i : i + 1, :] for i in range(6))

    def tile(step, carry):
        rows = pl.ds(step * TILE, TILE)
        branch = dot(attended[rows, :], wo_ref[...]) + bo
        n1, r1 = norm_parts(x_ref[rows, :].astype(F32) + branch)
        n1_all[rows, :] = n1
        r1_all[rows, :] = r1
        hidden = (n1 * g1 + s1).astype(BF16)
        hidden_all[rows, :] = hidden
        ffn = hidden.astype(F32) + bd
        for col in range(0, wide, COLS):
            to = slice(col, col + COLS)
            pre = dot(hidden, up_ref[:, to]) + up_bias_ref[0:1, to]
            cdf = 0.5 * (1.0 + lax.erf(pre * INV_SQRT2))
            act = (pre * cdf).astype(BF16)
            dup_all[rows, to] = (cdf + pre * (jnp.exp(-0.5 * pre * pre) * INV_SQRT_2PI)).astype(BF16)
            act_all[rows, to] = act
            ffn += dot(act, down_ref[to, :])
        n2, r2 = norm_parts(ffn)
        n2_all[rows, :] = n2
        r2_all[rows, :] = r2
        out_ref[rows, :] = (n2 * g2 + s2).astype(BF16)
        return carry

    lax.fori_loop(0, tok // TILE, tile, 0)


def middle_backward(grad_ref, cols_ref, heads, w_refs, vec_ref, kept, made):
    wo_ref, up_ref, down_ref = w_refs
    hidden_all, act_all, dup_all, n1_all, n2_all, r1_all, r2_all = kept
    dffn_all, dmid_ref, datt_all, gvec_ref, g_upb_ref = made
    tok, width = dmid_ref.shape
    wide = up_ref.shape[1]
    gvec_ref[...] = jnp.zeros_like(gvec_ref)
    g_upb_ref[...] = jnp.zeros_like(g_upb_ref)
    g1, g2 = vec_ref[1:2, :], vec_ref[4:5, :]

    def tile(step, carry):
        rows = pl.ds(step * TILE, TILE)
        mask = cols_ref[rows, heads : heads + 1].astype(F32)
        gout = grad_ref[rows, :].astype(F32) * mask
        n2 = n2_all[rows, :]
        gvec_ref[4:5, :] += column_sum(gout * n2)
        gvec_ref[5:6, :] += column_sum(gout)
        d_pre = norm_back(gout, g2, n2, r2_all[rows, :])
        d_ffn = d_pre.astype(BF16)
        dffn_all[rows, :] = d_ffn
        gvec_ref[3:4, :] += column_sum(d_ffn.astype(F32))
        d_hidden = d_pre
        for col in range(0, wide, COLS):
            to = slice(col, col + COLS)
            d_up = (dot_nt(d_ffn, down_ref[to, :]) * dup_all[rows, to].astype(F32)).astype(BF16)
            dup_all[rows, to] = d_up
            g_upb_ref[0:1, to] += column_sum(d_up.astype(F32))
            d_hidden += dot_nt(d_up, up_ref[:, to])
        n1 = n1_all[rows, :]
        gvec_ref[1:2, :] += column_sum(d_hidden * n1)
        gvec_ref[2:3, :] += column_sum(d_hidden)
        d_mid = norm_back(d_hidden, g1, n1, r1_all[rows, :])
        d_branch = d_mid.astype(BF16)
        dmid_ref[rows, :] = d_branch
        gvec_ref[0:1, :] += column_sum(d_branch.astype(F32))
        datt_all[rows, :] = dot_nt(d_branch, wo_ref[...]).astype(BF16)
        return carry

    lax.fori_loop(0, tok // TILE, tile, 0)


def permute_pair(pair, places_ref, datt_all, out_ref):
    tok = datt_all.shape[0]
    to = slice(pair * PAIR, (pair + 1) * PAIR)

    def permute(step, carry):
        start = step * ROWS
        out_ref[pair, pl.ds(start, ROWS), :] = move_pair(
            lambda i: place_rows(places_ref, 2 * pair + i, start, ROWS), datt_all[:, to]
        ).astype(BF16)
        return carry

    lax.fori_loop(0, tok // ROWS, permute, 0)


def middle_weights(attended, dmid_ref, kept, dffn_all, grads):
    hidden_all, act_all, dup_all = kept[:3]
    g_out_ref, g_up_ref, g_down_ref = grads
    wide, width = act_all.shape[1], hidden_all.shape[1]

    def weights(step, carry):
        to = pl.ds(pl.multiple_of(step * PART_ROWS, PART_ROWS), PART_ROWS)
        g_down_ref[to, :] = dot_tn(act_all[:, to], dffn_all[...]).astype(BF16)
        g_up_ref[:, to] = dot_tn(hidden_all[...], dup_all[:, to]).astype(BF16)
        return carry

    lax.fori_loop(0, wide // PART_ROWS, weights, 0)

    def out_weights(step, carry):
        to = pl.ds(pl.multiple_of(step * PART_ROWS, PART_ROWS), PART_ROWS)
        g_out_ref[:, to] = dot_tn(attended[...], dmid_ref[:, to]).astype(BF16)
        return carry

    lax.fori_loop(0, width // PART_ROWS, out_weights, 0)


def middle_kernel(
    g,
    x_ref,
    attended,
    places_ref,
    cols_ref,
    wo_ref,
    up_ref,
    down_ref,
    vec_ref,
    up_bias_ref,
    grad_ref,
    out_ref,
    dmid_ref,
    datt_ref,
    g_out_ref,
    g_up_ref,
    g_down_ref,
    gvec_ref,
    g_upb_ref,
    *refs,
):
    kept, sems = refs[:7], refs[12:]
    dffn_all, datt_all, work_out, work_grad, datt_sent = refs[7:12]
    pairs = datt_sent.shape[0]
    greet(Exchange.senders(g, "group") + [swap_partner(g)])
    there = Exchange(g, "group", datt_sent, datt_ref, *sems[:3])
    w_refs = (wo_ref, up_ref, down_ref)
    swap = Swap(g, grad_ref, work_grad, *sems[5:7])
    swap_out = Swap(g, work_out, out_ref, *sems[3:5])
    swap.start()
    middle_forward(x_ref, attended, w_refs, vec_ref, up_bias_ref, work_out, kept)
    swap.wait()
    swap_out.start()
    made = (dffn_all, dmid_ref, datt_all, gvec_ref, g_upb_ref)
    middle_backward(work_grad, cols_ref, 2 * pairs, w_refs, vec_ref, kept, made)
    for pair in range(pairs):
        permute_pair(pair, places_ref, datt_all, datt_sent)
        there.start(pair)
    middle_weights(attended, dmid_ref, kept, dffn_all, (g_out_ref, g_up_ref, g_down_ref))
    for pair in range(pairs):
        there.arrive(pair)
        there.sent(pair)
    swap_out.wait()


def middle_scratch(tok, width, wide):
    return [
        pltpu.VMEM((tok, width), BF16),
        pltpu.VMEM((tok, wide), BF16),
        pltpu.VMEM((tok, wide), BF16),
        pltpu.VMEM((tok, width), F32),
        pltpu.VMEM((tok, width), F32),
        pltpu.VMEM((tok, 1), F32),
        pltpu.VMEM((tok, 1), F32),
        pltpu.VMEM((tok, width), BF16),
        pltpu.VMEM((tok, width), BF16),
        pltpu.VMEM((tok, width), BF16),
        pltpu.VMEM((tok, width), BF16),
        pltpu.VMEM((width // PAIR, tok, PAIR), BF16),
    ]


def middle(g, *args):
    x, up = args[0], args[5]
    tok, width = x.shape
    wide = up.shape[1]
    pairs = width // PAIR
    shape = jax.ShapeDtypeStruct
    any_space, vmem = pl.BlockSpec(memory_space=pl.ANY), pl.BlockSpec(memory_space=pltpu.VMEM)
    return pl.pallas_call(
        functools.partial(middle_kernel, g),
        out_shape=[
            shape((tok, width), BF16),
            shape((tok, width), BF16),
            shape((pairs, g.seq, tok // g.seq, PAIR), BF16),
            shape((width, width), BF16),
            shape((width, wide), BF16),
            shape((wide, width), BF16),
            shape((8, width), F32),
            shape((8, wide), F32),
        ],
        in_specs=[vmem] * (len(args) - 1) + [any_space],
        out_specs=[any_space, vmem, any_space] + [vmem] * 5,
        scratch_shapes=[
            *middle_scratch(tok, width, wide),
            *exchange_sems(g, pairs),
            *Swap.sems(),
            *Swap.sems(),
        ],
        compiler_params=pltpu.CompilerParams(
            collective_id=3, has_side_effects=True, vmem_limit_bytes=VMEM_LIMIT
        ),
        name="middle",
    )(*args)


Y_FIRST = ("c", "y", "x", "l", "h")
TURNS = [("c", "l", "x", "y", "h"), ("c", "x", "l", "y", "h"), ("c", "y", "l", "x", "h"), Y_FIRST]


def step_of(unit, level):
    return unit // 2 + level - (level == 1)


def backward_kernel(
    g,
    scale,
    n,
    x_ref,
    wq_ref,
    wk_ref,
    wv_ref,
    dmid_ref,
    cols_ref,
    *refs,
):
    terms, refs = refs[:n], refs[n:]
    qkv_ref, grad_ref, gtok_ref, gq_ref, gk_ref, gv_ref, gvec_ref = refs[:7]
    sums, refs = refs[7 : 7 + n], refs[7 + n :]
    qkv_slots, grad_slots, sent, home, rhs, local, flat, total = refs[:8]
    bufs, refs = refs[8 : 8 + 5 * n], refs[8 + 5 * n :]
    rs_send, rs_recv, ex_send, ex_recv, ex_local, load_sem = refs
    pairs = sent.shape[0]
    tok, width = x_ref.shape
    greet(line_peers(g) + Exchange.senders(g, "group"))
    plan = Scatter(g, terms, bufs, [Y_FIRST] * n, rs_send, rs_recv)
    there = Exchange(g, "group", sent, home, ex_send, ex_recv, ex_local)
    units = len(plan.units)

    def loads(pair):
        slot = pair % 2
        return (
            pltpu.make_async_copy(qkv_ref.at[pair], qkv_slots.at[slot], load_sem.at[0, slot]),
            pltpu.make_async_copy(grad_ref.at[pair], grad_slots.at[slot], load_sem.at[1, slot]),
        )

    for copy in loads(0):
        copy.start()
    gvec_ref[...] = jnp.zeros_like(gvec_ref)
    total[...] = dmid_ref[...].astype(F32)
    for unit in range(units):
        plan.step(unit, 0)

    def step(t, carry):
        @pl.when(t < pairs)
        def _():
            for copy in loads(t):
                copy.wait()

            @pl.when(t + 1 < pairs)
            def _():
                for copy in loads(t + 1):
                    copy.start()

            attend_back_pair(t % 2, t, scale, qkv_slots, grad_slots, sent)
            there.start(t)

        for when in range(pairs + LAG):
            todo = [
                (unit, level)
                for level in range(1, 6)
                for unit in range(units)
                if step_of(unit, level) == when
            ]
            if todo:

                @pl.when(t == when)
                def _(todo=todo):
                    for unit, level in todo:
                        plan.step(unit, level, sums)

        @pl.when(t >= LAG)
        def _():
            pair = t - LAG
            head = pl.ds(pl.multiple_of(pair * PAIR, PAIR), PAIR)
            there.arrive(pair)
            pair_weights(pair, (wq_ref, wk_ref, wv_ref), flat)

            def gather_home(owner, carry):
                per = tok // g.seq
                rhs[pl.ds(pl.multiple_of(owner * per, per), per), :] = home[pair, owner]
                return carry

            lax.fori_loop(0, g.seq, gather_home, 0)

            def unpermute(k, carry):
                start = k * ROWS
                rows = pl.ds(start, ROWS)
                made = move_rows(lambda i: token_rows(cols_ref, 2 * pair + i, start, ROWS), rhs)
                sums = [column_sum(value) for value in made]
                low = head_lanes(sums[0].shape)
                gvec_ref[0:1, head] += jnp.where(low, sums[0], sums[1])
                gvec_ref[2:3, head] += jnp.where(low, sums[1], sums[2])
                for part, value in enumerate(made):
                    local[rows, part * PAIR : (part + 1) * PAIR] = value.astype(BF16)
                total[rows, :] += dot_nt(local[rows, :], flat[...])
                return carry

            lax.fori_loop(0, tok // ROWS, unpermute, 0)

            def weights(k, carry):
                rows = pl.ds(pl.multiple_of(k * PART_ROWS, PART_ROWS), PART_ROWS)
                value = dot_tn(x_ref[:, rows], local[...])
                made = unpack(*(value[:, i * PAIR : (i + 1) * PAIR] for i in range(3)))
                for part, g_ref in enumerate((gq_ref, gk_ref, gv_ref)):
                    g_ref[rows, head] = made[part].astype(BF16)
                return carry

            lax.fori_loop(0, width // PART_ROWS, weights, 0)

        return carry

    lax.fori_loop(0, pairs + LAG, step, 0)
    gtok_ref[...] = total[...].astype(BF16)
    for when in range(pairs + LAG, step_of(units - 1, 5) + 1):
        for level in range(1, 6):
            for unit in range(units):
                if step_of(unit, level) == when:
                    plan.step(unit, level, sums)
    plan.sent()

    def close(pair, carry):
        there.sent(pair)
        return carry

    lax.fori_loop(0, pairs, close, 0)


def backward(g, scale, x, wq, wk, wv, d_mid, cols, terms, qkv, grad):
    tok, width = x.shape
    pairs = width // PAIR
    n = len(terms)
    shape = jax.ShapeDtypeStruct
    any_space, vmem = pl.BlockSpec(memory_space=pl.ANY), pl.BlockSpec(memory_space=pltpu.VMEM)
    dma = pltpu.SemaphoreType.DMA
    made = pl.pallas_call(
        functools.partial(backward_kernel, g, scale, n),
        out_shape=[
            shape((tok, width), BF16),
            *([shape((width, width), BF16)] * 3),
            shape((8, width), F32),
            *(shape(item.shape[-2:], F32) for item in terms),
        ],
        in_specs=[vmem] * (6 + n) + [any_space] * 2,
        out_specs=[vmem] * (5 + n),
        scratch_shapes=[
            pltpu.VMEM((2, *qkv.shape[1:]), BF16),
            pltpu.VMEM((2, *grad.shape[1:]), BF16),
            pltpu.VMEM(qkv.shape, BF16),
            pltpu.VMEM(qkv.shape, BF16),
            pltpu.VMEM((tok, 3 * PAIR), BF16),
            pltpu.VMEM((tok, 3 * PAIR), BF16),
            pltpu.VMEM((width, 3 * PAIR), BF16),
            pltpu.VMEM((tok, width), F32),
            *Scatter.scratch(g, [item.shape for item in terms], [Y_FIRST] * n),
            *exchange_sems(g, pairs),
            dma((2, 2)),
        ],
        compiler_params=pltpu.CompilerParams(
            collective_id=5, has_side_effects=True, vmem_limit_bytes=VMEM_LIMIT
        ),
        name="backward",
    )(x, wq, wk, wv, d_mid, cols, *terms, qkv, grad)
    return made[0], made[1:4], made[4], made[5 : 5 + n]


def close_kernel(g, n, small_ref, *refs):
    terms, gtok_ref, refs = refs[:n], refs[n], refs[n + 1 :]
    small_out, sums, gtok_home, refs = refs[0], refs[1 : 1 + n], refs[1 + n], refs[2 + n :]
    bufs, refs = refs[: 5 * n], refs[5 * n :]
    rs_send, rs_recv, small_bufs, refs = refs[0], refs[1], refs[2:7], refs[7:]
    small_send, small_recv, swap_send, swap_recv = refs
    greet(line_peers(g) + [swap_partner(g)])
    plan = Scatter(g, terms, bufs, TURNS, rs_send, rs_recv)
    swap = Swap(g, gtok_ref, gtok_home, swap_send, swap_recv)
    small = Total(g, small_ref, small_bufs, small_send, small_recv)
    units = len(plan.units)
    for unit in range(units):
        plan.step(unit, 0)
    small.start(0, small_ref[...])
    swap.start()
    for level in range(1, 6):
        for unit in range(units):
            plan.step(unit, level, sums)
        value = small.take(level - 1)
        if level < len(AXES):
            small.start(level, value)
        else:
            small_out[...] = value
    swap.wait()
    plan.sent()
    small.sent()


def close_call(g, small, terms, gtok):
    n = len(terms)
    shape = jax.ShapeDtypeStruct
    any_space, vmem = pl.BlockSpec(memory_space=pl.ANY), pl.BlockSpec(memory_space=pltpu.VMEM)
    made = pl.pallas_call(
        functools.partial(close_kernel, g, n),
        out_shape=[
            shape(small.shape, F32),
            *(shape(item.shape[-2:], F32) for item in terms),
            shape(gtok.shape, BF16),
        ],
        in_specs=[vmem] * (1 + n) + [any_space],
        out_specs=[vmem] * (1 + n) + [any_space],
        scratch_shapes=[
            *Scatter.scratch(g, [item.shape for item in terms], TURNS),
            *Total.scratch(g, small.shape),
            *Swap.sems(),
        ],
        compiler_params=pltpu.CompilerParams(
            collective_id=6, has_side_effects=True, vmem_limit_bytes=VMEM_LIMIT
        ),
        name="close",
    )(small, *terms, gtok)
    return made[0], made[1:-1], made[-1]


def body(
    g,
    tokens,
    cluster_slot,
    loss_mask,
    out_grad,
    query_weight,
    key_weight,
    value_weight,
    output_weight,
    query_bias,
    value_bias,
    output_bias,
    first_gain,
    first_shift,
    up_weight,
    up_bias,
    down_weight,
    down_bias,
    second_gain,
    second_shift,
):
    tok, width = tokens.shape[1:]
    heads = cluster_slot.shape[1]
    pairs = heads // 2
    wide = up_weight.shape[1]
    per_owner = tok // g.seq
    scale = (width // heads) ** -0.5

    slots = cluster_slot[0]
    places = slots // tok * per_owner + slots % tok // g.seq
    table = jnp.concatenate(
        [places, loss_mask, jnp.zeros((16 - heads - 1, tok), jnp.int32)], axis=0
    )
    vectors = (
        query_bias,
        value_bias,
        output_bias,
        first_gain,
        first_shift,
        down_bias,
        second_gain,
        second_shift,
    )
    count = query_bias.shape[0]
    lines = (*vectors, up_bias)
    line = lax.broadcasted_iota(jnp.int32, (16, PAIR), 0)
    packed = jnp.zeros((16, PAIR), BF16)
    for index, value in enumerate(lines):
        packed = jnp.where(line == index, jnp.pad(value, (0, PAIR - value.shape[0]))[None], packed)
    gathered, partial, (work_x, work_table, work_mask) = open_call(
        g,
        [packed, query_weight, key_weight, value_weight],
        [output_weight, up_weight, down_weight],
        [tokens[0], table],
    )
    work_cols = work_table.T

    def whole(item):
        return item.reshape(g.n * item.shape[-2], item.shape[-1])

    wq, wk, wv = (whole(item) for item in gathered[1:])
    flat = gathered[0].reshape(g.n, 16, PAIR).astype(F32)
    rows = flat[:, :8, :count].transpose(1, 0, 2).reshape(8, width)
    up_row = flat[:, 8, : up_bias.shape[0]].reshape(1, wide)
    qkv_bias = jnp.stack([rows[0], jnp.zeros((width,), F32), rows[1]])

    spread, (qkv, attended, stats) = forward(
        g,
        scale,
        1.0 / (heads * CLUSTER * g.batch),
        work_x,
        wq,
        wk,
        wv,
        qkv_bias,
        work_table,
        work_cols,
        work_mask.reshape(1, tok, PAIR),
        partial,
    )
    wo, up, down = (whole(item) for item in spread)

    out, d_mid, routed, g_out, g_up, g_down, g_rows, g_upb = middle(
        g, work_x, attended, work_table, work_cols, wo, up, down, rows[2:], up_row, out_grad[0]
    )

    def parts(item):
        rows, cols = item.shape[0] // g.n, item.shape[1]
        if rows % 8:
            rows, cols = rows * cols // PAIR, PAIR
        return item.reshape(*(sizes(g)[axis] for axis in AXES), rows, cols)

    grad_tokens, g_attn, g_bias, s_ffn = backward(
        g,
        scale,
        work_x,
        wq,
        wk,
        wv,
        d_mid,
        work_cols,
        [parts(g_up), parts(g_out)],
        qkv,
        routed,
    )
    lines = wide // width
    small = jnp.concatenate(
        [
            g_bias[0:1],
            g_bias[2:3],
            g_rows[:6],
            g_upb[0].reshape(lines, width),
            jnp.pad(stats[:2], ((0, 0), (0, width - stats.shape[1]))),
            jnp.zeros((6 - lines, width), F32),
        ],
        axis=0,
    )
    small, s_attn, grad_tokens = close_call(
        g, small, [parts(item) for item in (*g_attn, g_down)], grad_tokens
    )

    b, s = lax.axis_index("batch"), lax.axis_index("seq")
    here = b * g.seq + s
    mine = lax.dynamic_slice(small, (0, here * count), (8, count))
    wide_count = wide // g.n
    gu = lax.dynamic_slice(small[8 : 8 + lines].reshape(wide), (here * wide_count,), (wide_count,))
    blocks = tok // CLUSTER
    cluster_stats = lax.dynamic_slice(small, (8 + lines, s * blocks), (2, blocks))
    s_up, s_out, s_query, s_key, s_value, s_down = (
        item.reshape(local.shape)
        for item, local in zip(
            (*s_ffn, *s_attn),
            (up_weight, output_weight, query_weight, key_weight, value_weight, down_weight),
        )
    )
    gq, gv, go, gg1, gs1, gd, gg2, gs2 = (mine[i] for i in range(8))
    return (
        out[None],
        grad_tokens[None],
        s_query,
        s_key,
        s_value,
        s_out,
        gq,
        gv,
        go,
        gg1,
        gs1,
        s_up,
        gu,
        s_down,
        gd,
        gg2,
        gs2,
        cluster_stats,
    )


def solution(mesh):
    g = Grid(mesh)
    tokens, rows, flat = P("batch", "seq", None), P(("batch", "seq"), None), P(("batch", "seq"))
    return jax.shard_map(
        functools.partial(body, g),
        mesh=mesh,
        in_specs=(
            tokens,
            P("batch", None, "seq"),
            P("batch", "seq"),
            tokens,
            *([rows] * 4),
            *([flat] * 5),
            rows,
            flat,
            rows,
            *([flat] * 3),
        ),
        out_specs=(
            tokens,
            tokens,
            *([rows] * 4),
            *([flat] * 5),
            rows,
            flat,
            rows,
            *([flat] * 3),
            P(None, "seq"),
        ),
        check_vma=False,
    )
```

```python
import functools

import jax
import jax.numpy as jnp
from jax import lax
from jax.experimental import pallas as pl
from jax.experimental.pallas import tpu as pltpu
from jax.sharding import PartitionSpec as P

MESH = pl.DeviceIdType.MESH
F32 = jnp.float32
BF16 = jnp.bfloat16
EPSILON = 1e-12
CLUSTER = 128
PAIR = 128
Z = 4
VMEM_LIMIT = 58 * 1024 * 1024


class Grid:
    def __init__(self, mesh):
        self.batch, self.seq = mesh.shape["batch"], mesh.shape["seq"]
        self.Y, self.X = self.batch // 2, self.seq // Z
        self.half = self.seq // 2
        self.n = self.batch * self.seq


AXES = ("y", "c", "h", "l", "x")


def sizes(g):
    return {"y": g.Y, "c": 2, "h": 2, "l": Z // 2, "x": g.X}


def coords(g):
    b, s = lax.axis_index("batch"), lax.axis_index("seq")
    z = s // g.X
    return {"y": b // 2, "c": b % 2, "h": z // (Z // 2), "l": z % (Z // 2), "x": s % g.X}


def device(g, at):
    return (at["y"] * 2 + at["c"], (at["h"] * (Z // 2) + at["l"]) * g.X + at["x"])


def along(g, at, axis):
    size = sizes(g)[axis]
    places = [(at[axis] + k) % size for k in range(1, size)]
    return [(place, device(g, {**at, axis: place})) for place in places]


def group_place(g):
    b, s = lax.axis_index("batch"), lax.axis_index("seq")
    return b % 2 * g.half + s % g.half


def group_device(g, place):
    b, s = lax.axis_index("batch"), lax.axis_index("seq")
    return (b // 2 * 2 + place // g.half, s // g.half * g.half + place % g.half)


def line_peers(g, axes=AXES):
    at = coords(g)
    return [peer for axis in axes for _, peer in along(g, at, axis)]


def greet(peers):
    barrier = pltpu.get_barrier_semaphore()
    for peer in peers:
        pl.semaphore_signal(barrier, inc=1, device_id=peer, device_id_type=MESH)
    pl.semaphore_wait(barrier, len(peers))


def remote(src, dst, send, recv, peer):
    return pltpu.make_async_remote_copy(
        src_ref=src,
        dst_ref=dst,
        send_sem=send,
        recv_sem=recv,
        device_id=peer,
        device_id_type=MESH,
    )


def lane_pieces(shape):
    rows, cols = shape
    if cols % PAIR or rows * cols <= 24 * 768:
        return [(0, cols)]
    count = {3072: 4, 768: 3}.get(cols, 1)
    return [(k * (cols // count), cols // count) for k in range(count)]


class Gather:
    def __init__(self, g, ins, outs, dims, done, plan, sends, recvs, local_sem):
        self.g, self.ins, self.outs, self.dims, self.done = g, ins, outs, dims, done
        self.plan = plan
        self.sends, self.recvs, self.local_sem = sends, recvs, local_sem
        self.at = coords(g)
        self.units = [
            (index, pl.ds(start, size))
            for index, item in enumerate(ins)
            for start, size in lane_pieces(item.shape[-2:])
        ]

    @staticmethod
    def sems(g, shapes):
        units = sum(len(lane_pieces(shape[-2:])) for shape in shapes)
        slots = units * sum(sizes(g).values())
        dma = pltpu.SemaphoreType.DMA
        return [dma((slots,)), dma((slots,)), dma((units,))]

    def source(self, unit):
        index, cols = self.units[unit]
        return self.ins[index].at[(*([slice(None)] * (len(self.ins[index].shape) - 1)), cols)]

    def view(self, unit, done):
        index, cols = self.units[unit]
        spot = tuple(slice(None) if axis in done else self.at[axis] for axis in self.dims)
        return self.outs[index].at[(*spot, slice(None), cols)]

    def own(self, unit):
        return pltpu.make_async_copy(
            self.source(unit), self.view(unit, self.done), self.local_sem.at[unit]
        )

    def levels(self, unit):
        return self.plan(unit)

    def moves(self, unit, level):
        g = self.g
        axes = self.levels(unit)
        view = self.view(unit, (*self.done, *axes[:level]))
        src = self.source(unit) if level == 0 else view
        size = sizes(g)
        base = unit * sum(size.values())
        for axis in AXES[: AXES.index(axes[level])]:
            base += size[axis]
        return [
            remote(src, view, self.sends.at[base + k], self.recvs.at[base + k], peer)
            for k, (_, peer) in enumerate(along(g, self.at, axes[level]))
        ]

    def start(self, unit, level):
        if level == 0:
            self.own(unit).start()
        else:
            if level == 1:
                self.own(unit).wait()
            for copy in self.moves(unit, level - 1):
                copy.wait_recv()
        for copy in self.moves(unit, level):
            copy.start()

    def finish(self):
        count = len(self.units)
        for unit in range(count):
            for copy in self.moves(unit, len(self.levels(unit)) - 1):
                copy.wait_recv()
        for unit in range(count):
            for level in range(len(self.levels(unit))):
                for copy in self.moves(unit, level):
                    copy.wait_send()


class Swap:
    def __init__(self, g, src, dst, sends, recvs, pieces=1):
        b, s = lax.axis_index("batch"), lax.axis_index("seq")
        self.native = b % 2 == s // g.half
        self.peer = swap_partner(g)
        self.ends = (src, dst, sends, recvs)
        self.pieces = pieces

    @staticmethod
    def sems(pieces=1):
        return [pltpu.SemaphoreType.DMA((pieces,)), pltpu.SemaphoreType.DMA((pieces,))]

    def piece(self, k):
        src, dst, sends, recvs = self.ends
        size = src.shape[0] // self.pieces
        rows = pl.ds(pl.multiple_of(k * size, size), size)
        return src.at[rows], dst.at[rows], sends.at[k], recvs.at[k]

    def start(self, k=0):
        src, dst, send, recv = self.piece(k)

        @pl.when(self.native)
        def _():
            pltpu.make_async_copy(src, dst, recv).start()

        @pl.when(jnp.logical_not(self.native))
        def _():
            remote(src, dst, send, recv, self.peer).start()

    def wait(self):
        for k in range(self.pieces):
            self.wait_piece(k)

    def wait_piece(self, k):
        src, dst, send, recv = self.piece(k)

        @pl.when(self.native)
        def _():
            pltpu.make_async_copy(src, dst, recv).wait()

        @pl.when(jnp.logical_not(self.native))
        def _():
            remote(src, dst, send, recv, self.peer).wait()


def swap_partner(g):
    b, s = lax.axis_index("batch"), lax.axis_index("seq")
    return (b // 2 * 2 + 1 - b % 2, (s + g.half) % g.seq)


PART = ("h", "l", "x")
PIECES, WINDOW = 16, 2


MASK_AT = 4


def masks_in_order(heads, table_ref, block, size, out_ref):
    tok = table_ref.shape[1]
    start = block * size
    rows = lax.broadcasted_iota(jnp.int32, (size, tok), 0) + start
    lanes = lax.broadcasted_iota(jnp.int32, (size, PAIR), 1)
    mask = table_ref[heads : heads + 1, :] > 0
    made = jnp.zeros((size, PAIR), F32)
    for head in range(heads):
        places = jnp.where(mask, table_ref[head : head + 1, :], -1)
        found = jnp.sum(jnp.where(rows == places, 1.0, 0.0), axis=1, keepdims=True)
        made = jnp.where(lanes == head, found, made)
    out_ref[start : start + size, :] = made.astype(BF16)


def open_kernel(g, n, m, *refs):
    ins, refs = refs[: n + m], refs[n + m :]
    swap_in, refs = refs[:2], refs[2:]
    outs, refs = refs[: n + m], refs[n + m :]
    swap_out, mask_ref, sems = refs[:2], refs[2], refs[3:]
    greet(line_peers(g) + [swap_partner(g)])
    whole = Gather(
        g,
        ins[:n],
        outs[:n],
        AXES,
        (),
        lambda unit: ("h", "l", "x", "y", "c"),
        *sems[:3],
    )
    part = Gather(g, ins[n:], outs[n:], PART, (), lambda unit: PART, *sems[3:6])
    tokens = Swap(g, swap_in[0], swap_out[0], *sems[6:8], PIECES)
    table = Swap(g, swap_in[1], swap_out[1], *sems[8:10])
    plans = [(whole, unit) for unit in range(len(whole.units))]
    plans += [(part, unit) for unit in range(len(part.units))]
    table.start()
    tok, width = swap_in[0].shape
    heads, blocks = width * 2 // PAIR, 8
    for t in range(len(plans) + 4 * WINDOW):
        for level in range(5):
            k = t - level * WINDOW
            if 0 <= k < len(plans):
                plan, unit = plans[k]
                if level < len(plan.levels(unit)):
                    plan.start(unit, level)
        if t < PIECES:
            tokens.start(t)
        if t == MASK_AT:
            table.wait()
        if 0 <= t - MASK_AT < blocks:
            masks_in_order(heads, swap_out[1], t - MASK_AT, tok // blocks, mask_ref)
    whole.finish()
    part.finish()
    tokens.wait()


def open_call(g, whole, part, swapped):
    any_space = pl.BlockSpec(memory_space=pl.ANY)
    shape = jax.ShapeDtypeStruct
    size = sizes(g)
    n, m = len(whole), len(part)
    outs = [
        *(shape((*(size[axis] for axis in AXES), *item.shape), item.dtype) for item in whole),
        *(shape((*(size[axis] for axis in PART), *item.shape), item.dtype) for item in part),
        *(shape(item.shape, item.dtype) for item in swapped),
    ]
    vmem = pl.BlockSpec(memory_space=pltpu.VMEM)
    made = pl.pallas_call(
        functools.partial(open_kernel, g, n, m),
        out_shape=[*outs, shape((swapped[0].shape[0], PAIR), BF16)],
        in_specs=[vmem] * (n + m) + [any_space, vmem],
        out_specs=[any_space] * (n + m) + [vmem] * 3,
        scratch_shapes=[
            *Gather.sems(g, [item.shape for item in whole]),
            *Gather.sems(g, [item.shape for item in part]),
            *Swap.sems(PIECES),
            *Swap.sems(),
        ],
        compiler_params=pltpu.CompilerParams(
            collective_id=0, has_side_effects=True, vmem_limit_bytes=VMEM_LIMIT
        ),
        name="open",
    )(*whole, *part, *swapped)
    return made[:n], made[n : n + m], made[n + m :]


class Scatter:
    def __init__(self, g, ins, bufs, plans, sends, recvs):
        self.g, self.ins, self.bufs, self.plans = g, ins, bufs, plans
        self.sends, self.recvs = sends, recvs
        self.at = coords(g)
        self.units = [
            (index, pl.ds(start, size))
            for index, item in enumerate(ins)
            for start, size in lane_pieces(item.shape[-2:])
        ]

    @staticmethod
    def scratch(g, shapes, plans):
        size = sizes(g)
        made = []
        for shape, plan in zip(shapes, plans):
            left = list(AXES)
            for axis in plan:
                left.remove(axis)
                lead = (size[axis] - 1, *(size[other] for other in left))
                made.append(pltpu.VMEM((*lead, *shape[-2:]), BF16))
        units = sum(len(lane_pieces(shape[-2:])) for shape in shapes)
        slots = units * sum(size.values())
        return [*made, pltpu.SemaphoreType.DMA((slots,)), pltpu.SemaphoreType.DMA((slots,))]

    def held(self, index, level):
        return self.bufs[index * len(AXES) + level]

    def store(self, index, level):
        if level == 0:
            return self.ins[index], AXES
        left = tuple(axis for axis in AXES if axis not in self.plans[index][:level])
        return self.held(index, level - 1).at[0], left

    def moves(self, unit, level):
        g = self.g
        index, cols = self.units[unit]
        axis = self.plans[index][level]
        src, left = self.store(index, level)
        held = self.held(index, level)
        size = sizes(g)
        base = unit * sum(size.values())
        for other in AXES[: AXES.index(axis)]:
            base += size[other]
        a = slice(None)
        rest = (a,) * len(left)
        made = []
        for k, (place, peer) in enumerate(along(g, self.at, axis)):
            spot = tuple(place if other == axis else a for other in left)
            made.append(
                remote(
                    src.at[(*spot, a, cols)],
                    held.at[(k, *rest, cols)],
                    self.sends.at[base + k],
                    self.recvs.at[base + k],
                    peer,
                )
            )
        return made

    def add(self, unit, level, out=None):
        g = self.g
        index, cols = self.units[unit]
        axis = self.plans[index][level]
        src, left = self.store(index, level)
        held = self.held(index, level)
        size = sizes(g)
        rest = [other for other in left if other != axis]
        loop = [other for other in rest if other in ("h", "l")]
        count = 1
        for other in loop:
            count *= size[other]
        static = [other for other in rest if other not in loop]
        a = slice(None)

        def some(step, carry):
            spots = [{}]
            for other in static:
                spots = [{**spot, other: k} for spot in spots for k in range(size[other])]
            for spot in spots:
                if len(loop) == 2:
                    spot = {**spot, "h": step // size["l"], "l": step % size["l"]}
                elif loop:
                    spot = {**spot, loop[0]: step}
                where = tuple(spot[other] for other in rest)
                mine = tuple(self.at[axis] if other == axis else spot[other] for other in left)
                total = src[(*mine, a, cols)].astype(F32)
                for k in range(size[axis] - 1):
                    total += held[(k, *where, a, cols)].astype(F32)
                if out is None:
                    held[(0, *where, a, cols)] = total.astype(BF16)
                else:
                    out[(*where, a, cols)] = total.astype(out.dtype)
            return carry

        lax.fori_loop(0, count, some, 0)

    def step(self, unit, level, out=None):
        if level:
            for copy in self.moves(unit, level - 1):
                copy.wait_recv()
            last = level == len(AXES)
            self.add(unit, level - 1, out[self.units[unit][0]] if last else None)
        if level < len(AXES):
            for copy in self.moves(unit, level):
                copy.start()

    def sent(self):
        for unit in range(len(self.units)):
            for level in range(len(AXES)):
                for copy in self.moves(unit, level):
                    copy.wait_send()


class Total:
    def __init__(self, g, held, bufs, sends, recvs):
        self.g, self.held, self.bufs = g, held, bufs
        self.sends, self.recvs = sends, recvs
        self.at = coords(g)

    @staticmethod
    def scratch(g, shape):
        slots = sum(sizes(g).values())
        return [
            *(pltpu.VMEM((sizes(g)[axis], *shape), F32) for axis in AXES),
            pltpu.SemaphoreType.DMA((slots,)),
            pltpu.SemaphoreType.DMA((slots,)),
        ]

    def moves(self, level):
        g = self.g
        axis = AXES[level]
        view = self.bufs[level].at[self.at[axis]]
        base = sum(sizes(g)[other] for other in AXES[:level])
        return [
            remote(view, view, self.sends.at[base + k], self.recvs.at[base + k], peer)
            for k, (_, peer) in enumerate(along(g, self.at, axis))
        ]

    def start(self, level, value):
        self.bufs[level][self.at[AXES[level]]] = value
        for copy in self.moves(level):
            copy.start()

    def take(self, level):
        for copy in self.moves(level):
            copy.wait_recv()
        buf = self.bufs[level]
        total = buf[0]
        for k in range(1, buf.shape[0]):
            total = total + buf[k]
        return total

    def sent(self):
        for level in range(len(AXES)):
            for copy in self.moves(level):
                copy.wait_send()


def dot(left, right):
    return lax.dot_general(left, right, (((1,), (0,)), ((), ())), preferred_element_type=F32)


def dot_nt(left, right):
    return lax.dot_general(left, right, (((1,), (1,)), ((), ())), preferred_element_type=F32)


def dot_tn(left, right):
    return lax.dot_general(left, right, (((0,), (0,)), ((), ())), preferred_element_type=F32)


def head_lanes(shape):
    return lax.broadcasted_iota(jnp.int32, shape, 1) < PAIR // 2


def split_pair(value, axis=0):
    low = head_lanes(value.shape)
    zero = jnp.zeros_like(value)
    return jnp.concatenate(
        [jnp.where(low, value, zero), jnp.where(low, zero, value)], axis=axis
    )


def swap_halves(value):
    return pltpu.roll(value.astype(F32), PAIR // 2, 1).astype(value.dtype)


def pack(q, k, v):
    low = head_lanes(q.shape)
    k = swap_halves(k)
    return jnp.where(low, q, k), jnp.where(low, v, q), jnp.where(low, k, v)


def unpack(first, second, third):
    low = head_lanes(first.shape)
    return (
        jnp.where(low, first, second),
        swap_halves(jnp.where(low, third, first)),
        jnp.where(low, second, third),
    )


def place_rows(places_ref, head, start, size):
    tok = places_ref.shape[1]
    rows = lax.broadcasted_iota(jnp.int32, (size, tok), 0) + start
    return (rows == places_ref[pl.ds(head, 1), :]).astype(F32).astype(BF16)


def token_rows(cols_ref, head, start, size):
    tok, width = cols_ref.shape
    lanes = lax.broadcasted_iota(jnp.int32, (size, tok), 1)
    heads = lax.broadcasted_iota(jnp.int32, (size, width), 1)
    table = cols_ref[pl.ds(start, size), :].astype(F32)
    place = jnp.sum(jnp.where(heads == head, table, 0.0), axis=1, keepdims=True)
    return (lanes == place.astype(jnp.int32)).astype(F32).astype(BF16)


def move_rows(pick, value_ref):
    one = dot(pick(0), value_ref[:, : 2 * PAIR])
    two = dot(pick(1), value_ref[:, PAIR:])
    low = head_lanes((one.shape[0], PAIR))
    return one[:, :PAIR], jnp.where(low, one[:, PAIR:], two[:, :PAIR]), two[:, PAIR:]


def move_pair(pick, value):
    one, two = dot(pick(0), value), dot(pick(1), value)
    return jnp.where(head_lanes(one.shape), one, two)


def gather_rows(block_ref, lead, start, size, lanes):
    part = block_ref[(*lead, slice(None), pl.ds(start, size), lanes)]
    if size % 16:
        part = part.astype(F32)
    return part.reshape(part.shape[0] * size, part.shape[2]).astype(block_ref.dtype)


def spread_rows(value, sources, kind):
    size = value.shape[0] // sources
    if size % 16:
        return value.astype(F32).reshape(sources, size, value.shape[1]).astype(kind)
    return value.astype(kind).reshape(sources, size, value.shape[1])


ROWS = 512


def pair_weights(pair, w_refs, out_ref):
    head = pl.ds(pl.multiple_of(pair * PAIR, PAIR), PAIR)
    for part, value in enumerate(pack(*(w_ref[:, head] for w_ref in w_refs))):
        out_ref[:, part * PAIR : (part + 1) * PAIR] = value


def project_pair(pair, x_ref, w_refs, bias_ref, places_ref, flat, rhs, out_ref):
    tok = x_ref.shape[0]
    head = pl.ds(pl.multiple_of(pair * PAIR, PAIR), PAIR)
    pair_weights(pair, w_refs, flat)
    bias = jnp.concatenate(
        pack(*(jnp.broadcast_to(bias_ref[i : i + 1, head], (8, PAIR)) for i in range(3))), axis=1
    )[0:1]

    def project(step, carry):
        rows = pl.ds(step * ROWS, ROWS)
        rhs[rows, :] = (dot(x_ref[rows, :], flat[...]) + bias).astype(BF16)
        return carry

    lax.fori_loop(0, tok // ROWS, project, 0)

    def permute(step, carry):
        start = step * ROWS
        made = move_rows(lambda i: place_rows(places_ref, 2 * pair + i, start, ROWS), rhs)
        for part, value in enumerate(made):
            out_ref[pair, pl.ds(start, ROWS), part * PAIR : (part + 1) * PAIR] = value.astype(BF16)
        return carry

    lax.fori_loop(0, tok // ROWS, permute, 0)


def attend_pair(pair, scale, qkv_ref, out_ref, entropy_ref):
    _, sources, per_owner, _ = qkv_ref.shape
    size = CLUSTER // sources
    clusters = per_owner // size
    lanes = lax.broadcasted_iota(jnp.int32, (CLUSTER, PAIR), 1)
    for cluster in range(clusters):
        q, k, v = unpack(
            *(
                gather_rows(qkv_ref, (pair,), cluster * size, size, slice(i * PAIR, (i + 1) * PAIR))
                for i in range(3)
            )
        )
        scores = cluster_scores(split_pair(q), k, scale)
        top = jnp.max(scores, axis=1, keepdims=True)
        weights = jnp.exp(scores - top)
        totals = jnp.sum(weights, axis=1, keepdims=True)
        probs = weights / totals
        entropy = top + jnp.log(totals) - jnp.sum(probs * scores, axis=1, keepdims=True)
        low = probs.astype(BF16)
        mixed = dot(
            jnp.concatenate([low[:CLUSTER], low[CLUSTER:]], axis=1), split_pair(v)
        )
        out_ref[pair, :, cluster * size : (cluster + 1) * size, :] = spread_rows(
            mixed, sources, BF16
        )
        entropy_ref[cluster] = jnp.where(
            lanes == 2 * pair,
            entropy[:CLUSTER],
            jnp.where(lanes == 2 * pair + 1, entropy[CLUSTER:], entropy_ref[cluster]),
        )


class Exchange:
    def __init__(self, g, kind, src, dst, sends, recvs, local_sem):
        self.g, self.kind, self.src, self.dst = g, kind, src, dst
        self.sends, self.recvs, self.local_sem = sends, recvs, local_sem
        b, s = lax.axis_index("batch"), lax.axis_index("seq")
        self.b, self.s = b, s
        self.me = s if kind == "work" else group_place(g)
        self.native = b % 2 == s // g.half

    def target(self, place):
        g, b, s = self.g, self.b, self.s
        if self.kind == "home":
            return (b // 2 * 2 + s // g.half, place)
        if self.kind == "work":
            return (b // 2 * 2 + place // g.half, b % 2 * g.half + place % g.half)
        return group_device(g, place)

    @staticmethod
    def senders(g, kind):
        b, s = lax.axis_index("batch"), lax.axis_index("seq")
        if kind == "home":
            places = [(s + k) % g.seq for k in range(1, g.seq)]
            return [
                (b // 2 * 2 + place // g.half, b % 2 * g.half + place % g.half) for place in places
            ]
        places = [(group_place(g) + k) % g.seq for k in range(1, g.seq)]
        if kind == "work":
            return [(b // 2 * 2 + s // g.half, place) for place in places]
        return [group_device(g, place) for place in places]

    def block(self, pair, peer):
        if len(self.src.shape) == 4:
            return self.src.at[pair, peer]
        per = self.src.shape[1] // self.g.seq
        return self.src.at[pair, pl.ds(pl.multiple_of(peer * per, per), per), :]

    def own(self, pair):
        return pltpu.make_async_copy(
            self.block(pair, self.me), self.dst.at[pair, self.me], self.local_sem.at[pair]
        )

    def crossing(self, pair):
        return remote(
            self.block(pair, self.me),
            self.dst.at[pair, self.me],
            self.sends.at[pair, self.g.seq - 1],
            self.local_sem.at[pair],
            swap_partner(self.g),
        )

    def moves(self, pair):
        g = self.g
        made = []
        for k in range(1, g.seq):
            peer = (self.me + k) % g.seq
            made.append(
                remote(
                    self.block(pair, peer),
                    self.dst.at[pair, self.me],
                    self.sends.at[pair, k - 1],
                    self.recvs.at[pair, k - 1],
                    self.target(peer),
                )
            )
        return made

    def either(self, here, there):
        if self.kind == "group":
            here()
            return
        pl.when(self.native)(here)
        pl.when(jnp.logical_not(self.native))(there)

    def start(self, pair):
        self.either(lambda: self.own(pair).start(), lambda: self.crossing(pair).start())
        for copy in self.moves(pair):
            copy.start()

    def arrive(self, pair):
        self.either(lambda: self.own(pair).wait(), lambda: self.crossing(pair).wait_recv())
        for copy in self.moves(pair):
            copy.wait_recv()

    def sent(self, pair):
        self.either(lambda: None, lambda: self.crossing(pair).wait_send())
        for copy in self.moves(pair):
            copy.wait_send()


def exchange_sems(g, pairs):
    return [
        pltpu.SemaphoreType.DMA((pairs, g.seq)),
        pltpu.SemaphoreType.DMA((pairs, g.seq)),
        pltpu.SemaphoreType.DMA((pairs,)),
    ]


LAG = 2
BACK = 2


def unpermute_pair(pair, cols_ref, ret_ref, out_ref):
    tok = out_ref.shape[0]
    head = pl.ds(pl.multiple_of(pair * PAIR, PAIR), PAIR)

    def pick(step, carry):
        start = step * ROWS
        value = ret_ref[pair].reshape(tok, PAIR)
        out_ref[pl.ds(start, ROWS), head] = move_pair(
            lambda i: token_rows(cols_ref, 2 * pair + i, start, ROWS), value
        ).astype(BF16)
        return carry

    lax.fori_loop(0, tok // ROWS, pick, 0)


def forward_kernel(
    g,
    scale,
    factor,
    x_ref,
    wq_ref,
    wk_ref,
    wv_ref,
    bias_ref,
    places_ref,
    cols_ref,
    mask_sent,
    *refs,
):
    parts, wholes = refs[:3], refs[3:6]
    qkv_out, attended_ref, stats_ref = refs[6:9]
    flat, rhs, sent, routed, mixed, ret, mask_routed, entropy = refs[9:17]
    sems = refs[17:]
    pairs = sent.shape[0]
    greet(line_peers(g, ("y", "c")) + Exchange.senders(g, "group"))
    plan = Gather(g, parts, wholes, AXES, PART, lambda unit: ("y", "c"), *sems[:3])
    there = Exchange(g, "group", sent, routed, *sems[3:6])
    back = Exchange(g, "group", mixed, ret, *sems[6:9])
    masks = Exchange(g, "group", mask_sent, mask_routed, *sems[9:12])
    save_sem = sems[12]
    units = len(plan.units)

    def keep(pair):
        return pltpu.make_async_copy(routed.at[pair], qkv_out.at[pair], save_sem.at[pair])

    masks.start(0)
    entropy[...] = jnp.zeros_like(entropy)
    steps = pairs + LAG + BACK

    def step(t, carry):
        @pl.when(t < pairs)
        def _():
            project_pair(
                t,
                x_ref,
                (wq_ref, wk_ref, wv_ref),
                bias_ref,
                places_ref,
                flat,
                rhs,
                sent,
            )
            there.start(t)

        for when in range(steps):
            todo = [
                (unit, level)
                for level in (1, 0)
                for unit in range(units)
                if min(unit + level * WINDOW, steps - 1) == when
            ]
            if todo:

                @pl.when(t == when)
                def _(todo=todo):
                    for unit, level in todo:
                        plan.start(unit, level)

        @pl.when((t >= LAG) & (t < pairs + LAG))
        def _():
            pair = t - LAG
            there.arrive(pair)
            keep(pair).start()
            attend_pair(pair, scale, routed, mixed, entropy)
            back.start(pair)

        @pl.when(t >= LAG + BACK)
        def _():
            pair = t - LAG - BACK
            back.arrive(pair)
            unpermute_pair(pair, cols_ref, ret, attended_ref)

        return carry

    lax.fori_loop(0, steps, step, 0)

    masks.arrive(0)
    sources, per_owner = mask_routed.shape[1:3]
    size = CLUSTER // sources
    blocks = per_owner // size
    spot = lax.broadcasted_iota(jnp.int32, stats_ref.shape, 1) - group_place(g) * blocks
    row = lax.broadcasted_iota(jnp.int32, stats_ref.shape, 0)
    stats = jnp.zeros(stats_ref.shape, F32)
    for cluster in range(blocks):
        mask = gather_rows(mask_routed, (0,), cluster * size, size, slice(None)).astype(F32)
        entropy_sum = jnp.sum(entropy[cluster] * mask) * factor
        count = jnp.sum(mask) * factor
        stats += jnp.where(
            spot == cluster, jnp.where(row == 0, entropy_sum, jnp.where(row == 1, count, 0.0)), 0.0
        )
    stats_ref[...] = stats
    plan.finish()

    def close(pair, carry):
        keep(pair).wait()
        there.sent(pair)
        back.sent(pair)
        return carry

    lax.fori_loop(0, pairs, close, 0)
    masks.sent(0)


def forward(g, scale, factor, x, wq, wk, wv, bias, places, cols, mask, parts):
    tok, width = x.shape
    pairs = width // PAIR
    per_owner = tok // g.seq
    clusters = tok // CLUSTER
    shape = jax.ShapeDtypeStruct
    any_space, vmem = pl.BlockSpec(memory_space=pl.ANY), pl.BlockSpec(memory_space=pltpu.VMEM)
    lead = tuple(sizes(g)[axis] for axis in AXES)
    made = pl.pallas_call(
        functools.partial(forward_kernel, g, scale, factor),
        out_shape=[
            *(shape((*lead, *item.shape[-2:]), BF16) for item in parts),
            shape((pairs, g.seq, per_owner, 3 * PAIR), BF16),
            shape((tok, width), BF16),
            shape((8, PAIR), F32),
        ],
        in_specs=[vmem] * 11,
        out_specs=[any_space] * 4 + [vmem, vmem],
        scratch_shapes=[
            pltpu.VMEM((width, 3 * PAIR), BF16),
            pltpu.VMEM((tok, 3 * PAIR), BF16),
            pltpu.VMEM((pairs, tok, 3 * PAIR), BF16),
            pltpu.VMEM((pairs, g.seq, per_owner, 3 * PAIR), BF16),
            pltpu.VMEM((pairs, g.seq, per_owner, PAIR), BF16),
            pltpu.VMEM((pairs, g.seq, per_owner, PAIR), BF16),
            pltpu.VMEM((1, g.seq, per_owner, PAIR), BF16),
            pltpu.VMEM((clusters, CLUSTER, PAIR), F32),
            *Gather.sems(g, [item.shape for item in parts]),
            *exchange_sems(g, pairs),
            *exchange_sems(g, pairs),
            *exchange_sems(g, 1),
            pltpu.SemaphoreType.DMA((pairs,)),
        ],
        compiler_params=pltpu.CompilerParams(
            collective_id=2, has_side_effects=True, vmem_limit_bytes=VMEM_LIMIT
        ),
        name="forward",
    )(x, wq, wk, wv, bias, places, cols, mask, *parts)
    return made[:3], made[3:]


def cluster_scores(q, k, scale):
    return dot_nt(q, k) * scale


def attend_back_pair(slot, pair, scale, qkv_ref, grad_ref, out_ref):
    _, sources, per_owner, _ = qkv_ref.shape
    size = CLUSTER // sources
    clusters = per_owner // size
    for cluster in range(clusters):
        q, k, v = unpack(
            *(
                gather_rows(qkv_ref, (slot,), cluster * size, size, slice(i * PAIR, (i + 1) * PAIR))
                for i in range(3)
            )
        )
        grad = gather_rows(grad_ref, (slot,), cluster * size, size, slice(None))
        q2, g2 = split_pair(q), split_pair(grad)
        scores = cluster_scores(q2, k, scale)
        top = jnp.max(scores, axis=1, keepdims=True)
        weights = jnp.exp(scores - top)
        probs = weights / jnp.sum(weights, axis=1, keepdims=True)
        low = probs.astype(BF16)
        d_value = dot_tn(low, g2)
        d_prob = dot_nt(g2, v)
        inner = jnp.sum(probs * d_prob, axis=1, keepdims=True)
        d_score = (probs * (d_prob - inner)).astype(BF16)
        d_query = (
            dot(jnp.concatenate([d_score[:CLUSTER], d_score[CLUSTER:]], axis=1), split_pair(k))
            * scale
        )
        d_key = dot_tn(d_score, q2) * scale
        for i, value in enumerate(pack(d_query, d_key, d_value)):
            out_ref[
                pair, :, cluster * size : (cluster + 1) * size, i * PAIR : (i + 1) * PAIR
            ] = spread_rows(value, sources, BF16)


INV_SQRT2 = 0.7071067811865476
INV_SQRT_2PI = 0.3989422804014327


def norm_parts(value):
    centred = value - jnp.mean(value, axis=1, keepdims=True)
    rate = lax.rsqrt(jnp.mean(centred * centred, axis=1, keepdims=True) + EPSILON)
    return centred * rate, rate


def norm_back(grad, gain, normed, rate):
    inner = grad * gain
    return rate * (
        inner
        - jnp.mean(inner, axis=1, keepdims=True)
        - normed * jnp.mean(inner * normed, axis=1, keepdims=True)
    )


TILE = 512
COLS = 512
PART_ROWS = 256


def column_sum(value):
    return jnp.sum(value, axis=0, keepdims=True)


def middle_forward(x_ref, attended, w_refs, vec_ref, up_bias_ref, out_ref, kept):
    wo_ref, up_ref, down_ref = w_refs
    hidden_all, act_all, dup_all, n1_all, n2_all, r1_all, r2_all = kept
    tok, width = x_ref.shape
    wide = up_ref.shape[1]
    bo, g1, s1, bd, g2, s2 = (vec_ref[i : i + 1, :] for i in range(6))

    def tile(step, carry):
        rows = pl.ds(step * TILE, TILE)
        branch = dot(attended[rows, :], wo_ref[...]) + bo
        n1, r1 = norm_parts(x_ref[rows, :].astype(F32) + branch)
        n1_all[rows, :] = n1
        r1_all[rows, :] = r1
        hidden = (n1 * g1 + s1).astype(BF16)
        hidden_all[rows, :] = hidden
        ffn = hidden.astype(F32) + bd
        for col in range(0, wide, COLS):
            to = slice(col, col + COLS)
            pre = dot(hidden, up_ref[:, to]) + up_bias_ref[0:1, to]
            cdf = 0.5 * (1.0 + lax.erf(pre * INV_SQRT2))
            act = (pre * cdf).astype(BF16)
            dup_all[rows, to] = (cdf + pre * (jnp.exp(-0.5 * pre * pre) * INV_SQRT_2PI)).astype(BF16)
            act_all[rows, to] = act
            ffn += dot(act, down_ref[to, :])
        n2, r2 = norm_parts(ffn)
        n2_all[rows, :] = n2
        r2_all[rows, :] = r2
        out_ref[rows, :] = (n2 * g2 + s2).astype(BF16)
        return carry

    lax.fori_loop(0, tok // TILE, tile, 0)


def middle_backward(grad_ref, cols_ref, heads, w_refs, vec_ref, kept, made):
    wo_ref, up_ref, down_ref = w_refs
    hidden_all, act_all, dup_all, n1_all, n2_all, r1_all, r2_all = kept
    dffn_all, dmid_ref, datt_all, gvec_ref, g_upb_ref = made
    tok, width = dmid_ref.shape
    wide = up_ref.shape[1]
    gvec_ref[...] = jnp.zeros_like(gvec_ref)
    g_upb_ref[...] = jnp.zeros_like(g_upb_ref)
    g1, g2 = vec_ref[1:2, :], vec_ref[4:5, :]

    def tile(step, carry):
        rows = pl.ds(step * TILE, TILE)
        mask = cols_ref[rows, heads : heads + 1].astype(F32)
        gout = grad_ref[rows, :].astype(F32) * mask
        n2 = n2_all[rows, :]
        gvec_ref[4:5, :] += column_sum(gout * n2)
        gvec_ref[5:6, :] += column_sum(gout)
        d_pre = norm_back(gout, g2, n2, r2_all[rows, :])
        d_ffn = d_pre.astype(BF16)
        dffn_all[rows, :] = d_ffn
        gvec_ref[3:4, :] += column_sum(d_ffn.astype(F32))
        d_hidden = d_pre
        for col in range(0, wide, COLS):
            to = slice(col, col + COLS)
            d_up = (dot_nt(d_ffn, down_ref[to, :]) * dup_all[rows, to].astype(F32)).astype(BF16)
            dup_all[rows, to] = d_up
            g_upb_ref[0:1, to] += column_sum(d_up.astype(F32))
            d_hidden += dot_nt(d_up, up_ref[:, to])
        n1 = n1_all[rows, :]
        gvec_ref[1:2, :] += column_sum(d_hidden * n1)
        gvec_ref[2:3, :] += column_sum(d_hidden)
        d_mid = norm_back(d_hidden, g1, n1, r1_all[rows, :])
        d_branch = d_mid.astype(BF16)
        dmid_ref[rows, :] = d_branch
        gvec_ref[0:1, :] += column_sum(d_branch.astype(F32))
        datt_all[rows, :] = dot_nt(d_branch, wo_ref[...]).astype(BF16)
        return carry

    lax.fori_loop(0, tok // TILE, tile, 0)


def permute_pair(pair, places_ref, datt_all, out_ref):
    tok = datt_all.shape[0]
    to = slice(pair * PAIR, (pair + 1) * PAIR)

    def permute(step, carry):
        start = step * ROWS
        out_ref[pair, pl.ds(start, ROWS), :] = move_pair(
            lambda i: place_rows(places_ref, 2 * pair + i, start, ROWS), datt_all[:, to]
        ).astype(BF16)
        return carry

    lax.fori_loop(0, tok // ROWS, permute, 0)


def middle_weights(attended, dmid_ref, kept, dffn_all, grads):
    hidden_all, act_all, dup_all = kept[:3]
    g_out_ref, g_up_ref, g_down_ref = grads
    wide, width = act_all.shape[1], hidden_all.shape[1]

    def weights(step, carry):
        to = pl.ds(pl.multiple_of(step * PART_ROWS, PART_ROWS), PART_ROWS)
        g_down_ref[to, :] = dot_tn(act_all[:, to], dffn_all[...]).astype(BF16)
        g_up_ref[:, to] = dot_tn(hidden_all[...], dup_all[:, to]).astype(BF16)
        return carry

    lax.fori_loop(0, wide // PART_ROWS, weights, 0)

    def out_weights(step, carry):
        to = pl.ds(pl.multiple_of(step * PART_ROWS, PART_ROWS), PART_ROWS)
        g_out_ref[:, to] = dot_tn(attended[...], dmid_ref[:, to]).astype(BF16)
        return carry

    lax.fori_loop(0, width // PART_ROWS, out_weights, 0)


def middle_kernel(
    g,
    x_ref,
    attended,
    places_ref,
    cols_ref,
    wo_ref,
    up_ref,
    down_ref,
    vec_ref,
    up_bias_ref,
    grad_ref,
    out_ref,
    dmid_ref,
    datt_ref,
    g_out_ref,
    g_up_ref,
    g_down_ref,
    gvec_ref,
    g_upb_ref,
    *refs,
):
    kept, sems = refs[:7], refs[12:]
    dffn_all, datt_all, work_out, work_grad, datt_sent = refs[7:12]
    pairs = datt_sent.shape[0]
    greet(Exchange.senders(g, "group") + [swap_partner(g)])
    there = Exchange(g, "group", datt_sent, datt_ref, *sems[:3])
    w_refs = (wo_ref, up_ref, down_ref)
    swap = Swap(g, grad_ref, work_grad, *sems[5:7])
    swap_out = Swap(g, work_out, out_ref, *sems[3:5])
    swap.start()
    middle_forward(x_ref, attended, w_refs, vec_ref, up_bias_ref, work_out, kept)
    swap.wait()
    swap_out.start()
    made = (dffn_all, dmid_ref, datt_all, gvec_ref, g_upb_ref)
    middle_backward(work_grad, cols_ref, 2 * pairs, w_refs, vec_ref, kept, made)
    for pair in range(pairs):
        permute_pair(pair, places_ref, datt_all, datt_sent)
        there.start(pair)
    middle_weights(attended, dmid_ref, kept, dffn_all, (g_out_ref, g_up_ref, g_down_ref))
    for pair in range(pairs):
        there.arrive(pair)
        there.sent(pair)
    swap_out.wait()


def middle_scratch(tok, width, wide):
    return [
        pltpu.VMEM((tok, width), BF16),
        pltpu.VMEM((tok, wide), BF16),
        pltpu.VMEM((tok, wide), BF16),
        pltpu.VMEM((tok, width), F32),
        pltpu.VMEM((tok, width), F32),
        pltpu.VMEM((tok, 1), F32),
        pltpu.VMEM((tok, 1), F32),
        pltpu.VMEM((tok, width), BF16),
        pltpu.VMEM((tok, width), BF16),
        pltpu.VMEM((tok, width), BF16),
        pltpu.VMEM((tok, width), BF16),
        pltpu.VMEM((width // PAIR, tok, PAIR), BF16),
    ]


def middle(g, *args):
    x, up = args[0], args[5]
    tok, width = x.shape
    wide = up.shape[1]
    pairs = width // PAIR
    shape = jax.ShapeDtypeStruct
    any_space, vmem = pl.BlockSpec(memory_space=pl.ANY), pl.BlockSpec(memory_space=pltpu.VMEM)
    return pl.pallas_call(
        functools.partial(middle_kernel, g),
        out_shape=[
            shape((tok, width), BF16),
            shape((tok, width), BF16),
            shape((pairs, g.seq, tok // g.seq, PAIR), BF16),
            shape((width, width), BF16),
            shape((width, wide), BF16),
            shape((wide, width), BF16),
            shape((8, width), F32),
            shape((8, wide), F32),
        ],
        in_specs=[vmem] * (len(args) - 1) + [any_space],
        out_specs=[any_space, vmem, any_space] + [vmem] * 5,
        scratch_shapes=[
            *middle_scratch(tok, width, wide),
            *exchange_sems(g, pairs),
            *Swap.sems(),
            *Swap.sems(),
        ],
        compiler_params=pltpu.CompilerParams(
            collective_id=3, has_side_effects=True, vmem_limit_bytes=VMEM_LIMIT
        ),
        name="middle",
    )(*args)


Y_FIRST = ("c", "y", "x", "l", "h")
TURNS = [("c", "l", "x", "y", "h"), ("c", "x", "l", "y", "h"), ("c", "y", "l", "x", "h"), Y_FIRST]


def step_of(unit, level):
    return unit // 2 + level - (level == 1)


def backward_kernel(
    g,
    scale,
    n,
    x_ref,
    wq_ref,
    wk_ref,
    wv_ref,
    dmid_ref,
    cols_ref,
    *refs,
):
    terms, refs = refs[:n], refs[n:]
    qkv_ref, grad_ref, gtok_ref, gq_ref, gk_ref, gv_ref, gvec_ref = refs[:7]
    sums, refs = refs[7 : 7 + n], refs[7 + n :]
    qkv_slots, grad_slots, sent, home, rhs, local, flat, total = refs[:8]
    bufs, refs = refs[8 : 8 + 5 * n], refs[8 + 5 * n :]
    rs_send, rs_recv, ex_send, ex_recv, ex_local, load_sem = refs
    pairs = sent.shape[0]
    tok, width = x_ref.shape
    greet(line_peers(g) + Exchange.senders(g, "group"))
    plan = Scatter(g, terms, bufs, [Y_FIRST] * n, rs_send, rs_recv)
    there = Exchange(g, "group", sent, home, ex_send, ex_recv, ex_local)
    units = len(plan.units)

    def loads(pair):
        slot = pair % 2
        return (
            pltpu.make_async_copy(qkv_ref.at[pair], qkv_slots.at[slot], load_sem.at[0, slot]),
            pltpu.make_async_copy(grad_ref.at[pair], grad_slots.at[slot], load_sem.at[1, slot]),
        )

    for copy in loads(0):
        copy.start()
    gvec_ref[...] = jnp.zeros_like(gvec_ref)
    total[...] = dmid_ref[...].astype(F32)
    for unit in range(units):
        plan.step(unit, 0)

    def step(t, carry):
        @pl.when(t < pairs)
        def _():
            for copy in loads(t):
                copy.wait()

            @pl.when(t + 1 < pairs)
            def _():
                for copy in loads(t + 1):
                    copy.start()

            attend_back_pair(t % 2, t, scale, qkv_slots, grad_slots, sent)
            there.start(t)

        for when in range(pairs + LAG):
            todo = [
                (unit, level)
                for level in range(1, 6)
                for unit in range(units)
                if step_of(unit, level) == when
            ]
            if todo:

                @pl.when(t == when)
                def _(todo=todo):
                    for unit, level in todo:
                        plan.step(unit, level, sums)

        @pl.when(t >= LAG)
        def _():
            pair = t - LAG
            head = pl.ds(pl.multiple_of(pair * PAIR, PAIR), PAIR)
            there.arrive(pair)
            pair_weights(pair, (wq_ref, wk_ref, wv_ref), flat)

            def gather_home(owner, carry):
                per = tok // g.seq
                rhs[pl.ds(pl.multiple_of(owner * per, per), per), :] = home[pair, owner]
                return carry

            lax.fori_loop(0, g.seq, gather_home, 0)

            def unpermute(k, carry):
                start = k * ROWS
                rows = pl.ds(start, ROWS)
                made = move_rows(lambda i: token_rows(cols_ref, 2 * pair + i, start, ROWS), rhs)
                sums = [column_sum(value) for value in made]
                low = head_lanes(sums[0].shape)
                gvec_ref[0:1, head] += jnp.where(low, sums[0], sums[1])
                gvec_ref[2:3, head] += jnp.where(low, sums[1], sums[2])
                for part, value in enumerate(made):
                    local[rows, part * PAIR : (part + 1) * PAIR] = value.astype(BF16)
                total[rows, :] += dot_nt(local[rows, :], flat[...])
                return carry

            lax.fori_loop(0, tok // ROWS, unpermute, 0)

            def weights(k, carry):
                rows = pl.ds(pl.multiple_of(k * PART_ROWS, PART_ROWS), PART_ROWS)
                value = dot_tn(x_ref[:, rows], local[...])
                made = unpack(*(value[:, i * PAIR : (i + 1) * PAIR] for i in range(3)))
                for part, g_ref in enumerate((gq_ref, gk_ref, gv_ref)):
                    g_ref[rows, head] = made[part].astype(BF16)
                return carry

            lax.fori_loop(0, width // PART_ROWS, weights, 0)

        return carry

    lax.fori_loop(0, pairs + LAG, step, 0)
    gtok_ref[...] = total[...].astype(BF16)
    for when in range(pairs + LAG, step_of(units - 1, 5) + 1):
        for level in range(1, 6):
            for unit in range(units):
                if step_of(unit, level) == when:
                    plan.step(unit, level, sums)
    plan.sent()

    def close(pair, carry):
        there.sent(pair)
        return carry

    lax.fori_loop(0, pairs, close, 0)


def backward(g, scale, x, wq, wk, wv, d_mid, cols, terms, qkv, grad):
    tok, width = x.shape
    pairs = width // PAIR
    n = len(terms)
    shape = jax.ShapeDtypeStruct
    any_space, vmem = pl.BlockSpec(memory_space=pl.ANY), pl.BlockSpec(memory_space=pltpu.VMEM)
    dma = pltpu.SemaphoreType.DMA
    made = pl.pallas_call(
        functools.partial(backward_kernel, g, scale, n),
        out_shape=[
            shape((tok, width), BF16),
            *([shape((width, width), BF16)] * 3),
            shape((8, width), F32),
            *(shape(item.shape[-2:], F32) for item in terms),
        ],
        in_specs=[vmem] * (6 + n) + [any_space] * 2,
        out_specs=[vmem] * (5 + n),
        scratch_shapes=[
            pltpu.VMEM((2, *qkv.shape[1:]), BF16),
            pltpu.VMEM((2, *grad.shape[1:]), BF16),
            pltpu.VMEM(qkv.shape, BF16),
            pltpu.VMEM(qkv.shape, BF16),
            pltpu.VMEM((tok, 3 * PAIR), BF16),
            pltpu.VMEM((tok, 3 * PAIR), BF16),
            pltpu.VMEM((width, 3 * PAIR), BF16),
            pltpu.VMEM((tok, width), F32),
            *Scatter.scratch(g, [item.shape for item in terms], [Y_FIRST] * n),
            *exchange_sems(g, pairs),
            dma((2, 2)),
        ],
        compiler_params=pltpu.CompilerParams(
            collective_id=5, has_side_effects=True, vmem_limit_bytes=VMEM_LIMIT
        ),
        name="backward",
    )(x, wq, wk, wv, d_mid, cols, *terms, qkv, grad)
    return made[0], made[1:4], made[4], made[5 : 5 + n]


def small_lines(bias_ref, rows_ref, up_ref, stats_ref):
    width = bias_ref.shape[1]
    lines = up_ref.shape[1] // width
    stats = jnp.concatenate(
        [stats_ref[0:2, :], jnp.zeros((2, width - stats_ref.shape[1]), F32)], axis=1
    )
    return jnp.concatenate(
        [
            bias_ref[0:1, :],
            bias_ref[2:3, :],
            rows_ref[0:6, :],
            *(up_ref[0:1, i * width : (i + 1) * width] for i in range(lines)),
            stats,
            jnp.zeros((6 - lines, width), F32),
        ],
        axis=0,
    )


def own_lines(g, held, outs):
    width = held.shape[1]
    b, s = lax.axis_index("batch"), lax.axis_index("seq")
    here = b * g.seq + s
    vectors, (up_out, stats_out) = outs[:8], outs[8:]
    count, wide = vectors[0].shape[1], up_out.shape[1]
    lines = wide * g.n // width
    per_line = width // wide
    mine = pltpu.roll(held[...], (width - here * count) % width, 1)
    for i, out in enumerate(vectors):
        out[...] = mine[i : i + 1, :count]
    up = pltpu.roll(held[...], (width - here % per_line * wide) % width, 1)
    total = jnp.zeros((1, wide), F32)
    for i in range(lines):
        total += jnp.where(here // per_line == i, up[8 + i : 9 + i, :wide], 0.0)
    up_out[...] = total
    blocks = stats_out.shape[1]
    stats = pltpu.roll(held[...], (width - s * blocks) % width, 1)
    stats_out[...] = stats[8 + lines : 10 + lines, :blocks]


def close_kernel(g, n, bias_ref, rows_ref, up_ref, stats_ref, *refs):
    terms, gtok_ref, refs = refs[:n], refs[n], refs[n + 1 :]
    small_outs, sums, gtok_home, refs = refs[:10], refs[10 : 10 + n], refs[10 + n], refs[11 + n :]
    held, refs = refs[0], refs[1:]
    bufs, refs = refs[: 5 * n], refs[5 * n :]
    rs_send, rs_recv, small_bufs, refs = refs[0], refs[1], refs[2:7], refs[7:]
    small_send, small_recv, swap_send, swap_recv = refs
    greet(line_peers(g) + [swap_partner(g)])
    plan = Scatter(g, terms, bufs, TURNS, rs_send, rs_recv)
    swap = Swap(g, gtok_ref, gtok_home, swap_send, swap_recv)
    small = Total(g, held, small_bufs, small_send, small_recv)
    units = len(plan.units)
    for unit in range(units):
        plan.step(unit, 0)
    small.start(0, small_lines(bias_ref, rows_ref, up_ref, stats_ref))
    swap.start()
    for level in range(1, 6):
        for unit in range(units):
            plan.step(unit, level, sums)
        value = small.take(level - 1)
        if level < len(AXES):
            small.start(level, value)
        else:
            held[...] = value
            own_lines(g, held, small_outs)
    swap.wait()
    plan.sent()
    small.sent()


def close_call(g, small, sizes_out, terms, gtok):
    n = len(terms)
    lines = (16, small[0].shape[1])
    shape = jax.ShapeDtypeStruct
    any_space, vmem = pl.BlockSpec(memory_space=pl.ANY), pl.BlockSpec(memory_space=pltpu.VMEM)
    made = pl.pallas_call(
        functools.partial(close_kernel, g, n),
        out_shape=[
            *(shape(item, F32) for item in sizes_out),
            *(shape(item.shape[-2:], F32) for item in terms),
            shape(gtok.shape, BF16),
        ],
        in_specs=[vmem] * (5 + n),
        out_specs=[vmem] * (10 + n) + [any_space],
        scratch_shapes=[
            pltpu.VMEM(lines, F32),
            *Scatter.scratch(g, [item.shape for item in terms], TURNS),
            *Total.scratch(g, lines),
            *Swap.sems(),
        ],
        compiler_params=pltpu.CompilerParams(
            collective_id=6, has_side_effects=True, vmem_limit_bytes=VMEM_LIMIT
        ),
        name="close",
    )(*small, *terms, gtok)
    return made[:10], made[10:-1], made[-1]


def finish_kernel(n, *refs):
    ins, outs, sems = refs[:n], refs[n : 2 * n], refs[2 * n]
    copies = [
        pltpu.make_async_copy(src, dst, sems.at[k]) for k, (src, dst) in enumerate(zip(ins, outs))
    ]
    for copy in copies:
        copy.start()
    for copy in copies:
        copy.wait()


def finish(arrays):
    n = len(arrays)
    any_space = pl.BlockSpec(memory_space=pl.ANY)
    return pl.pallas_call(
        functools.partial(finish_kernel, n),
        out_shape=[jax.ShapeDtypeStruct(item.shape, item.dtype) for item in arrays],
        in_specs=[pl.BlockSpec(memory_space=pltpu.VMEM)] * n,
        out_specs=[any_space] * n,
        scratch_shapes=[pltpu.SemaphoreType.DMA((n,))],
        name="finish",
    )(*arrays)


def body(
    g,
    tokens,
    cluster_slot,
    loss_mask,
    out_grad,
    query_weight,
    key_weight,
    value_weight,
    output_weight,
    query_bias,
    value_bias,
    output_bias,
    first_gain,
    first_shift,
    up_weight,
    up_bias,
    down_weight,
    down_bias,
    second_gain,
    second_shift,
):
    tok, width = tokens.shape[1:]
    heads = cluster_slot.shape[1]
    pairs = heads // 2
    wide = up_weight.shape[1]
    per_owner = tok // g.seq
    scale = (width // heads) ** -0.5

    slots = cluster_slot[0]
    places = slots // tok * per_owner + slots % tok // g.seq
    table = jnp.concatenate(
        [places, loss_mask, jnp.zeros((16 - heads - 1, tok), jnp.int32)], axis=0
    )
    vectors = (
        query_bias,
        value_bias,
        output_bias,
        first_gain,
        first_shift,
        down_bias,
        second_gain,
        second_shift,
    )
    count = query_bias.shape[0]
    packed = jnp.pad(jnp.stack(vectors), ((0, 8), (0, PAIR - count))) + jnp.pad(
        up_bias[None], ((8, 7), (0, PAIR - up_bias.shape[0]))
    )
    gathered, partial, (work_x, work_table, work_mask) = open_call(
        g,
        [packed, query_weight, key_weight, value_weight],
        [output_weight, up_weight, down_weight],
        [tokens[0], table],
    )
    work_cols = work_table.T

    def whole(item):
        return item.reshape(g.n * item.shape[-2], item.shape[-1])

    wq, wk, wv = (whole(item) for item in gathered[1:])
    flat = gathered[0].reshape(g.n, 16, PAIR).astype(F32)
    rows = flat[:, :8, :count].transpose(1, 0, 2).reshape(8, width)
    up_row = flat[:, 8, : up_bias.shape[0]].reshape(1, wide)
    qkv_bias = jnp.stack([rows[0], jnp.zeros((width,), F32), rows[1]])

    spread, (qkv, attended, stats) = forward(
        g,
        scale,
        1.0 / (heads * CLUSTER * g.batch),
        work_x,
        wq,
        wk,
        wv,
        qkv_bias,
        work_table,
        work_cols,
        work_mask.reshape(1, tok, PAIR),
        partial,
    )
    wo, up, down = (whole(item) for item in spread)

    out, d_mid, routed, g_out, g_up, g_down, g_rows, g_upb = middle(
        g, work_x, attended, work_table, work_cols, wo, up, down, rows[2:], up_row, out_grad[0]
    )

    def parts(item):
        rows, cols = item.shape[0] // g.n, item.shape[1]
        if rows % 8:
            rows, cols = rows * cols // PAIR, PAIR
        return item.reshape(*(sizes(g)[axis] for axis in AXES), rows, cols)

    grad_tokens, g_attn, g_bias, s_ffn = backward(
        g,
        scale,
        work_x,
        wq,
        wk,
        wv,
        d_mid,
        work_cols,
        [parts(g_up), parts(g_out)],
        qkv,
        routed,
    )
    blocks = tok // CLUSTER
    small, s_attn, grad_tokens = close_call(
        g,
        [g_bias, g_rows, g_upb, stats],
        [(1, count)] * 8 + [(1, wide // g.n), (2, blocks)],
        [parts(item) for item in (*g_attn, g_down)],
        grad_tokens,
    )
    made = finish([out, grad_tokens, *small, *s_ffn, *s_attn])
    out, grad_tokens, small, sums = made[0], made[1], made[2:12], made[12:]
    s_up, s_out, s_query, s_key, s_value, s_down = (
        item.reshape(local.shape)
        for item, local in zip(
            sums,
            (up_weight, output_weight, query_weight, key_weight, value_weight, down_weight),
        )
    )
    gq, gv, go, gg1, gs1, gd, gg2, gs2, gu = (item.reshape(-1) for item in small[:9])
    return (
        out[None],
        grad_tokens[None],
        s_query,
        s_key,
        s_value,
        s_out,
        gq,
        gv,
        go,
        gg1,
        gs1,
        s_up,
        gu,
        s_down,
        gd,
        gg2,
        gs2,
        small[9],
    )


def solution(mesh):
    g = Grid(mesh)
    tokens, rows, flat = P("batch", "seq", None), P(("batch", "seq"), None), P(("batch", "seq"))
    return jax.shard_map(
        functools.partial(body, g),
        mesh=mesh,
        in_specs=(
            tokens,
            P("batch", None, "seq"),
            P("batch", "seq"),
            tokens,
            *([rows] * 4),
            *([flat] * 5),
            rows,
            flat,
            rows,
            *([flat] * 3),
        ),
        out_specs=(
            tokens,
            tokens,
            *([rows] * 4),
            *([flat] * 5),
            rows,
            flat,
            rows,
            *([flat] * 3),
            P(None, "seq"),
        ),
        check_vma=False,
    )
```

```python
import functools

import jax
import jax.numpy as jnp
from jax import lax
from jax.experimental import pallas as pl
from jax.experimental.pallas import tpu as pltpu
from jax.sharding import PartitionSpec as P

MESH = pl.DeviceIdType.MESH
F32 = jnp.float32
BF16 = jnp.bfloat16
EPSILON = 1e-12
CLUSTER = 128
PAIR = 128
Z = 4
VMEM_LIMIT = 58 * 1024 * 1024


class Grid:
    def __init__(self, mesh):
        self.batch, self.seq = mesh.shape["batch"], mesh.shape["seq"]
        self.Y, self.X = self.batch // 2, self.seq // Z
        self.half = self.seq // 2
        self.n = self.batch * self.seq


AXES = ("y", "c", "h", "l", "x")


def sizes(g):
    return {"y": g.Y, "c": 2, "h": 2, "l": Z // 2, "x": g.X}


def coords(g):
    b, s = lax.axis_index("batch"), lax.axis_index("seq")
    z = s // g.X
    return {"y": b // 2, "c": b % 2, "h": z // (Z // 2), "l": z % (Z // 2), "x": s % g.X}


def device(g, at):
    return (at["y"] * 2 + at["c"], (at["h"] * (Z // 2) + at["l"]) * g.X + at["x"])


def along(g, at, axis):
    size = sizes(g)[axis]
    places = [(at[axis] + k) % size for k in range(1, size)]
    return [(place, device(g, {**at, axis: place})) for place in places]


def group_place(g):
    b, s = lax.axis_index("batch"), lax.axis_index("seq")
    return b % 2 * g.half + s % g.half


def group_device(g, place):
    b, s = lax.axis_index("batch"), lax.axis_index("seq")
    return (b // 2 * 2 + place // g.half, s // g.half * g.half + place % g.half)


def line_peers(g, axes=AXES):
    at = coords(g)
    return [peer for axis in axes for _, peer in along(g, at, axis)]


def greet(peers):
    barrier = pltpu.get_barrier_semaphore()
    for peer in peers:
        pl.semaphore_signal(barrier, inc=1, device_id=peer, device_id_type=MESH)
    pl.semaphore_wait(barrier, len(peers))


def remote(src, dst, send, recv, peer):
    return pltpu.make_async_remote_copy(
        src_ref=src,
        dst_ref=dst,
        send_sem=send,
        recv_sem=recv,
        device_id=peer,
        device_id_type=MESH,
    )


def lane_pieces(shape):
    rows, cols = shape
    if cols % PAIR or rows * cols <= 24 * 768:
        return [(0, cols)]
    count = {3072: 4, 768: 3}.get(cols, 1)
    return [(k * (cols // count), cols // count) for k in range(count)]


class Gather:
    def __init__(self, g, ins, outs, dims, done, plan, sends, recvs, local_sem):
        self.g, self.ins, self.outs, self.dims, self.done = g, ins, outs, dims, done
        self.plan = plan
        self.sends, self.recvs, self.local_sem = sends, recvs, local_sem
        self.at = coords(g)
        self.units = [
            (index, pl.ds(start, size))
            for index, item in enumerate(ins)
            for start, size in lane_pieces(item.shape[-2:])
        ]

    @staticmethod
    def sems(g, shapes):
        units = sum(len(lane_pieces(shape[-2:])) for shape in shapes)
        slots = units * sum(sizes(g).values())
        dma = pltpu.SemaphoreType.DMA
        return [dma((slots,)), dma((slots,)), dma((units,))]

    def source(self, unit):
        index, cols = self.units[unit]
        return self.ins[index].at[(*([slice(None)] * (len(self.ins[index].shape) - 1)), cols)]

    def view(self, unit, done):
        index, cols = self.units[unit]
        spot = tuple(slice(None) if axis in done else self.at[axis] for axis in self.dims)
        return self.outs[index].at[(*spot, slice(None), cols)]

    def own(self, unit):
        return pltpu.make_async_copy(
            self.source(unit), self.view(unit, self.done), self.local_sem.at[unit]
        )

    def levels(self, unit):
        return self.plan(unit)

    def moves(self, unit, level):
        g = self.g
        axes = self.levels(unit)
        view = self.view(unit, (*self.done, *axes[:level]))
        src = self.source(unit) if level == 0 else view
        size = sizes(g)
        base = unit * sum(size.values())
        for axis in AXES[: AXES.index(axes[level])]:
            base += size[axis]
        return [
            remote(src, view, self.sends.at[base + k], self.recvs.at[base + k], peer)
            for k, (_, peer) in enumerate(along(g, self.at, axes[level]))
        ]

    def start(self, unit, level):
        if level == 0:
            self.own(unit).start()
        else:
            if level == 1:
                self.own(unit).wait()
            for copy in self.moves(unit, level - 1):
                copy.wait_recv()
        for copy in self.moves(unit, level):
            copy.start()

    def finish(self):
        count = len(self.units)
        for unit in range(count):
            for copy in self.moves(unit, len(self.levels(unit)) - 1):
                copy.wait_recv()
        for unit in range(count):
            for level in range(len(self.levels(unit))):
                for copy in self.moves(unit, level):
                    copy.wait_send()


class Swap:
    def __init__(self, g, src, dst, sends, recvs, pieces=1):
        b, s = lax.axis_index("batch"), lax.axis_index("seq")
        self.native = b % 2 == s // g.half
        self.peer = swap_partner(g)
        self.ends = (src, dst, sends, recvs)
        self.pieces = pieces

    @staticmethod
    def sems(pieces=1):
        return [pltpu.SemaphoreType.DMA((pieces,)), pltpu.SemaphoreType.DMA((pieces,))]

    def piece(self, k):
        src, dst, sends, recvs = self.ends
        size = src.shape[0] // self.pieces
        rows = pl.ds(pl.multiple_of(k * size, size), size)
        return src.at[rows], dst.at[rows], sends.at[k], recvs.at[k]

    def start(self, k=0):
        src, dst, send, recv = self.piece(k)

        @pl.when(self.native)
        def _():
            pltpu.make_async_copy(src, dst, recv).start()

        @pl.when(jnp.logical_not(self.native))
        def _():
            remote(src, dst, send, recv, self.peer).start()

    def wait(self):
        for k in range(self.pieces):
            self.wait_piece(k)

    def wait_piece(self, k):
        src, dst, send, recv = self.piece(k)

        @pl.when(self.native)
        def _():
            pltpu.make_async_copy(src, dst, recv).wait()

        @pl.when(jnp.logical_not(self.native))
        def _():
            remote(src, dst, send, recv, self.peer).wait()


def swap_partner(g):
    b, s = lax.axis_index("batch"), lax.axis_index("seq")
    return (b // 2 * 2 + 1 - b % 2, (s + g.half) % g.seq)


PART = ("h", "l", "x")
PIECES, WINDOW = 16, 2


MASK_AT = 4


def masks_in_order(heads, table_ref, block, size, out_ref):
    tok = table_ref.shape[1]
    start = block * size
    rows = lax.broadcasted_iota(jnp.int32, (size, tok), 0) + start
    lanes = lax.broadcasted_iota(jnp.int32, (size, PAIR), 1)
    mask = table_ref[heads : heads + 1, :] > 0
    made = jnp.zeros((size, PAIR), F32)
    for head in range(heads):
        places = jnp.where(mask, table_ref[head : head + 1, :], -1)
        found = jnp.sum(jnp.where(rows == places, 1.0, 0.0), axis=1, keepdims=True)
        made = jnp.where(lanes == head, found, made)
    out_ref[start : start + size, :] = made.astype(BF16)


def open_kernel(g, n, m, *refs):
    ins, refs = refs[: n + m], refs[n + m :]
    swap_in, refs = refs[:2], refs[2:]
    outs, refs = refs[: n + m], refs[n + m :]
    swap_out, mask_ref, sems = refs[:2], refs[2], refs[3:]
    greet(line_peers(g) + [swap_partner(g)])
    whole = Gather(
        g,
        ins[:n],
        outs[:n],
        AXES,
        (),
        lambda unit: ("h", "l", "x", "y", "c"),
        *sems[:3],
    )
    part = Gather(g, ins[n:], outs[n:], PART, (), lambda unit: PART, *sems[3:6])
    tokens = Swap(g, swap_in[0], swap_out[0], *sems[6:8], PIECES)
    table = Swap(g, swap_in[1], swap_out[1], *sems[8:10])
    plans = [(whole, unit) for unit in range(len(whole.units))]
    plans += [(part, unit) for unit in range(len(part.units))]
    table.start()
    tok, width = swap_in[0].shape
    heads, blocks = width * 2 // PAIR, 8
    for t in range(len(plans) + 4 * WINDOW):
        for level in range(5):
            k = t - level * WINDOW
            if 0 <= k < len(plans):
                plan, unit = plans[k]
                if level < len(plan.levels(unit)):
                    plan.start(unit, level)
        if t < PIECES:
            tokens.start(t)
        if t == MASK_AT:
            table.wait()
        if 0 <= t - MASK_AT < blocks:
            masks_in_order(heads, swap_out[1], t - MASK_AT, tok // blocks, mask_ref)
    whole.finish()
    part.finish()
    tokens.wait()


def open_call(g, whole, part, swapped):
    any_space = pl.BlockSpec(memory_space=pl.ANY)
    shape = jax.ShapeDtypeStruct
    size = sizes(g)
    n, m = len(whole), len(part)
    outs = [
        *(shape((*(size[axis] for axis in AXES), *item.shape), item.dtype) for item in whole),
        *(shape((*(size[axis] for axis in PART), *item.shape), item.dtype) for item in part),
        *(shape(item.shape, item.dtype) for item in swapped),
    ]
    vmem = pl.BlockSpec(memory_space=pltpu.VMEM)
    made = pl.pallas_call(
        functools.partial(open_kernel, g, n, m),
        out_shape=[*outs, shape((swapped[0].shape[0], PAIR), BF16)],
        in_specs=[vmem] * (n + m) + [any_space, vmem],
        out_specs=[any_space] * (n + m) + [vmem] * 3,
        scratch_shapes=[
            *Gather.sems(g, [item.shape for item in whole]),
            *Gather.sems(g, [item.shape for item in part]),
            *Swap.sems(PIECES),
            *Swap.sems(),
        ],
        compiler_params=pltpu.CompilerParams(
            collective_id=0, has_side_effects=True, vmem_limit_bytes=VMEM_LIMIT
        ),
        name="open",
    )(*whole, *part, *swapped)
    return made[:n], made[n : n + m], made[n + m :]


class Scatter:
    def __init__(self, g, ins, bufs, plans, sends, recvs):
        self.g, self.ins, self.bufs, self.plans = g, ins, bufs, plans
        self.sends, self.recvs = sends, recvs
        self.at = coords(g)
        self.units = [
            (index, pl.ds(start, size))
            for index, item in enumerate(ins)
            for start, size in lane_pieces(item.shape[-2:])
        ]

    @staticmethod
    def scratch(g, shapes, plans):
        size = sizes(g)
        made = []
        for shape, plan in zip(shapes, plans):
            left = list(AXES)
            for axis in plan:
                left.remove(axis)
                lead = (size[axis] - 1, *(size[other] for other in left))
                made.append(pltpu.VMEM((*lead, *shape[-2:]), BF16))
        units = sum(len(lane_pieces(shape[-2:])) for shape in shapes)
        slots = units * sum(size.values())
        return [*made, pltpu.SemaphoreType.DMA((slots,)), pltpu.SemaphoreType.DMA((slots,))]

    def held(self, index, level):
        return self.bufs[index * len(AXES) + level]

    def store(self, index, level):
        if level == 0:
            return self.ins[index], AXES
        left = tuple(axis for axis in AXES if axis not in self.plans[index][:level])
        return self.held(index, level - 1).at[0], left

    def moves(self, unit, level):
        g = self.g
        index, cols = self.units[unit]
        axis = self.plans[index][level]
        src, left = self.store(index, level)
        held = self.held(index, level)
        size = sizes(g)
        base = unit * sum(size.values())
        for other in AXES[: AXES.index(axis)]:
            base += size[other]
        a = slice(None)
        rest = (a,) * len(left)
        made = []
        for k, (place, peer) in enumerate(along(g, self.at, axis)):
            spot = tuple(place if other == axis else a for other in left)
            made.append(
                remote(
                    src.at[(*spot, a, cols)],
                    held.at[(k, *rest, cols)],
                    self.sends.at[base + k],
                    self.recvs.at[base + k],
                    peer,
                )
            )
        return made

    def add(self, unit, level, out=None):
        g = self.g
        index, cols = self.units[unit]
        axis = self.plans[index][level]
        src, left = self.store(index, level)
        held = self.held(index, level)
        size = sizes(g)
        rest = [other for other in left if other != axis]
        loop = [other for other in rest if other in ("h", "l")]
        count = 1
        for other in loop:
            count *= size[other]
        static = [other for other in rest if other not in loop]
        a = slice(None)

        def some(step, carry):
            spots = [{}]
            for other in static:
                spots = [{**spot, other: k} for spot in spots for k in range(size[other])]
            for spot in spots:
                if len(loop) == 2:
                    spot = {**spot, "h": step // size["l"], "l": step % size["l"]}
                elif loop:
                    spot = {**spot, loop[0]: step}
                where = tuple(spot[other] for other in rest)
                mine = tuple(self.at[axis] if other == axis else spot[other] for other in left)
                total = src[(*mine, a, cols)].astype(F32)
                for k in range(size[axis] - 1):
                    total += held[(k, *where, a, cols)].astype(F32)
                if out is None:
                    held[(0, *where, a, cols)] = total.astype(BF16)
                else:
                    out[(*where, a, cols)] = total.astype(out.dtype)
            return carry

        lax.fori_loop(0, count, some, 0)

    def step(self, unit, level, out=None):
        if level:
            for copy in self.moves(unit, level - 1):
                copy.wait_recv()
            last = level == len(AXES)
            self.add(unit, level - 1, out[self.units[unit][0]] if last else None)
        if level < len(AXES):
            for copy in self.moves(unit, level):
                copy.start()

    def sent(self):
        for unit in range(len(self.units)):
            for level in range(len(AXES)):
                for copy in self.moves(unit, level):
                    copy.wait_send()


class Total:
    def __init__(self, g, held, bufs, sends, recvs):
        self.g, self.held, self.bufs = g, held, bufs
        self.sends, self.recvs = sends, recvs
        self.at = coords(g)

    @staticmethod
    def scratch(g, shape):
        slots = sum(sizes(g).values())
        return [
            *(pltpu.VMEM((sizes(g)[axis], *shape), F32) for axis in AXES),
            pltpu.SemaphoreType.DMA((slots,)),
            pltpu.SemaphoreType.DMA((slots,)),
        ]

    def moves(self, level):
        g = self.g
        axis = AXES[level]
        view = self.bufs[level].at[self.at[axis]]
        base = sum(sizes(g)[other] for other in AXES[:level])
        return [
            remote(view, view, self.sends.at[base + k], self.recvs.at[base + k], peer)
            for k, (_, peer) in enumerate(along(g, self.at, axis))
        ]

    def start(self, level, value):
        self.bufs[level][self.at[AXES[level]]] = value
        for copy in self.moves(level):
            copy.start()

    def take(self, level):
        for copy in self.moves(level):
            copy.wait_recv()
        buf = self.bufs[level]
        total = buf[0]
        for k in range(1, buf.shape[0]):
            total = total + buf[k]
        return total

    def sent(self):
        for level in range(len(AXES)):
            for copy in self.moves(level):
                copy.wait_send()


def dot(left, right):
    return lax.dot_general(left, right, (((1,), (0,)), ((), ())), preferred_element_type=F32)


def dot_nt(left, right):
    return lax.dot_general(left, right, (((1,), (1,)), ((), ())), preferred_element_type=F32)


def dot_tn(left, right):
    return lax.dot_general(left, right, (((0,), (0,)), ((), ())), preferred_element_type=F32)


def head_lanes(shape):
    return lax.broadcasted_iota(jnp.int32, shape, 1) < PAIR // 2


def split_pair(value, axis=0):
    low = head_lanes(value.shape)
    zero = jnp.zeros_like(value)
    return jnp.concatenate(
        [jnp.where(low, value, zero), jnp.where(low, zero, value)], axis=axis
    )


def swap_halves(value):
    return pltpu.roll(value.astype(F32), PAIR // 2, 1).astype(value.dtype)


def pack(q, k, v):
    low = head_lanes(q.shape)
    k = swap_halves(k)
    return jnp.where(low, q, k), jnp.where(low, v, q), jnp.where(low, k, v)


def unpack(first, second, third):
    low = head_lanes(first.shape)
    return (
        jnp.where(low, first, second),
        swap_halves(jnp.where(low, third, first)),
        jnp.where(low, second, third),
    )


def place_rows(places_ref, head, start, size):
    tok = places_ref.shape[1]
    rows = lax.broadcasted_iota(jnp.int32, (size, tok), 0) + start
    return (rows == places_ref[pl.ds(head, 1), :]).astype(F32).astype(BF16)


def token_rows(cols_ref, head, start, size):
    tok, width = cols_ref.shape
    lanes = lax.broadcasted_iota(jnp.int32, (size, tok), 1)
    heads = lax.broadcasted_iota(jnp.int32, (size, width), 1)
    table = cols_ref[pl.ds(start, size), :].astype(F32)
    place = jnp.sum(jnp.where(heads == head, table, 0.0), axis=1, keepdims=True)
    return (lanes == place.astype(jnp.int32)).astype(F32).astype(BF16)


def move_rows(pick, value_ref):
    one = dot(pick(0), value_ref[:, : 2 * PAIR])
    two = dot(pick(1), value_ref[:, PAIR:])
    low = head_lanes((one.shape[0], PAIR))
    return one[:, :PAIR], jnp.where(low, one[:, PAIR:], two[:, :PAIR]), two[:, PAIR:]


def move_pair(pick, value):
    one, two = dot(pick(0), value), dot(pick(1), value)
    return jnp.where(head_lanes(one.shape), one, two)


def gather_rows(block_ref, lead, start, size, lanes):
    part = block_ref[(*lead, slice(None), pl.ds(start, size), lanes)]
    if size % 16:
        part = part.astype(F32)
    return part.reshape(part.shape[0] * size, part.shape[2]).astype(block_ref.dtype)


def spread_rows(value, sources, kind):
    size = value.shape[0] // sources
    if size % 16:
        return value.astype(F32).reshape(sources, size, value.shape[1]).astype(kind)
    return value.astype(kind).reshape(sources, size, value.shape[1])


ROWS = 1024


def pair_weights(pair, w_refs, out_ref):
    head = pl.ds(pl.multiple_of(pair * PAIR, PAIR), PAIR)
    for part, value in enumerate(pack(*(w_ref[:, head] for w_ref in w_refs))):
        out_ref[:, part * PAIR : (part + 1) * PAIR] = value


def project_pair(pair, x_ref, w_refs, bias_ref, places_ref, flat, rhs, out_ref):
    tok = x_ref.shape[0]
    head = pl.ds(pl.multiple_of(pair * PAIR, PAIR), PAIR)
    pair_weights(pair, w_refs, flat)
    bias = jnp.concatenate(
        pack(*(jnp.broadcast_to(bias_ref[i : i + 1, head], (8, PAIR)) for i in range(3))), axis=1
    )[0:1]

    def project(step, carry):
        rows = pl.ds(step * ROWS, ROWS)
        rhs[rows, :] = (dot(x_ref[rows, :], flat[...]) + bias).astype(BF16)
        return carry

    lax.fori_loop(0, tok // ROWS, project, 0)

    def permute(step, carry):
        start = step * ROWS
        made = move_rows(lambda i: place_rows(places_ref, 2 * pair + i, start, ROWS), rhs)
        for part, value in enumerate(made):
            out_ref[pair, pl.ds(start, ROWS), part * PAIR : (part + 1) * PAIR] = value.astype(BF16)
        return carry

    lax.fori_loop(0, tok // ROWS, permute, 0)


def attend_pair(pair, scale, qkv_ref, out_ref, entropy_ref):
    _, sources, per_owner, _ = qkv_ref.shape
    size = CLUSTER // sources
    clusters = per_owner // size
    lanes = lax.broadcasted_iota(jnp.int32, (CLUSTER, PAIR), 1)
    for cluster in range(clusters):
        q, k, v = unpack(
            *(
                gather_rows(qkv_ref, (pair,), cluster * size, size, slice(i * PAIR, (i + 1) * PAIR))
                for i in range(3)
            )
        )
        scores = cluster_scores(split_pair(q), k, scale)
        top = jnp.max(scores, axis=1, keepdims=True)
        weights = jnp.exp(scores - top)
        totals = jnp.sum(weights, axis=1, keepdims=True)
        probs = weights / totals
        entropy = top + jnp.log(totals) - jnp.sum(probs * scores, axis=1, keepdims=True)
        low = probs.astype(BF16)
        mixed = dot(
            jnp.concatenate([low[:CLUSTER], low[CLUSTER:]], axis=1), split_pair(v)
        )
        out_ref[pair, :, cluster * size : (cluster + 1) * size, :] = spread_rows(
            mixed, sources, BF16
        )
        entropy_ref[cluster] = jnp.where(
            lanes == 2 * pair,
            entropy[:CLUSTER],
            jnp.where(lanes == 2 * pair + 1, entropy[CLUSTER:], entropy_ref[cluster]),
        )


class Exchange:
    def __init__(self, g, kind, src, dst, sends, recvs, local_sem):
        self.g, self.kind, self.src, self.dst = g, kind, src, dst
        self.sends, self.recvs, self.local_sem = sends, recvs, local_sem
        b, s = lax.axis_index("batch"), lax.axis_index("seq")
        self.b, self.s = b, s
        self.me = s if kind == "work" else group_place(g)
        self.native = b % 2 == s // g.half

    def target(self, place):
        g, b, s = self.g, self.b, self.s
        if self.kind == "home":
            return (b // 2 * 2 + s // g.half, place)
        if self.kind == "work":
            return (b // 2 * 2 + place // g.half, b % 2 * g.half + place % g.half)
        return group_device(g, place)

    @staticmethod
    def senders(g, kind):
        b, s = lax.axis_index("batch"), lax.axis_index("seq")
        if kind == "home":
            places = [(s + k) % g.seq for k in range(1, g.seq)]
            return [
                (b // 2 * 2 + place // g.half, b % 2 * g.half + place % g.half) for place in places
            ]
        places = [(group_place(g) + k) % g.seq for k in range(1, g.seq)]
        if kind == "work":
            return [(b // 2 * 2 + s // g.half, place) for place in places]
        return [group_device(g, place) for place in places]

    def block(self, pair, peer):
        if len(self.src.shape) == 4:
            return self.src.at[pair, peer]
        per = self.src.shape[1] // self.g.seq
        return self.src.at[pair, pl.ds(pl.multiple_of(peer * per, per), per), :]

    def own(self, pair):
        return pltpu.make_async_copy(
            self.block(pair, self.me), self.dst.at[pair, self.me], self.local_sem.at[pair]
        )

    def crossing(self, pair):
        return remote(
            self.block(pair, self.me),
            self.dst.at[pair, self.me],
            self.sends.at[pair, self.g.seq - 1],
            self.local_sem.at[pair],
            swap_partner(self.g),
        )

    def moves(self, pair):
        g = self.g
        made = []
        for k in range(1, g.seq):
            peer = (self.me + k) % g.seq
            made.append(
                remote(
                    self.block(pair, peer),
                    self.dst.at[pair, self.me],
                    self.sends.at[pair, k - 1],
                    self.recvs.at[pair, k - 1],
                    self.target(peer),
                )
            )
        return made

    def either(self, here, there):
        if self.kind == "group":
            here()
            return
        pl.when(self.native)(here)
        pl.when(jnp.logical_not(self.native))(there)

    def start(self, pair):
        self.either(lambda: self.own(pair).start(), lambda: self.crossing(pair).start())
        for copy in self.moves(pair):
            copy.start()

    def arrive(self, pair):
        self.either(lambda: self.own(pair).wait(), lambda: self.crossing(pair).wait_recv())
        for copy in self.moves(pair):
            copy.wait_recv()

    def sent(self, pair):
        self.either(lambda: None, lambda: self.crossing(pair).wait_send())
        for copy in self.moves(pair):
            copy.wait_send()


def exchange_sems(g, pairs):
    return [
        pltpu.SemaphoreType.DMA((pairs, g.seq)),
        pltpu.SemaphoreType.DMA((pairs, g.seq)),
        pltpu.SemaphoreType.DMA((pairs,)),
    ]


LAG = 2
BACK = 2


def unpermute_pair(pair, cols_ref, ret_ref, out_ref):
    tok = out_ref.shape[0]
    head = pl.ds(pl.multiple_of(pair * PAIR, PAIR), PAIR)

    def pick(step, carry):
        start = step * ROWS
        value = ret_ref[pair].reshape(tok, PAIR)
        out_ref[pl.ds(start, ROWS), head] = move_pair(
            lambda i: token_rows(cols_ref, 2 * pair + i, start, ROWS), value
        ).astype(BF16)
        return carry

    lax.fori_loop(0, tok // ROWS, pick, 0)


def forward_kernel(
    g,
    scale,
    factor,
    x_ref,
    wq_ref,
    wk_ref,
    wv_ref,
    bias_ref,
    places_ref,
    cols_ref,
    mask_sent,
    *refs,
):
    parts, wholes = refs[:3], refs[3:6]
    qkv_out, attended_ref, stats_ref = refs[6:9]
    flat, rhs, sent, routed, mixed, ret, mask_routed, entropy = refs[9:17]
    sems = refs[17:]
    pairs = sent.shape[0]
    greet(line_peers(g, ("y", "c")) + Exchange.senders(g, "group"))
    plan = Gather(g, parts, wholes, AXES, PART, lambda unit: ("y", "c"), *sems[:3])
    there = Exchange(g, "group", sent, routed, *sems[3:6])
    back = Exchange(g, "group", mixed, ret, *sems[6:9])
    masks = Exchange(g, "group", mask_sent, mask_routed, *sems[9:12])
    save_sem = sems[12]
    units = len(plan.units)

    def keep(pair):
        return pltpu.make_async_copy(routed.at[pair], qkv_out.at[pair], save_sem.at[pair])

    masks.start(0)
    entropy[...] = jnp.zeros_like(entropy)
    steps = pairs + LAG + BACK

    def step(t, carry):
        @pl.when(t < pairs)
        def _():
            project_pair(
                t,
                x_ref,
                (wq_ref, wk_ref, wv_ref),
                bias_ref,
                places_ref,
                flat,
                rhs,
                sent,
            )
            there.start(t)

        for when in range(steps):
            todo = [
                (unit, level)
                for level in (1, 0)
                for unit in range(units)
                if min(unit + level * WINDOW, steps - 1) == when
            ]
            if todo:

                @pl.when(t == when)
                def _(todo=todo):
                    for unit, level in todo:
                        plan.start(unit, level)

        @pl.when((t >= LAG) & (t < pairs + LAG))
        def _():
            pair = t - LAG
            there.arrive(pair)
            keep(pair).start()
            attend_pair(pair, scale, routed, mixed, entropy)
            back.start(pair)

        @pl.when(t >= LAG + BACK)
        def _():
            pair = t - LAG - BACK
            back.arrive(pair)
            unpermute_pair(pair, cols_ref, ret, attended_ref)

        return carry

    lax.fori_loop(0, steps, step, 0)

    masks.arrive(0)
    sources, per_owner = mask_routed.shape[1:3]
    size = CLUSTER // sources
    blocks = per_owner // size
    spot = lax.broadcasted_iota(jnp.int32, stats_ref.shape, 1) - group_place(g) * blocks
    row = lax.broadcasted_iota(jnp.int32, stats_ref.shape, 0)
    stats = jnp.zeros(stats_ref.shape, F32)
    for cluster in range(blocks):
        mask = gather_rows(mask_routed, (0,), cluster * size, size, slice(None)).astype(F32)
        entropy_sum = jnp.sum(entropy[cluster] * mask) * factor
        count = jnp.sum(mask) * factor
        stats += jnp.where(
            spot == cluster, jnp.where(row == 0, entropy_sum, jnp.where(row == 1, count, 0.0)), 0.0
        )
    stats_ref[...] = stats
    plan.finish()

    def close(pair, carry):
        keep(pair).wait()
        there.sent(pair)
        back.sent(pair)
        return carry

    lax.fori_loop(0, pairs, close, 0)
    masks.sent(0)


def forward(g, scale, factor, x, wq, wk, wv, bias, places, cols, mask, parts):
    tok, width = x.shape
    pairs = width // PAIR
    per_owner = tok // g.seq
    clusters = tok // CLUSTER
    shape = jax.ShapeDtypeStruct
    any_space, vmem = pl.BlockSpec(memory_space=pl.ANY), pl.BlockSpec(memory_space=pltpu.VMEM)
    lead = tuple(sizes(g)[axis] for axis in AXES)
    made = pl.pallas_call(
        functools.partial(forward_kernel, g, scale, factor),
        out_shape=[
            *(shape((*lead, *item.shape[-2:]), BF16) for item in parts),
            shape((pairs, g.seq, per_owner, 3 * PAIR), BF16),
            shape((tok, width), BF16),
            shape((8, PAIR), F32),
        ],
        in_specs=[vmem] * 11,
        out_specs=[any_space] * 4 + [vmem, vmem],
        scratch_shapes=[
            pltpu.VMEM((width, 3 * PAIR), BF16),
            pltpu.VMEM((tok, 3 * PAIR), BF16),
            pltpu.VMEM((pairs, tok, 3 * PAIR), BF16),
            pltpu.VMEM((pairs, g.seq, per_owner, 3 * PAIR), BF16),
            pltpu.VMEM((pairs, g.seq, per_owner, PAIR), BF16),
            pltpu.VMEM((pairs, g.seq, per_owner, PAIR), BF16),
            pltpu.VMEM((1, g.seq, per_owner, PAIR), BF16),
            pltpu.VMEM((clusters, CLUSTER, PAIR), F32),
            *Gather.sems(g, [item.shape for item in parts]),
            *exchange_sems(g, pairs),
            *exchange_sems(g, pairs),
            *exchange_sems(g, 1),
            pltpu.SemaphoreType.DMA((pairs,)),
        ],
        compiler_params=pltpu.CompilerParams(
            collective_id=2, has_side_effects=True, vmem_limit_bytes=VMEM_LIMIT
        ),
        name="forward",
    )(x, wq, wk, wv, bias, places, cols, mask, *parts)
    return made[:3], made[3:]


def cluster_scores(q, k, scale):
    return dot_nt(q, k) * scale


def attend_back_pair(slot, pair, scale, qkv_ref, grad_ref, out_ref):
    _, sources, per_owner, _ = qkv_ref.shape
    size = CLUSTER // sources
    clusters = per_owner // size
    for cluster in range(clusters):
        q, k, v = unpack(
            *(
                gather_rows(qkv_ref, (slot,), cluster * size, size, slice(i * PAIR, (i + 1) * PAIR))
                for i in range(3)
            )
        )
        grad = gather_rows(grad_ref, (slot,), cluster * size, size, slice(None))
        q2, g2 = split_pair(q), split_pair(grad)
        scores = cluster_scores(q2, k, scale)
        top = jnp.max(scores, axis=1, keepdims=True)
        weights = jnp.exp(scores - top)
        probs = weights / jnp.sum(weights, axis=1, keepdims=True)
        low = probs.astype(BF16)
        d_value = dot_tn(low, g2)
        d_prob = dot_nt(g2, v)
        inner = jnp.sum(probs * d_prob, axis=1, keepdims=True)
        d_score = (probs * (d_prob - inner)).astype(BF16)
        d_query = (
            dot(jnp.concatenate([d_score[:CLUSTER], d_score[CLUSTER:]], axis=1), split_pair(k))
            * scale
        )
        d_key = dot_tn(d_score, q2) * scale
        for i, value in enumerate(pack(d_query, d_key, d_value)):
            out_ref[
                pair, :, cluster * size : (cluster + 1) * size, i * PAIR : (i + 1) * PAIR
            ] = spread_rows(value, sources, BF16)


INV_SQRT2 = 0.7071067811865476
INV_SQRT_2PI = 0.3989422804014327


def norm_parts(value):
    centred = value - jnp.mean(value, axis=1, keepdims=True)
    rate = lax.rsqrt(jnp.mean(centred * centred, axis=1, keepdims=True) + EPSILON)
    return centred * rate, rate


def norm_back(grad, gain, normed, rate):
    inner = grad * gain
    return rate * (
        inner
        - jnp.mean(inner, axis=1, keepdims=True)
        - normed * jnp.mean(inner * normed, axis=1, keepdims=True)
    )


TILE = 512
COLS = 512
PART_ROWS = 256


def column_sum(value):
    return jnp.sum(value, axis=0, keepdims=True)


def middle_forward(x_ref, attended, w_refs, vec_ref, up_bias_ref, out_ref, kept):
    wo_ref, up_ref, down_ref = w_refs
    hidden_all, act_all, dup_all, n1_all, n2_all, r1_all, r2_all = kept
    tok, width = x_ref.shape
    wide = up_ref.shape[1]
    bo, g1, s1, bd, g2, s2 = (vec_ref[i : i + 1, :] for i in range(6))

    def tile(step, carry):
        rows = pl.ds(step * TILE, TILE)
        branch = dot(attended[rows, :], wo_ref[...]) + bo
        n1, r1 = norm_parts(x_ref[rows, :].astype(F32) + branch)
        n1_all[rows, :] = n1
        r1_all[rows, :] = r1
        hidden = (n1 * g1 + s1).astype(BF16)
        hidden_all[rows, :] = hidden
        ffn = hidden.astype(F32) + bd
        for col in range(0, wide, COLS):
            to = slice(col, col + COLS)
            pre = dot(hidden, up_ref[:, to]) + up_bias_ref[0:1, to]
            cdf = 0.5 * (1.0 + lax.erf(pre * INV_SQRT2))
            act = (pre * cdf).astype(BF16)
            dup_all[rows, to] = (cdf + pre * (jnp.exp(-0.5 * pre * pre) * INV_SQRT_2PI)).astype(BF16)
            act_all[rows, to] = act
            ffn += dot(act, down_ref[to, :])
        n2, r2 = norm_parts(ffn)
        n2_all[rows, :] = n2
        r2_all[rows, :] = r2
        out_ref[rows, :] = (n2 * g2 + s2).astype(BF16)
        return carry

    lax.fori_loop(0, tok // TILE, tile, 0)


def middle_backward(grad_ref, cols_ref, heads, w_refs, vec_ref, kept, made):
    wo_ref, up_ref, down_ref = w_refs
    hidden_all, act_all, dup_all, n1_all, n2_all, r1_all, r2_all = kept
    dffn_all, dmid_ref, datt_all, gvec_ref, g_upb_ref = made
    tok, width = dmid_ref.shape
    wide = up_ref.shape[1]
    gvec_ref[...] = jnp.zeros_like(gvec_ref)
    g_upb_ref[...] = jnp.zeros_like(g_upb_ref)
    g1, g2 = vec_ref[1:2, :], vec_ref[4:5, :]

    def tile(step, carry):
        rows = pl.ds(step * TILE, TILE)
        mask = cols_ref[rows, heads : heads + 1].astype(F32)
        gout = grad_ref[rows, :].astype(F32) * mask
        n2 = n2_all[rows, :]
        gvec_ref[4:5, :] += column_sum(gout * n2)
        gvec_ref[5:6, :] += column_sum(gout)
        d_pre = norm_back(gout, g2, n2, r2_all[rows, :])
        d_ffn = d_pre.astype(BF16)
        dffn_all[rows, :] = d_ffn
        gvec_ref[3:4, :] += column_sum(d_ffn.astype(F32))
        d_hidden = d_pre
        for col in range(0, wide, COLS):
            to = slice(col, col + COLS)
            d_up = (dot_nt(d_ffn, down_ref[to, :]) * dup_all[rows, to].astype(F32)).astype(BF16)
            dup_all[rows, to] = d_up
            g_upb_ref[0:1, to] += column_sum(d_up.astype(F32))
            d_hidden += dot_nt(d_up, up_ref[:, to])
        n1 = n1_all[rows, :]
        gvec_ref[1:2, :] += column_sum(d_hidden * n1)
        gvec_ref[2:3, :] += column_sum(d_hidden)
        d_mid = norm_back(d_hidden, g1, n1, r1_all[rows, :])
        d_branch = d_mid.astype(BF16)
        dmid_ref[rows, :] = d_branch
        gvec_ref[0:1, :] += column_sum(d_branch.astype(F32))
        datt_all[rows, :] = dot_nt(d_branch, wo_ref[...]).astype(BF16)
        return carry

    lax.fori_loop(0, tok // TILE, tile, 0)


def permute_pair(pair, places_ref, datt_all, out_ref):
    tok = datt_all.shape[0]
    to = slice(pair * PAIR, (pair + 1) * PAIR)

    def permute(step, carry):
        start = step * ROWS
        out_ref[pair, pl.ds(start, ROWS), :] = move_pair(
            lambda i: place_rows(places_ref, 2 * pair + i, start, ROWS), datt_all[:, to]
        ).astype(BF16)
        return carry

    lax.fori_loop(0, tok // ROWS, permute, 0)


def middle_weights(attended, dmid_ref, kept, dffn_all, grads):
    hidden_all, act_all, dup_all = kept[:3]
    g_out_ref, g_up_ref, g_down_ref = grads
    wide, width = act_all.shape[1], hidden_all.shape[1]

    def weights(step, carry):
        to = pl.ds(pl.multiple_of(step * PART_ROWS, PART_ROWS), PART_ROWS)
        g_down_ref[to, :] = dot_tn(act_all[:, to], dffn_all[...]).astype(BF16)
        g_up_ref[:, to] = dot_tn(hidden_all[...], dup_all[:, to]).astype(BF16)
        return carry

    lax.fori_loop(0, wide // PART_ROWS, weights, 0)

    def out_weights(step, carry):
        to = pl.ds(pl.multiple_of(step * PART_ROWS, PART_ROWS), PART_ROWS)
        g_out_ref[:, to] = dot_tn(attended[...], dmid_ref[:, to]).astype(BF16)
        return carry

    lax.fori_loop(0, width // PART_ROWS, out_weights, 0)


def middle_kernel(
    g,
    x_ref,
    attended,
    places_ref,
    cols_ref,
    wo_ref,
    up_ref,
    down_ref,
    vec_ref,
    up_bias_ref,
    grad_ref,
    out_ref,
    dmid_ref,
    datt_ref,
    g_out_ref,
    g_up_ref,
    g_down_ref,
    gvec_ref,
    g_upb_ref,
    *refs,
):
    kept, sems = refs[:7], refs[12:]
    dffn_all, datt_all, work_out, work_grad, datt_sent = refs[7:12]
    pairs = datt_sent.shape[0]
    greet(Exchange.senders(g, "group") + [swap_partner(g)])
    there = Exchange(g, "group", datt_sent, datt_ref, *sems[:3])
    w_refs = (wo_ref, up_ref, down_ref)
    swap = Swap(g, grad_ref, work_grad, *sems[5:7])
    swap_out = Swap(g, work_out, out_ref, *sems[3:5])
    swap.start()
    middle_forward(x_ref, attended, w_refs, vec_ref, up_bias_ref, work_out, kept)
    swap.wait()
    swap_out.start()
    made = (dffn_all, dmid_ref, datt_all, gvec_ref, g_upb_ref)
    middle_backward(work_grad, cols_ref, 2 * pairs, w_refs, vec_ref, kept, made)
    for pair in range(pairs):
        permute_pair(pair, places_ref, datt_all, datt_sent)
        there.start(pair)
    middle_weights(attended, dmid_ref, kept, dffn_all, (g_out_ref, g_up_ref, g_down_ref))
    for pair in range(pairs):
        there.arrive(pair)
        there.sent(pair)
    swap_out.wait()


def middle_scratch(tok, width, wide):
    return [
        pltpu.VMEM((tok, width), BF16),
        pltpu.VMEM((tok, wide), BF16),
        pltpu.VMEM((tok, wide), BF16),
        pltpu.VMEM((tok, width), F32),
        pltpu.VMEM((tok, width), F32),
        pltpu.VMEM((tok, 1), F32),
        pltpu.VMEM((tok, 1), F32),
        pltpu.VMEM((tok, width), BF16),
        pltpu.VMEM((tok, width), BF16),
        pltpu.VMEM((tok, width), BF16),
        pltpu.VMEM((tok, width), BF16),
        pltpu.VMEM((width // PAIR, tok, PAIR), BF16),
    ]


def middle(g, *args):
    x, up = args[0], args[5]
    tok, width = x.shape
    wide = up.shape[1]
    pairs = width // PAIR
    shape = jax.ShapeDtypeStruct
    any_space, vmem = pl.BlockSpec(memory_space=pl.ANY), pl.BlockSpec(memory_space=pltpu.VMEM)
    return pl.pallas_call(
        functools.partial(middle_kernel, g),
        out_shape=[
            shape((tok, width), BF16),
            shape((tok, width), BF16),
            shape((pairs, g.seq, tok // g.seq, PAIR), BF16),
            shape((width, width), BF16),
            shape((width, wide), BF16),
            shape((wide, width), BF16),
            shape((8, width), F32),
            shape((8, wide), F32),
        ],
        in_specs=[vmem] * (len(args) - 1) + [any_space],
        out_specs=[any_space, vmem, any_space] + [vmem] * 5,
        scratch_shapes=[
            *middle_scratch(tok, width, wide),
            *exchange_sems(g, pairs),
            *Swap.sems(),
            *Swap.sems(),
        ],
        compiler_params=pltpu.CompilerParams(
            collective_id=3, has_side_effects=True, vmem_limit_bytes=VMEM_LIMIT
        ),
        name="middle",
    )(*args)


Y_FIRST = ("c", "y", "x", "l", "h")
TURNS = [("c", "l", "x", "y", "h"), ("c", "x", "l", "y", "h"), ("c", "y", "l", "x", "h"), Y_FIRST]


def step_of(unit, level):
    return unit // 2 + level - (level == 1)


def backward_kernel(
    g,
    scale,
    n,
    x_ref,
    wq_ref,
    wk_ref,
    wv_ref,
    dmid_ref,
    cols_ref,
    *refs,
):
    terms, refs = refs[:n], refs[n:]
    qkv_ref, grad_ref, gtok_ref, gq_ref, gk_ref, gv_ref, gvec_ref = refs[:7]
    sums, refs = refs[7 : 7 + n], refs[7 + n :]
    qkv_slots, grad_slots, sent, home, rhs, local, flat, total = refs[:8]
    bufs, refs = refs[8 : 8 + 5 * n], refs[8 + 5 * n :]
    rs_send, rs_recv, ex_send, ex_recv, ex_local, load_sem = refs
    pairs = sent.shape[0]
    tok, width = x_ref.shape
    greet(line_peers(g) + Exchange.senders(g, "group"))
    plan = Scatter(g, terms, bufs, [Y_FIRST] * n, rs_send, rs_recv)
    there = Exchange(g, "group", sent, home, ex_send, ex_recv, ex_local)
    units = len(plan.units)

    def loads(pair):
        slot = pair % 2
        return (
            pltpu.make_async_copy(qkv_ref.at[pair], qkv_slots.at[slot], load_sem.at[0, slot]),
            pltpu.make_async_copy(grad_ref.at[pair], grad_slots.at[slot], load_sem.at[1, slot]),
        )

    for copy in loads(0):
        copy.start()
    gvec_ref[...] = jnp.zeros_like(gvec_ref)
    total[...] = dmid_ref[...].astype(F32)
    for unit in range(units):
        plan.step(unit, 0)

    def step(t, carry):
        @pl.when(t < pairs)
        def _():
            for copy in loads(t):
                copy.wait()

            @pl.when(t + 1 < pairs)
            def _():
                for copy in loads(t + 1):
                    copy.start()

            attend_back_pair(t % 2, t, scale, qkv_slots, grad_slots, sent)
            there.start(t)

        for when in range(pairs + LAG):
            todo = [
                (unit, level)
                for level in range(1, 6)
                for unit in range(units)
                if step_of(unit, level) == when
            ]
            if todo:

                @pl.when(t == when)
                def _(todo=todo):
                    for unit, level in todo:
                        plan.step(unit, level, sums)

        @pl.when(t >= LAG)
        def _():
            pair = t - LAG
            head = pl.ds(pl.multiple_of(pair * PAIR, PAIR), PAIR)
            there.arrive(pair)
            pair_weights(pair, (wq_ref, wk_ref, wv_ref), flat)

            def gather_home(owner, carry):
                per = tok // g.seq
                rhs[pl.ds(pl.multiple_of(owner * per, per), per), :] = home[pair, owner]
                return carry

            lax.fori_loop(0, g.seq, gather_home, 0)

            def unpermute(k, carry):
                start = k * ROWS
                rows = pl.ds(start, ROWS)
                made = move_rows(lambda i: token_rows(cols_ref, 2 * pair + i, start, ROWS), rhs)
                sums = [column_sum(value) for value in made]
                low = head_lanes(sums[0].shape)
                gvec_ref[0:1, head] += jnp.where(low, sums[0], sums[1])
                gvec_ref[2:3, head] += jnp.where(low, sums[1], sums[2])
                for part, value in enumerate(made):
                    local[rows, part * PAIR : (part + 1) * PAIR] = value.astype(BF16)
                total[rows, :] += dot_nt(local[rows, :], flat[...])
                return carry

            lax.fori_loop(0, tok // ROWS, unpermute, 0)

            def weights(k, carry):
                rows = pl.ds(pl.multiple_of(k * PART_ROWS, PART_ROWS), PART_ROWS)
                value = dot_tn(x_ref[:, rows], local[...])
                made = unpack(*(value[:, i * PAIR : (i + 1) * PAIR] for i in range(3)))
                for part, g_ref in enumerate((gq_ref, gk_ref, gv_ref)):
                    g_ref[rows, head] = made[part].astype(BF16)
                return carry

            lax.fori_loop(0, width // PART_ROWS, weights, 0)

        return carry

    lax.fori_loop(0, pairs + LAG, step, 0)
    gtok_ref[...] = total[...].astype(BF16)
    for when in range(pairs + LAG, step_of(units - 1, 5) + 1):
        for level in range(1, 6):
            for unit in range(units):
                if step_of(unit, level) == when:
                    plan.step(unit, level, sums)
    plan.sent()

    def close(pair, carry):
        there.sent(pair)
        return carry

    lax.fori_loop(0, pairs, close, 0)


def backward(g, scale, x, wq, wk, wv, d_mid, cols, terms, qkv, grad):
    tok, width = x.shape
    pairs = width // PAIR
    n = len(terms)
    shape = jax.ShapeDtypeStruct
    any_space, vmem = pl.BlockSpec(memory_space=pl.ANY), pl.BlockSpec(memory_space=pltpu.VMEM)
    dma = pltpu.SemaphoreType.DMA
    made = pl.pallas_call(
        functools.partial(backward_kernel, g, scale, n),
        out_shape=[
            shape((tok, width), BF16),
            *([shape((width, width), BF16)] * 3),
            shape((8, width), F32),
            *(shape(item.shape[-2:], F32) for item in terms),
        ],
        in_specs=[vmem] * (6 + n) + [any_space] * 2,
        out_specs=[vmem] * (5 + n),
        scratch_shapes=[
            pltpu.VMEM((2, *qkv.shape[1:]), BF16),
            pltpu.VMEM((2, *grad.shape[1:]), BF16),
            pltpu.VMEM(qkv.shape, BF16),
            pltpu.VMEM(qkv.shape, BF16),
            pltpu.VMEM((tok, 3 * PAIR), BF16),
            pltpu.VMEM((tok, 3 * PAIR), BF16),
            pltpu.VMEM((width, 3 * PAIR), BF16),
            pltpu.VMEM((tok, width), F32),
            *Scatter.scratch(g, [item.shape for item in terms], [Y_FIRST] * n),
            *exchange_sems(g, pairs),
            dma((2, 2)),
        ],
        compiler_params=pltpu.CompilerParams(
            collective_id=5, has_side_effects=True, vmem_limit_bytes=VMEM_LIMIT
        ),
        name="backward",
    )(x, wq, wk, wv, d_mid, cols, *terms, qkv, grad)
    return made[0], made[1:4], made[4], made[5 : 5 + n]


def small_lines(bias_ref, rows_ref, up_ref, stats_ref):
    width = bias_ref.shape[1]
    lines = up_ref.shape[1] // width
    stats = jnp.concatenate(
        [stats_ref[0:2, :], jnp.zeros((2, width - stats_ref.shape[1]), F32)], axis=1
    )
    return jnp.concatenate(
        [
            bias_ref[0:1, :],
            bias_ref[2:3, :],
            rows_ref[0:6, :],
            *(up_ref[0:1, i * width : (i + 1) * width] for i in range(lines)),
            stats,
            jnp.zeros((6 - lines, width), F32),
        ],
        axis=0,
    )


def own_lines(g, held, outs):
    width = held.shape[1]
    b, s = lax.axis_index("batch"), lax.axis_index("seq")
    here = b * g.seq + s
    vectors, (up_out, stats_out) = outs[:8], outs[8:]
    count, wide = vectors[0].shape[1], up_out.shape[1]
    lines = wide * g.n // width
    per_line = width // wide
    mine = pltpu.roll(held[...], (width - here * count) % width, 1)
    for i, out in enumerate(vectors):
        out[...] = mine[i : i + 1, :count]
    up = pltpu.roll(held[...], (width - here % per_line * wide) % width, 1)
    total = jnp.zeros((1, wide), F32)
    for i in range(lines):
        total += jnp.where(here // per_line == i, up[8 + i : 9 + i, :wide], 0.0)
    up_out[...] = total
    blocks = stats_out.shape[1]
    stats = pltpu.roll(held[...], (width - s * blocks) % width, 1)
    stats_out[...] = stats[8 + lines : 10 + lines, :blocks]


def close_kernel(g, n, bias_ref, rows_ref, up_ref, stats_ref, *refs):
    terms, gtok_ref, refs = refs[:n], refs[n], refs[n + 1 :]
    small_outs, sums, gtok_home, refs = refs[:10], refs[10 : 10 + n], refs[10 + n], refs[11 + n :]
    held, refs = refs[0], refs[1:]
    bufs, refs = refs[: 5 * n], refs[5 * n :]
    rs_send, rs_recv, small_bufs, refs = refs[0], refs[1], refs[2:7], refs[7:]
    small_send, small_recv, swap_send, swap_recv = refs
    greet(line_peers(g) + [swap_partner(g)])
    plan = Scatter(g, terms, bufs, TURNS, rs_send, rs_recv)
    swap = Swap(g, gtok_ref, gtok_home, swap_send, swap_recv)
    small = Total(g, held, small_bufs, small_send, small_recv)
    units = len(plan.units)
    for unit in range(units):
        plan.step(unit, 0)
    small.start(0, small_lines(bias_ref, rows_ref, up_ref, stats_ref))
    swap.start()
    for level in range(1, 6):
        for unit in range(units):
            plan.step(unit, level, sums)
        value = small.take(level - 1)
        if level < len(AXES):
            small.start(level, value)
        else:
            held[...] = value
            own_lines(g, held, small_outs)
    swap.wait()
    plan.sent()
    small.sent()


def close_call(g, small, sizes_out, terms, gtok):
    n = len(terms)
    lines = (16, small[0].shape[1])
    shape = jax.ShapeDtypeStruct
    any_space, vmem = pl.BlockSpec(memory_space=pl.ANY), pl.BlockSpec(memory_space=pltpu.VMEM)
    made = pl.pallas_call(
        functools.partial(close_kernel, g, n),
        out_shape=[
            *(shape(item, F32) for item in sizes_out),
            *(shape(item.shape[-2:], F32) for item in terms),
            shape(gtok.shape, BF16),
        ],
        in_specs=[vmem] * (5 + n),
        out_specs=[vmem] * (10 + n) + [any_space],
        scratch_shapes=[
            pltpu.VMEM(lines, F32),
            *Scatter.scratch(g, [item.shape for item in terms], TURNS),
            *Total.scratch(g, lines),
            *Swap.sems(),
        ],
        compiler_params=pltpu.CompilerParams(
            collective_id=6, has_side_effects=True, vmem_limit_bytes=VMEM_LIMIT
        ),
        name="close",
    )(*small, *terms, gtok)
    return made[:10], made[10:-1], made[-1]


def finish_kernel(n, *refs):
    ins, outs, sems = refs[:n], refs[n : 2 * n], refs[2 * n]
    copies = [
        pltpu.make_async_copy(src, dst, sems.at[k]) for k, (src, dst) in enumerate(zip(ins, outs))
    ]
    for copy in copies:
        copy.start()
    for copy in copies:
        copy.wait()


def finish(arrays):
    n = len(arrays)
    any_space = pl.BlockSpec(memory_space=pl.ANY)
    return pl.pallas_call(
        functools.partial(finish_kernel, n),
        out_shape=[jax.ShapeDtypeStruct(item.shape, item.dtype) for item in arrays],
        in_specs=[pl.BlockSpec(memory_space=pltpu.VMEM)] * n,
        out_specs=[any_space] * n,
        scratch_shapes=[pltpu.SemaphoreType.DMA((n,))],
        name="finish",
    )(*arrays)


def body(
    g,
    tokens,
    cluster_slot,
    loss_mask,
    out_grad,
    query_weight,
    key_weight,
    value_weight,
    output_weight,
    query_bias,
    value_bias,
    output_bias,
    first_gain,
    first_shift,
    up_weight,
    up_bias,
    down_weight,
    down_bias,
    second_gain,
    second_shift,
):
    tok, width = tokens.shape[1:]
    heads = cluster_slot.shape[1]
    pairs = heads // 2
    wide = up_weight.shape[1]
    per_owner = tok // g.seq
    scale = (width // heads) ** -0.5

    slots = cluster_slot[0]
    places = slots // tok * per_owner + slots % tok // g.seq
    table = jnp.concatenate(
        [places, loss_mask, jnp.zeros((16 - heads - 1, tok), jnp.int32)], axis=0
    )
    vectors = (
        query_bias,
        value_bias,
        output_bias,
        first_gain,
        first_shift,
        down_bias,
        second_gain,
        second_shift,
    )
    count = query_bias.shape[0]
    packed = jnp.pad(jnp.stack(vectors), ((0, 8), (0, PAIR - count))) + jnp.pad(
        up_bias[None], ((8, 7), (0, PAIR - up_bias.shape[0]))
    )
    gathered, partial, (work_x, work_table, work_mask) = open_call(
        g,
        [packed, query_weight, key_weight, value_weight],
        [output_weight, up_weight, down_weight],
        [tokens[0], table],
    )
    work_cols = work_table.T

    def whole(item):
        return item.reshape(g.n * item.shape[-2], item.shape[-1])

    wq, wk, wv = (whole(item) for item in gathered[1:])
    flat = gathered[0].reshape(g.n, 16, PAIR).astype(F32)
    rows = flat[:, :8, :count].transpose(1, 0, 2).reshape(8, width)
    up_row = flat[:, 8, : up_bias.shape[0]].reshape(1, wide)
    qkv_bias = jnp.stack([rows[0], jnp.zeros((width,), F32), rows[1]])

    spread, (qkv, attended, stats) = forward(
        g,
        scale,
        1.0 / (heads * CLUSTER * g.batch),
        work_x,
        wq,
        wk,
        wv,
        qkv_bias,
        work_table,
        work_cols,
        work_mask.reshape(1, tok, PAIR),
        partial,
    )
    wo, up, down = (whole(item) for item in spread)

    out, d_mid, routed, g_out, g_up, g_down, g_rows, g_upb = middle(
        g, work_x, attended, work_table, work_cols, wo, up, down, rows[2:], up_row, out_grad[0]
    )

    def parts(item):
        rows, cols = item.shape[0] // g.n, item.shape[1]
        if rows % 8:
            rows, cols = rows * cols // PAIR, PAIR
        return item.reshape(*(sizes(g)[axis] for axis in AXES), rows, cols)

    grad_tokens, g_attn, g_bias, s_ffn = backward(
        g,
        scale,
        work_x,
        wq,
        wk,
        wv,
        d_mid,
        work_cols,
        [parts(g_up), parts(g_out)],
        qkv,
        routed,
    )
    blocks = tok // CLUSTER
    small, s_attn, grad_tokens = close_call(
        g,
        [g_bias, g_rows, g_upb, stats],
        [(1, count)] * 8 + [(1, wide // g.n), (2, blocks)],
        [parts(item) for item in (*g_attn, g_down)],
        grad_tokens,
    )
    made = finish([out, grad_tokens, *small, *s_ffn, *s_attn])
    out, grad_tokens, small, sums = made[0], made[1], made[2:12], made[12:]
    s_up, s_out, s_query, s_key, s_value, s_down = (
        item.reshape(local.shape)
        for item, local in zip(
            sums,
            (up_weight, output_weight, query_weight, key_weight, value_weight, down_weight),
        )
    )
    gq, gv, go, gg1, gs1, gd, gg2, gs2, gu = (item.reshape(-1) for item in small[:9])
    return (
        out[None],
        grad_tokens[None],
        s_query,
        s_key,
        s_value,
        s_out,
        gq,
        gv,
        go,
        gg1,
        gs1,
        s_up,
        gu,
        s_down,
        gd,
        gg2,
        gs2,
        small[9],
    )


def solution(mesh):
    g = Grid(mesh)
    tokens, rows, flat = P("batch", "seq", None), P(("batch", "seq"), None), P(("batch", "seq"))
    return jax.shard_map(
        functools.partial(body, g),
        mesh=mesh,
        in_specs=(
            tokens,
            P("batch", None, "seq"),
            P("batch", "seq"),
            tokens,
            *([rows] * 4),
            *([flat] * 5),
            rows,
            flat,
            rows,
            *([flat] * 3),
        ),
        out_specs=(
            tokens,
            tokens,
            *([rows] * 4),
            *([flat] * 5),
            rows,
            flat,
            rows,
            *([flat] * 3),
            P(None, "seq"),
        ),
        check_vma=False,
    )
```
